256 devices in a mesh: ctx: 16 (over z_lo, y), fsdp: 16 (over z_hi, x, core).
Axes of the slice: x: 4, y: 4, z: 8 (z_hi: 2, z_lo: 4; z = z_hi * 4 + z_lo), core: 2. Of those that a mesh axis runs over, the one named last changes fastest.
Arguments:
- inputs: bfloat16 [4096, 7168], P('ctx'), may hold values from -12 to 12
- w_qkv: bfloat16 [7168, 3, 4096], P('ctx', None, 'fsdp'), may hold values from -1 to 1, as said below
- selected: int32 [8, 4], replicated, may hold values from -1 to 7, as said below
- d_attn: bfloat16 [4096, 4096], P('ctx', 'fsdp'), may hold values from -6 to 6
Outputs:
- d_input: bfloat16 [4096, 7168], P('ctx', 'fsdp')
The draws below stay inside these ranges and needn't reach their ends.
Inputs may be any that keep to these rules, and one draw needn't show every extreme that they name: `selected`: row b lists min(b + 1, 4) different blocks of 0 to b, b among them, in the first slots; the other slots hold -1. `w_qkv`: projection weights scaled by the fan-in.
All inputs are finite; a program needn't handle non-finite values.
Results may differ from the reference program's by a relative error of at most 0.023.
Values may be sent and summed in bfloat16 or wider, within the bound.
A program may use at most 128 MiB of HBM per device.

```python
import jax
import jax.numpy as jnp
from jax import lax

D = 7168
HD = 128
H_DEV = 2
BLOCK = 512
TOP = 4
TOK_DEV = 256
HEADS = 32
SEQ = 4096
NBLK = 8
N_CTX = 16
N_FSDP = 16


def draw_inputs(key, part):
    base = jnp.clip(jax.random.normal(key, (SEQ, D), jnp.float32), -6.0, 6.0)
    return base.astype(jnp.bfloat16)


def draw_w_qkv(key, part):
    base = jnp.clip(jax.random.normal(key, (D, 3, HEADS * HD), jnp.float32), -6.0, 6.0) * D ** (-0.5)
    return base.astype(jnp.bfloat16)


def draw_selected(key, part):
    first_key = jax.random.fold_in(key, 21)
    second_key = jax.random.fold_in(key, 22)
    noise = jax.random.randint(first_key, (NBLK, NBLK), 0, 4096)
    popular = jax.random.randint(second_key, (NBLK,), 0, 4)
    row_ids = jnp.arange(NBLK, dtype=jnp.int32)[:, None]
    col_ids = jnp.arange(NBLK, dtype=jnp.int32)[None, :]
    score = (noise + popular[None, :] * 4096) * NBLK + col_ids
    score = jnp.where(col_ids == row_ids, -1, score)
    score = jnp.where(col_ids > row_ids, 1 << 30, score)
    order = jnp.argsort(score, axis=1, stable=True)[:, :TOP].astype(jnp.int32)
    slot_ids = jnp.arange(TOP, dtype=jnp.int32)[None, :]
    return jnp.where(slot_ids <= row_ids, order, -1).astype(jnp.int32)


def block_levels(stream_key, shape, cuts, least, high):
    loudness = 1.0
    for dim, shards_of in cuts:
        steps = jax.random.uniform(jax.random.fold_in(jax.random.fold_in(stream_key, 6), dim), (shards_of,), jnp.float32, least / len(cuts), high / len(cuts))
        loudness = loudness * jnp.repeat(jnp.exp(steps), shape[dim] // shards_of).reshape((-1,) + (1,) * (len(shape) - 1 - dim))
    return loudness


def bell_draw(rng, extent, spread, most, split=(), kind=jnp.bfloat16):
    array = spread * jax.random.normal(rng, extent, jnp.float32)
    if split:
        array = array * block_levels(rng, extent, split, -0.22, 0.18)
    return jnp.clip(array, -most, most).astype(kind)


def setup_inputs(seed: int = 0) -> dict:
    seeds = jax.random.split(jax.random.key(seed), 5)
    inputs = draw_inputs(jax.random.fold_in(seeds[4], 71), 0)
    w_qkv = draw_w_qkv(jax.random.fold_in(seeds[4], 71), 0)
    selected = draw_selected(jax.random.fold_in(seeds[4], 71), 0)
    d_attn = bell_draw(seeds[3], (SEQ, HEADS * HD), 1.0, 6.0, ((0, 16), (1, 16)))
    return dict(inputs=inputs, w_qkv=w_qkv, selected=selected, d_attn=d_attn)


def reference(inputs, w_qkv, selected, d_attn):
    scaling = HD ** -0.5
    col_total = HEADS * HD
    flat_w = w_qkv.reshape(D, 3 * col_total)
    projected = jnp.dot(inputs, flat_w, preferred_element_type=jnp.float32).astype(jnp.bfloat16)
    projected = projected.reshape(SEQ, 3, HEADS, HD)
    block_ids = jnp.arange(NBLK, dtype=jnp.int32)
    chosen = jnp.any(selected[:, :, None] == block_ids[None, None, :], axis=1)
    position = jnp.arange(SEQ, dtype=jnp.int32)
    owner = position // BLOCK
    allowed = chosen[owner][:, owner] & (position[:, None] >= position[None, :])
    grad_out = d_attn.reshape(SEQ, HEADS, HD)
    stacked = (projected[:, 0].transpose(1, 0, 2), projected[:, 1].transpose(1, 0, 2),
               projected[:, 2].transpose(1, 0, 2), grad_out.transpose(1, 0, 2))

    def one_head(item):
        query, keys, values, grad_head = item
        scores = jnp.dot(query, keys.T, preferred_element_type=jnp.float32) * scaling
        masked = jnp.where(allowed, scores, -jnp.inf)
        highest = jnp.max(masked, axis=1, keepdims=True)
        expo = jnp.exp(masked - highest)
        probs = expo / jnp.sum(expo, axis=1, keepdims=True)
        probs_low = probs.astype(jnp.bfloat16)
        attended = jnp.dot(probs_low, values, preferred_element_type=jnp.float32).astype(jnp.bfloat16)
        delta = jnp.sum(grad_head.astype(jnp.float32) * attended.astype(jnp.float32), axis=1, keepdims=True)
        dprobs = jnp.dot(grad_head, values.T, preferred_element_type=jnp.float32)
        dscores = (probs * (dprobs - delta)).astype(jnp.bfloat16)
        dquery = (jnp.dot(dscores, keys, preferred_element_type=jnp.float32) * scaling).astype(jnp.bfloat16)
        runs = (dscores.reshape(N_CTX, TOK_DEV, SEQ), query.reshape(N_CTX, TOK_DEV, HD),
                probs_low.reshape(N_CTX, TOK_DEV, SEQ), grad_head.reshape(N_CTX, TOK_DEV, HD))

        def add_run(carry, run):
            ds_run, query_run, probs_run, grad_run = run
            key_part = (jnp.dot(ds_run.T, query_run, preferred_element_type=jnp.float32) * scaling).astype(jnp.bfloat16)
            value_part = jnp.dot(probs_run.T, grad_run, preferred_element_type=jnp.float32).astype(jnp.bfloat16)
            key_part, value_part = lax.optimization_barrier((key_part, value_part))
            return (carry[0] + key_part.astype(jnp.float32), carry[1] + value_part.astype(jnp.float32)), None

        zeros_run = jnp.zeros((SEQ, HD), jnp.float32)
        (dkeys, dvalues), _ = lax.scan(add_run, (zeros_run, zeros_run), runs)
        return dquery, dkeys.astype(jnp.bfloat16), dvalues.astype(jnp.bfloat16)

    dquery, dkeys, dvalues = lax.map(one_head, stacked)
    grads = jnp.stack([dquery, dkeys, dvalues], axis=0).transpose(2, 0, 1, 3)
    group_cols = H_DEV * HD
    grad_groups = grads.reshape(SEQ, 3, N_FSDP, group_cols).transpose(2, 0, 1, 3).reshape(N_FSDP, SEQ, 3 * group_cols)
    weight_groups = w_qkv.reshape(D, 3, N_FSDP, group_cols).transpose(2, 0, 1, 3).reshape(N_FSDP, D, 3 * group_cols)

    def add_group(carry, pair):
        part = lax.dot_general(pair[0], pair[1], (((1,), (1,)), ((), ())),
                               preferred_element_type=jnp.float32).astype(jnp.bfloat16)
        part = lax.optimization_barrier(part)
        return carry + part.astype(jnp.float32), None

    total, _ = lax.scan(add_group, jnp.zeros((SEQ, D), jnp.float32), (grad_groups, weight_groups))
    return total.astype(jnp.bfloat16)
```

```python
import functools

import jax
import jax.numpy as jnp
from jax import lax
from jax.experimental import pallas as pl
from jax.experimental.pallas import tpu as pltpu
from jax.sharding import PartitionSpec as P

MESH = pl.DeviceIdType.MESH
F32 = jnp.float32
BF16 = jnp.bfloat16
HD = 128
BLOCK = 512
TOP = 4
SCALE = HD ** (-0.5)
VMEM_BYTES = 60 * 1024 * 1024


def place():
    c = lax.axis_index("ctx")
    f = lax.axis_index("fsdp")
    return (
        lax.div(c, 4), lax.rem(c, 4),
        lax.div(f, 8), lax.rem(lax.div(f, 2), 4), lax.rem(f, 2),
    )


def device(z, y, zh, x, k):
    return (z * 4 + y, zh * 8 + x * 2 + k)


def turn(i, by):
    return lax.rem(i + by, 4)


def rows(start, size):
    return pl.ds(pl.multiple_of(start, size & -size), size)


class Mail:
    def __init__(self, send_sems):
        self.send_sems = send_sems
        self.used = 0
        self.sent = []

    def copy(self, src, dst, recv, dev):
        sem = self.send_sems.at[self.used]
        self.used += 1
        return pltpu.make_async_remote_copy(
            src_ref=src, dst_ref=dst, send_sem=sem, recv_sem=recv,
            device_id=dev, device_id_type=MESH,
        )

    def send(self, src, dst, recv, dev):
        copy = self.copy(src, dst, recv, dev)
        copy.start()
        self.sent.append((copy, None, None))

    def send_or_keep(self, away, src, dst, recv, dev):
        copy = self.copy(src, dst, recv, dev)
        stay = pltpu.make_async_copy(src, dst, recv)

        @pl.when(away)
        def _():
            copy.start()

        @pl.when(jnp.logical_not(away))
        def _():
            stay.start()

        self.sent.append((copy, away, None))

    def send_if(self, away, src, dst, recv, dev):
        copy = self.copy(src, dst, recv, dev)

        @pl.when(away)
        def _():
            copy.start()

        self.sent.append((copy, away, None))

    def flush(self):
        for copy, away, _ in self.sent:
            if away is None:
                copy.wait_send()
            else:
                pl.when(away)(copy.wait_send)


def got(dst, recv):
    pltpu.make_async_copy(dst, dst, recv).wait()


class Ring:
    def __init__(self, mail, view, pos, core, right, left, partner, ring, cores):
        self.mail, self.view, self.pos, self.core = mail, view, pos, core
        self.right, self.left, self.partner = right, left, partner
        self.ring, self.cores = ring, cores

    def pass_on(self, pos, half, recv, dev):
        ref = self.view(self.core, pos, half)
        self.mail.send(ref, ref, recv, dev)

    def start(self):
        self.pass_on(self.pos, None, self.ring.at[0], self.right)
        self.pass_on(self.pos, None, self.ring.at[1], self.left)
        self.pass_on(self.pos, None, self.cores.at[0], self.partner)

    def relay(self):
        before, after = turn(self.pos, 3), turn(self.pos, 1)
        got(self.view(self.core, before, None), self.ring.at[0])
        self.pass_on(before, 0, self.ring.at[2], self.right)
        self.pass_on(before, None, self.cores.at[1], self.partner)
        got(self.view(self.core, after, None), self.ring.at[1])
        self.pass_on(after, 1, self.ring.at[3], self.left)
        self.pass_on(after, None, self.cores.at[2], self.partner)

    def finish(self):
        far = turn(self.pos, 2)
        for half in (0, 1):
            got(self.view(self.core, far, half), self.ring.at[2 + half])
            self.pass_on(far, half, self.cores.at[3 + half], self.partner)

    def settle(self):
        other = 1 - self.core
        before, after, far = turn(self.pos, 3), turn(self.pos, 1), turn(self.pos, 2)
        got(self.view(other, self.pos, None), self.cores.at[0])
        got(self.view(other, before, None), self.cores.at[1])
        got(self.view(other, after, None), self.cores.at[2])
        got(self.view(other, far, 0), self.cores.at[3])
        got(self.view(other, far, 1), self.cores.at[4])


def enter(devices, more=0):
    barrier = pltpu.get_barrier_semaphore()
    for dev in devices:
        pl.semaphore_signal(barrier, inc=1, device_id=dev, device_id_type=MESH)
    return barrier, len(devices) + more


def project_kernel(
    inp, w3, d_attn, q_out, kv_out, do_out, w_out,
    wall, xall, dall, part, parts_in, own, kvall,
    send_sems, load_sems, w_ring, w_cores, x_z, x_x, d_sems, p_sems, kv_ring, kv_cores, out_sems,
):
    z, y, zh, x, j = place()
    here = functools.partial(device, z, y, zh, x)
    partner = here(1 - j)
    right = device(z, turn(y, 1), zh, x, j)
    left = device(z, turn(y, 3), zh, x, j)
    d = wall.shape[1] // 4
    dq = wall.shape[1]

    loads = []
    for s in (0, 1):
        for at, p in ((0, 1), (1, 2), (2, 0)):
            loads.append(pltpu.make_async_copy(
                w3.at[p, :, pl.ds(HD * s, HD)],
                wall.at[2 * j + s, rows(d * y, d), pl.ds(HD * at, HD)],
                load_sems.at[3 * s + at],
            ))
    own_x = pltpu.make_async_copy(
        inp.at[rows(HD * j, HD), rows(dq * z, dq)], xall.at[rows(HD * z, HD)], load_sems.at[6]
    )
    for copy in loads:
        copy.start()
    own_x.start()

    peers = [device(turn(z, t), y, zh, x, k) for t in (1, 2, 3) for k in (j, 1 - j)]
    peers += [partner, right, left]
    peers += [device(z, y, zh, turn(x, u), j) for u in (1, 2, 3)]
    barrier, expected = enter(peers)
    pl.semaphore_wait(barrier, expected)

    mail = Mail(send_sems)

    def w_view(s):
        def view(core, pos, half):
            if half is None:
                return wall.at[2 * core + s, rows(d * pos, d)]
            return wall.at[2 * core + s, rows(d * pos + (d // 2) * half, d // 2)]
        return view

    w_rings = [
        Ring(mail, w_view(s), y, j, right, left, partner, w_ring.at[s], w_cores.at[s])
        for s in (0, 1)
    ]
    for copy in loads[:3]:
        copy.wait()
    w_rings[0].start()

    piece = HD // 4
    for t in (1, 2, 3):
        zd = turn(z, t)
        mail.send(
            inp.at[rows(HD * j + piece * x, piece), rows(dq * zd, dq)],
            xall.at[rows(HD * z + piece * x, piece)],
            x_z.at[t - 1], device(zd, y, zh, x, j),
        )
    for copy in loads[3:]:
        copy.wait()
    for t in (1, 2, 3):
        zs = turn(z, 4 - t)
        mine = xall.at[rows(HD * zs + piece * x, piece)]
        got(mine, x_z.at[t - 1])
        for u in (1, 3, 2):
            mail.send(mine, mine, x_x.at[t - 1, u - 1], device(z, y, zh, turn(x, u), j))
    w_rings[0].relay()
    w_rings[1].start()
    for s in (0, 1):
        for k in (0, 1):
            zd = 2 * j + s
            away = jnp.logical_or(zd != z, j != k)
            mail.send_or_keep(
                away,
                d_attn.at[pl.ds(HD * k, HD), pl.ds(HD * s, HD)],
                dall.at[z], d_sems.at[z], device(zd, y, zh, x, k),
            )
    own_x.wait()
    for t in (1, 2, 3):
        zs = turn(z, 4 - t)
        for u in (1, 3, 2):
            xs = turn(x, 4 - u)
            got(xall.at[rows(HD * zs + piece * xs, piece)], x_x.at[t - 1, u - 1])
    w_rings[0].finish()
    w_rings[0].settle()

    def project(s, turned):
        head = 2 * lax.rem(j + turned, 2) + s
        slot = 2 * s + turned
        away = head != z

        for tile in (0, 1):
            at = pl.ds(256 * tile, 256)
            total = jnp.dot(xall[at], wall[head], preferred_element_type=F32)
            part[slot, at] = total.astype(BF16)

            @pl.when(jnp.logical_not(away))
            def _():
                own[at] = total

        mail.send_if(
            away, part.at[slot], parts_in.at[z], p_sems.at[z], device(head, y, zh, x, j)
        )

    project(0, 0)
    project(0, 1)
    w_rings[1].relay()
    w_rings[1].finish()
    w_rings[1].settle()
    project(1, 0)
    project(1, 1)
    keep_w = pltpu.make_async_copy(wall, w_out, out_sems.at[0])
    keep_w.start()

    for t in (1, 2, 3):
        zs = turn(z, t)
        got(parts_in.at[zs], p_sems.at[zs])
    for run in range(4):
        at = pl.ds(HD * run, HD)
        total = own[at]
        for t in (1, 2, 3):
            total += parts_in[turn(z, t), at].astype(F32)
        low = total.astype(BF16)
        kvall[run, y, j] = low[:, : 2 * HD]
        q_out[at] = low[:, 2 * HD :]

    def kv_view(core, pos, half):
        if half is None:
            return kvall.at[:, pos, core]
        return kvall.at[pl.ds(2 * half, 2), pos, core]

    kv = Ring(mail, kv_view, y, j, right, left, partner, kv_ring, kv_cores)
    kv.start()
    for zs in range(4):
        got(dall.at[zs], d_sems.at[zs])
    do_out[...] = dall[...]
    kv.relay()
    kv.finish()
    kv.settle()
    keep_kv = pltpu.make_async_copy(kvall, kv_out, out_sems.at[1])
    keep_kv.start()
    mail.flush()
    keep_w.wait()
    keep_kv.wait()


def project_and_gather(inputs, w3, d_attn):
    rows_here, width = inputs.shape
    quarter = width // 4
    any_space = pl.BlockSpec(memory_space=pl.ANY)
    vmem = pl.BlockSpec(memory_space=pltpu.VMEM)
    dma = pltpu.SemaphoreType.DMA
    return pl.pallas_call(
        project_kernel,
        name="project_and_gather",
        out_shape=(
            jax.ShapeDtypeStruct((4 * HD, HD), BF16),
            jax.ShapeDtypeStruct((4, 4, 2, HD, 2 * HD), BF16),
            jax.ShapeDtypeStruct((4, HD, HD), BF16),
            jax.ShapeDtypeStruct((4, quarter, 3 * HD), BF16),
        ),
        in_specs=[any_space] * 3,
        out_specs=(vmem, any_space, vmem, any_space),
        scratch_shapes=[
            pltpu.VMEM((4, quarter, 3 * HD), BF16),
            pltpu.VMEM((4 * HD, quarter), BF16),
            pltpu.VMEM((4, HD, HD), BF16),
            pltpu.VMEM((4, 4 * HD, 3 * HD), BF16),
            pltpu.VMEM((4, 4 * HD, 3 * HD), BF16),
            pltpu.VMEM((4 * HD, 3 * HD), F32),
            pltpu.VMEM((4, 4, 2, HD, 2 * HD), BF16),
            dma((60,)), dma((7,)), dma((2, 4)), dma((2, 5)), dma((3,)), dma((3, 3)),
            dma((4,)), dma((4,)), dma((4,)), dma((5,)), dma((2,)),
        ],
        compiler_params=pltpu.CompilerParams(
            collective_id=0, has_side_effects=True, vmem_limit_bytes=VMEM_BYTES
        ),
    )(inputs, w3, d_attn)


def attend_kernel(selected, q_ref, kv_ref, do_ref, dq_ref, dkv_ref, score, soft, total):
    _, y, _, _, j = place()
    total[...] = jnp.zeros_like(total)
    contract = lambda a, b: (((a,), (b,)), ((), ()))
    dot = functools.partial(lax.dot_general, preferred_element_type=F32)
    key_at = lax.broadcasted_iota(jnp.int32, (BLOCK, HD), 0)
    query_at = lax.broadcasted_iota(jnp.int32, (BLOCK, HD), 1)

    def tile(run, carry):
        first = (run * 4 + y) * 256 + HD * j
        block = lax.div(first, BLOCK)
        q = q_ref[run]
        do = do_ref[run]
        highest = jnp.full((1, HD), -jnp.inf, F32)
        for t in range(TOP):
            chosen = selected[block, t]
            kb = jnp.maximum(chosen, 0)
            s = dot(kv_ref[kb, :, :HD], q, contract(1, 1)) * SCALE
            limit = jnp.where(chosen >= 0, first - kb * BLOCK, -2 * BLOCK)
            s = jnp.where(key_at - query_at <= limit, s, -jnp.inf)
            score[t] = s
            highest = jnp.maximum(highest, jnp.max(s, axis=0, keepdims=True))
        totals = jnp.zeros((1, HD), F32)
        for t in range(TOP):
            e = jnp.exp(score[t] - highest)
            score[t] = e
            totals += jnp.sum(e, axis=0, keepdims=True)
        share = 1.0 / totals
        attended = jnp.zeros((HD, HD), F32)
        for t in range(TOP):
            kb = jnp.maximum(selected[block, t], 0)
            p = score[t] * share
            low = p.astype(BF16)
            score[t] = p
            soft[t] = low
            attended += dot(kv_ref[kb, :, HD:], low, contract(0, 0))
        attended = attended.astype(BF16).astype(F32)
        delta = jnp.sum(do.astype(F32).T * attended, axis=0, keepdims=True)
        dq = jnp.zeros((HD, HD), F32)
        for t in range(TOP):
            kb = jnp.maximum(selected[block, t], 0)
            dp = dot(kv_ref[kb, :, HD:], do, contract(1, 1))
            ds = (score[t] * (dp - delta)).astype(BF16)
            total[kb, :, :HD] += dot(ds, q, contract(1, 0))
            total[kb, :, HD:] += dot(soft[t], do, contract(1, 0))
            dq += dot(ds, kv_ref[kb, :, :HD], contract(0, 0))
        dq_ref[run] = (dq * SCALE).astype(BF16)
        return carry

    lax.fori_loop(0, 4, tile, 0)
    for b in range(8):
        dkv_ref[b, :, :HD] = (total[b, :, :HD] * SCALE).astype(BF16)
        dkv_ref[b, :, HD:] = total[b, :, HD:].astype(BF16)


def attend(selected, q, kv, do):
    vmem = pl.BlockSpec(memory_space=pltpu.VMEM)
    return pl.pallas_call(
        attend_kernel,
        name="attend",
        out_shape=(
            jax.ShapeDtypeStruct((4, HD, HD), BF16),
            jax.ShapeDtypeStruct((8, BLOCK, 2 * HD), BF16),
        ),
        in_specs=[pl.BlockSpec(memory_space=pltpu.SMEM), vmem, vmem, vmem],
        out_specs=(vmem, vmem),
        scratch_shapes=[
            pltpu.VMEM((TOP, BLOCK, HD), F32),
            pltpu.VMEM((TOP, BLOCK, HD), BF16),
            pltpu.VMEM((8, BLOCK, 2 * HD), F32),
        ],
        compiler_params=pltpu.CompilerParams(vmem_limit_bytes=VMEM_BYTES),
    )(selected, q, kv, do)


def owner_x(z, pair, zp):
    same = 2 * lax.rem(z, 2) + pair
    other = 2 * (1 - lax.rem(z, 2)) + 1 - pair
    return jnp.where(zp == 0, same, other)


def portion(z, x):
    same = lax.div(x, 2) == lax.rem(z, 2)
    pair = jnp.where(same, lax.rem(x, 2), 1 - lax.rem(x, 2))
    return pair, jnp.where(same, 0, 1)


def gradient_kernel(
    dkv, dq, w_in, out,
    wall, gall, core_out, core_in, near_out, far_out, far_in, near_in, own_kv,
    x_out, x_in, own_x, fin, fin_in,
    send_sems, load_sem, core_sems, far_sems, near_sems, q_sems, g_sems, xf_sems, xn_sems, f_sems,
):
    z, y, zh, x, j = place()
    d = wall.shape[1] // 4
    partner = device(z, y, zh, x, 1 - j)
    right = device(z, turn(y, 1), zh, x, j)
    left = device(z, turn(y, 3), zh, x, j)
    x_right = device(z, y, zh, turn(x, 1), j)
    x_left = device(z, y, zh, turn(x, 3), j)
    across = [device(turn(z, t), y, zh, x, j) for t in (1, 2, 3)]
    f = lax.axis_index("fsdp")
    source_z = lax.div(f, 4)
    source_x = owner_x(source_z, lax.div(lax.rem(f, 4), 2), lax.div(z, 2))

    load = pltpu.make_async_copy(w_in, wall, load_sem)
    load.start()

    barrier, expected = enter([partner, right, left, x_right, x_left] + across, more=4)
    for h in (0, 1):
        for k in (0, 1):
            pl.semaphore_signal(
                barrier, inc=1, device_id=device(source_z, y, h, source_x, k),
                device_id_type=MESH,
            )
    pl.semaphore_wait(barrier, expected)

    mail = Mail(send_sems)
    for n, t in enumerate((2, 1, 3, 0)):
        yd = turn(y, t)
        mail.send(dkv.at[:, yd, 1 - j], core_in.at[n], core_sems.at[n], partner)
    for t in (1, 2, 3):
        mail.send(dq, gall.at[z, :, pl.ds(2 * HD, HD)], q_sems.at[z], across[t - 1])
    gall[z, :, pl.ds(2 * HD, HD)] = dq[...]

    def chip_sum(n, t, half):
        at = pl.ds(2 * half, 2)
        yd = turn(y, t)
        return dkv[at, yd, j].astype(F32) + core_in[n, at].astype(F32)

    got(core_in.at[0], core_sems.at[0])
    for half, dev in ((0, right), (1, left)):
        far_out[half] = chip_sum(0, 2, half).astype(BF16)
        mail.send(far_out.at[half], far_in.at[half], far_sems.at[half], dev)
    for side, (t, dev) in enumerate(((1, right), (3, left))):
        got(core_in.at[1 + side], core_sems.at[1 + side])
        alone = 1 - side
        near_out[side, alone] = chip_sum(1 + side, t, alone).astype(BF16)
        mail.send(
            near_out.at[side, alone], near_in.at[side, alone], near_sems.at[side, alone], dev
        )
    for side, (t, dev) in enumerate(((1, right), (3, left))):
        got(far_in.at[side], far_sems.at[side])
        near_out[side, side] = (
            chip_sum(1 + side, t, side) + far_in[side].astype(F32)
        ).astype(BF16)
        mail.send(
            near_out.at[side, side], near_in.at[side, side], near_sems.at[side, side], dev
        )
    got(core_in.at[3], core_sems.at[3])
    for half in (0, 1):
        own_kv[half] = chip_sum(3, 0, half)
    for side in (0, 1):
        for half in (1 - side, side):
            got(near_in.at[side, half], near_sems.at[side, half])
    for half in (0, 1):
        for i in (0, 1):
            total = own_kv[half, i]
            for side in (0, 1):
                total += near_in[side, half, i].astype(F32)
            gall[z, pl.ds(HD * (2 * half + i), HD), pl.ds(0, 2 * HD)] = total.astype(BF16)
    mine = gall.at[z, :, pl.ds(0, 2 * HD)]
    for t in (1, 2, 3):
        mail.send(mine, mine, g_sems.at[z], across[t - 1])
    load.wait()
    for t in (1, 2, 3):
        zs = turn(z, t)
        got(gall.at[zs, :, pl.ds(2 * HD, HD)], q_sems.at[zs])
        got(gall.at[zs, :, pl.ds(0, 2 * HD)], g_sems.at[zs])

    def part(t, e):
        pair, zp = portion(z, turn(x, t))
        at = rows(256 * zp, 256)
        cols = rows(d * (2 * pair + e), d)
        total = jnp.zeros((256, d), F32)
        for h in range(4):
            total += lax.dot_general(
                gall[h, at], wall[h, cols], (((1,), (1,)), ((), ())),
                preferred_element_type=F32,
            )
        return total

    for half, dev in ((0, x_right), (1, x_left)):
        x_out[half] = part(2, half).astype(BF16)
        mail.send(x_out.at[half], x_in.at[half], xf_sems.at[half], dev)
    for side, (t, dev) in enumerate(((1, x_right), (3, x_left))):
        alone = 1 - side
        x_out[2 + side] = part(t, alone).astype(BF16)
        mail.send(x_out.at[2 + side], x_in.at[2 + side], xn_sems.at[side], dev)
    for side, (t, dev) in enumerate(((1, x_right), (3, x_left))):
        total = part(t, side)
        got(x_in.at[side], xf_sems.at[side])
        x_out[4 + side] = (total + x_in[side].astype(F32)).astype(BF16)
        mail.send(x_out.at[4 + side], x_in.at[4 + side], xn_sems.at[2 + side], dev)
    for e in (0, 1):
        own_x[e] = part(0, e)
    for side in (0, 1):
        got(x_in.at[2 + side], xn_sems.at[side])
        got(x_in.at[4 + side], xn_sems.at[2 + side])
    pair, zp = portion(z, x)
    for e in (0, 1):
        fin[e] = (
            own_x[e] + x_in[2 + 1 - e].astype(F32) + x_in[4 + e].astype(F32)
        ).astype(BF16)
        for i in (0, 1):
            run = 2 * zp + i
            fd = 4 * z + 2 * pair + e
            away = jnp.logical_or(run != z, fd != f)
            mail.send_or_keep(
                away, fin.at[e, pl.ds(HD * i, HD)], fin_in.at[zh, j], f_sems.at[zh, j],
                (run * 4 + y, fd),
            )
    for h in (0, 1):
        for k in (0, 1):
            got(fin_in.at[h, k], f_sems.at[h, k])
    for k in (0, 1):
        out[pl.ds(HD * k, HD)] = (
            fin_in[0, k].astype(F32) + fin_in[1, k].astype(F32)
        ).astype(BF16)
    mail.flush()


def input_gradient(dkv, dq, w_all):
    quarter = w_all.shape[1]
    d = quarter // 4
    any_space = pl.BlockSpec(memory_space=pl.ANY)
    vmem = pl.BlockSpec(memory_space=pltpu.VMEM)
    dma = pltpu.SemaphoreType.DMA
    chunk = (4, HD, 2 * HD)
    half = (2, HD, 2 * HD)
    return pl.pallas_call(
        gradient_kernel,
        name="input_gradient",
        out_shape=jax.ShapeDtypeStruct((2 * HD, d), BF16),
        in_specs=[vmem, vmem, any_space],
        out_specs=vmem,
        scratch_shapes=[
            pltpu.VMEM(w_all.shape, BF16),
            pltpu.VMEM((4, 4 * HD, 3 * HD), BF16),
            pltpu.VMEM((1,) + chunk, BF16),
            pltpu.VMEM((4,) + chunk, BF16),
            pltpu.VMEM((2, 2) + half, BF16),
            pltpu.VMEM((2,) + half, BF16),
            pltpu.VMEM((2,) + half, BF16),
            pltpu.VMEM((2, 2) + half, BF16),
            pltpu.VMEM((2,) + half, F32),
            pltpu.VMEM((6, 2 * HD, d), BF16),
            pltpu.VMEM((6, 2 * HD, d), BF16),
            pltpu.VMEM((2, 2 * HD, d), F32),
            pltpu.VMEM((2, 2 * HD, d), BF16),
            pltpu.VMEM((2, 2, HD, d), BF16),
            dma((32,)), dma, dma((4,)), dma((2,)), dma((2, 2)), dma((4,)), dma((4,)),
            dma((2,)), dma((4,)), dma((2, 2)),
        ],
        compiler_params=pltpu.CompilerParams(
            collective_id=1, has_side_effects=True, vmem_limit_bytes=VMEM_BYTES
        ),
    )(dkv, dq, w_all)


def shards(inputs, w_qkv, selected, d_attn):
    w3 = w_qkv.transpose(1, 0, 2)
    q, kv, do, w_all = project_and_gather(inputs, w3, d_attn)
    dq, dkv = attend(
        selected, q.reshape(4, HD, HD), kv.reshape(8, BLOCK, 2 * HD), do
    )
    return input_gradient(dkv.reshape(4, 4, 2, HD, 2 * HD), dq.reshape(4 * HD, HD), w_all)


def solution(mesh):
    placed = (P("ctx", None), P("ctx", None, "fsdp"), P(), P("ctx", "fsdp"))
    return jax.shard_map(
        shards, mesh=mesh, in_specs=placed, out_specs=P("ctx", "fsdp"), check_vma=False
    )
```

```python
import functools

import jax
import jax.numpy as jnp
from jax import lax
from jax.experimental import pallas as pl
from jax.experimental.pallas import tpu as pltpu
from jax.sharding import PartitionSpec as P

MESH = pl.DeviceIdType.MESH
F32 = jnp.float32
BF16 = jnp.bfloat16
HD = 128
BLOCK = 512
TOP = 4
SCALE = HD ** (-0.5)
VMEM_BYTES = 60 * 1024 * 1024


def place():
    c = lax.axis_index("ctx")
    f = lax.axis_index("fsdp")
    return (
        lax.div(c, 4), lax.rem(c, 4),
        lax.div(f, 8), lax.rem(lax.div(f, 2), 4), lax.rem(f, 2),
    )


def device(z, y, zh, x, k):
    return (z * 4 + y, zh * 8 + x * 2 + k)


def turn(i, by):
    return lax.rem(i + by, 4)


def rows(start, size):
    return pl.ds(pl.multiple_of(start, size & -size), size)


class Mail:
    def __init__(self, send_sems):
        self.send_sems = send_sems
        self.used = 0
        self.sent = []

    def copy(self, src, dst, recv, dev):
        sem = self.send_sems.at[self.used]
        self.used += 1
        return pltpu.make_async_remote_copy(
            src_ref=src, dst_ref=dst, send_sem=sem, recv_sem=recv,
            device_id=dev, device_id_type=MESH,
        )

    def send(self, src, dst, recv, dev):
        copy = self.copy(src, dst, recv, dev)
        copy.start()
        self.sent.append((copy, None, None))

    def send_or_keep(self, away, src, dst, recv, dev):
        copy = self.copy(src, dst, recv, dev)
        stay = pltpu.make_async_copy(src, dst, recv)

        @pl.when(away)
        def _():
            copy.start()

        @pl.when(jnp.logical_not(away))
        def _():
            stay.start()

        self.sent.append((copy, away, None))

    def send_if(self, away, src, dst, recv, dev):
        copy = self.copy(src, dst, recv, dev)

        @pl.when(away)
        def _():
            copy.start()

        self.sent.append((copy, away, None))

    def flush(self):
        for copy, away, _ in self.sent:
            if away is None:
                copy.wait_send()
            else:
                pl.when(away)(copy.wait_send)


def got(dst, recv):
    pltpu.make_async_copy(dst, dst, recv).wait()


class Ring:
    def __init__(self, mail, view, pos, core, right, left, partner, ring, cores):
        self.mail, self.view, self.pos, self.core = mail, view, pos, core
        self.right, self.left, self.partner = right, left, partner
        self.ring, self.cores = ring, cores

    def pass_on(self, pos, half, recv, dev):
        ref = self.view(self.core, pos, half)
        self.mail.send(ref, ref, recv, dev)

    def across(self, pos, half, n):
        if self.partner is not None:
            self.pass_on(pos, half, self.cores.at[n], self.partner)

    def start(self):
        self.pass_on(self.pos, None, self.ring.at[0], self.right)
        self.pass_on(self.pos, None, self.ring.at[1], self.left)
        self.across(self.pos, None, 0)

    def relay(self):
        before, after = turn(self.pos, 3), turn(self.pos, 1)
        got(self.view(self.core, before, None), self.ring.at[0])
        self.pass_on(before, 0, self.ring.at[2], self.right)
        self.across(before, None, 1)
        got(self.view(self.core, after, None), self.ring.at[1])
        self.pass_on(after, 1, self.ring.at[3], self.left)
        self.across(after, None, 2)

    def finish(self):
        far = turn(self.pos, 2)
        for half in (0, 1):
            got(self.view(self.core, far, half), self.ring.at[2 + half])
            self.across(far, half, 3 + half)

    def settle(self):
        other = 1 - self.core
        before, after, far = turn(self.pos, 3), turn(self.pos, 1), turn(self.pos, 2)
        got(self.view(other, self.pos, None), self.cores.at[0])
        got(self.view(other, before, None), self.cores.at[1])
        got(self.view(other, after, None), self.cores.at[2])
        got(self.view(other, far, 0), self.cores.at[3])
        got(self.view(other, far, 1), self.cores.at[4])


def enter(devices, more=0):
    barrier = pltpu.get_barrier_semaphore()
    for dev in devices:
        pl.semaphore_signal(barrier, inc=1, device_id=dev, device_id_type=MESH)
    return barrier, len(devices) + more


def project_kernel(
    inp, w3, d_attn, q_out, kv_out, do_out, w_out,
    wall, xall, dall, part, parts_in, via_in, own, kvall,
    send_sems, load_sems, w_ring, w_cores, x_z, x_ring, d_sems, p_sems, via_sems,
    kv_ring, kv_cores, out_sems,
):
    z, y, zh, x, j = place()
    partner = device(z, y, zh, x, 1 - j)
    right = device(z, turn(y, 1), zh, x, j)
    left = device(z, turn(y, 3), zh, x, j)
    dq = wall.shape[1]
    d = dq // 4
    up = z >= 2
    end = jnp.logical_or(z == 0, z == 3)
    mid = jnp.logical_not(end)
    flip = lambda h: jnp.where(up, h, 3 - h)
    heads = (
        flip(jnp.where(end, 0, 2)), flip(jnp.where(end, 2, 0)), flip(1), flip(3),
    )
    inner = jnp.where(up, 2, 1)
    first = jnp.where(up, 0, 1)
    kv_cols, q_cols = pl.ds(0, 2 * HD), pl.ds(2 * HD, HD)

    loads = []
    for n, s in enumerate((first, 1 - first)):
        for at in (0, 1):
            loads.append(pltpu.make_async_copy(
                w3.at[1 + at, :, rows(HD * s, HD)],
                wall.at[2 * j + s, rows(d * y, d), pl.ds(HD * at, HD)],
                load_sems.at[2 * n + at],
            ))
    for s in (0, 1):
        loads.append(pltpu.make_async_copy(
            w3.at[0, :, pl.ds(HD * s, HD)],
            wall.at[2 * j + s, rows(d * y, d), q_cols],
            load_sems.at[4 + s],
        ))
    own_x = pltpu.make_async_copy(
        inp.at[rows(HD * j, HD), rows(dq * z, dq)], xall.at[pl.ds(0, HD)], load_sems.at[6]
    )
    for copy in loads:
        copy.start()
    own_x.start()

    peers = [device(turn(z, t), y, zh, x, k) for t in (1, 2, 3) for k in (j, 1 - j)]
    peers += [partner, right, left]
    peers += [device(z, y, zh, turn(x, u), j) for u in (1, 3)]
    barrier, expected = enter(peers)
    pl.semaphore_wait(barrier, expected)

    mail = Mail(send_sems)

    def w_view(s):
        def view(core, pos, half):
            if half is None:
                return wall.at[2 * core + s, rows(d * pos, d), kv_cols]
            return wall.at[2 * core + s, rows(d * pos + (d // 2) * half, d // 2), kv_cols]
        return view

    def q_view(core, pos, half):
        if half is None:
            return wall.at[pl.ds(2 * core, 2), rows(d * pos, d), q_cols]
        return wall.at[pl.ds(2 * core, 2), rows(d * pos + (d // 2) * half, d // 2), q_cols]

    w_rings = [
        Ring(mail, view, y, j, right, left, partner, w_ring.at[n], w_cores.at[n])
        for n, view in enumerate((w_view(first), w_view(1 - first), q_view))
    ]
    piece = HD // 4

    def x_view(t):
        def view(core, pos, half):
            if half is None:
                return xall.at[rows(HD * t + piece * pos, piece)]
            return xall.at[rows(HD * t + piece * pos + (piece // 2) * half, piece // 2)]
        return view

    x_rings = {
        t: Ring(
            mail, x_view(t), x, j, device(z, y, zh, turn(x, 1), j),
            device(z, y, zh, turn(x, 3), j), None, x_ring.at[t - 1], None,
        )
        for t in (1, 2, 3)
    }

    blocks = ((0, HD, 0, 2 * HD), (HD, 3 * HD, 0, 2 * HD), (0, 4 * HD, 2 * HD, HD))

    def project(p, i):
        low, size, col, wide = blocks[i]
        at, cols = pl.ds(low, size), pl.ds(col, wide)
        head = heads[p]
        total = jnp.dot(xall[at], wall[head, :, cols], preferred_element_type=F32)
        mine = part.at[p, at, cols]

        def keep():
            own[at, cols] = total

        def store():
            part[p, at, cols] = total.astype(BF16)

        def store_both():
            for n in ((0, 1), (), (2,))[i]:
                first_row, length, *_ = blocks[n]
                got(via_in.at[pl.ds(first_row, length), cols], via_sems.at[n])
            for t in range(low // HD, (low + size) // HD):
                there_t = turn(t, jnp.where(up, 3, 1))
                part[p, pl.ds(HD * t, HD), cols] = (
                    total[HD * t - low : HD * (t + 1) - low]
                    + via_in[rows(HD * there_t, HD), cols].astype(F32)
                ).astype(BF16)

        there = parts_in.at[z, at, cols]
        target = device(head, y, zh, x, j)
        if p == 0:
            pl.when(end)(store)
            pl.when(mid)(keep)
            mail.send_if(
                end, mine, via_in.at[at, cols], via_sems.at[i], device(inner, y, zh, x, j)
            )
        elif p == 1:
            pl.when(end)(store)
            pl.when(mid)(store_both)
            mail.send(mine, there, p_sems.at[z, i], target)
        elif p == 2:
            store()
            mail.send(mine, there, p_sems.at[z, i], target)
        else:
            pl.when(mid)(store)
            pl.when(end)(keep)
            mail.send_if(mid, mine, there, p_sems.at[z, i], target)

    for copy in loads[:2]:
        copy.wait()
    w_rings[0].start()
    for t in (1, 3, 2):
        zd = turn(z, t)
        back = 4 - t
        mail.send(
            inp.at[rows(HD * j + piece * x, piece), rows(dq * zd, dq)],
            xall.at[rows(HD * back + piece * x, piece)],
            x_z.at[back - 1], device(zd, y, zh, x, j),
        )
    for copy in loads[2:]:
        copy.wait()
    w_rings[0].relay()
    w_rings[1].start()
    for t in (1, 3, 2):
        got(xall.at[rows(HD * t + piece * x, piece)], x_z.at[t - 1])
        x_rings[t].start()
    own_x.wait()
    w_rings[0].finish()
    w_rings[0].settle()
    project(0, 0)
    for t in (1, 3, 2):
        x_rings[t].relay()
    w_rings[1].relay()
    w_rings[2].start()
    for t in (1, 3, 2):
        x_rings[t].finish()
    project(0, 1)
    project(1, 0)
    project(1, 1)
    w_rings[1].finish()
    w_rings[1].settle()
    project(2, 0)
    project(2, 1)
    project(3, 0)
    project(3, 1)
    w_rings[2].relay()
    w_rings[2].finish()
    w_rings[2].settle()
    keep_w = pltpu.make_async_copy(wall, w_out, out_sems.at[0])
    keep_w.start()
    for p in range(4):
        project(p, 2)
    for s in (0, 1):
        for k in (0, 1):
            zd = 2 * j + s
            away = jnp.logical_or(zd != z, j != k)
            mail.send_or_keep(
                away,
                d_attn.at[pl.ds(HD * k, HD), pl.ds(HD * s, HD)],
                dall.at[z], d_sems.at[z], device(zd, y, zh, x, k),
            )

    one = jnp.where(z == 1, 2, 1)
    two = jnp.where(end, 2, 0)

    def collect(which, cols, put):
        def arrived(source):
            for i in which:
                low, size, col, wide = blocks[i]
                got(parts_in.at[source, pl.ds(low, size), pl.ds(col, wide)], p_sems.at[source, i])

        def total(run):
            at = lambda source: rows(HD * lax.rem(run + 4 - source, 4), HD)
            term = lambda source: parts_in[source, at(source), cols].astype(F32)
            return own[at(z), cols] + term(one) + term(two), term

        arrived(one)
        arrived(two)

        @pl.when(mid)
        def _():
            arrived(3)
            for run in range(4):
                base, term = total(run)
                put(run, (base + term(3)).astype(BF16))

        @pl.when(end)
        def _():
            for run in range(4):
                put(run, total(run)[0].astype(BF16))

    def put_kv(run, low):
        kvall[run, y, j] = low

    def put_q(run, low):
        q_out[run] = low

    def kv_view(core, pos, half):
        if half is None:
            return kvall.at[:, pos, core]
        return kvall.at[pl.ds(2 * half, 2), pos, core]

    kv = Ring(mail, kv_view, y, j, right, left, partner, kv_ring, kv_cores)
    collect((0, 1), kv_cols, put_kv)
    kv.start()
    for zs in range(4):
        got(dall.at[zs], d_sems.at[zs])
    do_out[...] = dall[...]
    kv.relay()
    collect((2,), q_cols, put_q)
    kv.finish()
    kv.settle()
    keep_kv = pltpu.make_async_copy(kvall, kv_out, out_sems.at[1])
    keep_kv.start()
    mail.flush()
    keep_w.wait()
    keep_kv.wait()


def project_and_gather(inputs, w3, d_attn):
    rows_here, width = inputs.shape
    quarter = width // 4
    any_space = pl.BlockSpec(memory_space=pl.ANY)
    vmem = pl.BlockSpec(memory_space=pltpu.VMEM)
    dma = pltpu.SemaphoreType.DMA
    return pl.pallas_call(
        project_kernel,
        name="project_and_gather",
        out_shape=(
            jax.ShapeDtypeStruct((4, HD, HD), BF16),
            jax.ShapeDtypeStruct((4, 4, 2, HD, 2 * HD), BF16),
            jax.ShapeDtypeStruct((4, HD, HD), BF16),
            jax.ShapeDtypeStruct((4, quarter, 3 * HD), BF16),
        ),
        in_specs=[any_space] * 3,
        out_specs=(vmem, any_space, vmem, any_space),
        scratch_shapes=[
            pltpu.VMEM((4, quarter, 3 * HD), BF16),
            pltpu.VMEM((4 * HD, quarter), BF16),
            pltpu.VMEM((4, HD, HD), BF16),
            pltpu.VMEM((4, 4 * HD, 3 * HD), BF16),
            pltpu.VMEM((4, 4 * HD, 3 * HD), BF16),
            pltpu.VMEM((4 * HD, 3 * HD), BF16),
            pltpu.VMEM((4 * HD, 3 * HD), F32),
            pltpu.VMEM((4, 4, 2, HD, 2 * HD), BF16),
            dma((72,)), dma((7,)), dma((3, 4)), dma((3, 5)), dma((3,)), dma((3, 4)),
            dma((4,)), dma((4, 3)), dma((3,)), dma((4,)), dma((5,)), dma((2,)),
        ],
        compiler_params=pltpu.CompilerParams(
            collective_id=0, has_side_effects=True, vmem_limit_bytes=VMEM_BYTES
        ),
    )(inputs, w3, d_attn)


def attend_kernel(selected, q_ref, kv_ref, do_ref, dq_ref, dkv_ref, score, soft, total):
    _, y, _, _, j = place()
    total[...] = jnp.zeros_like(total)
    contract = lambda a, b: (((a,), (b,)), ((), ()))
    dot = functools.partial(lax.dot_general, preferred_element_type=F32)
    key_at = lax.broadcasted_iota(jnp.int32, (BLOCK, HD), 0)
    query_at = lax.broadcasted_iota(jnp.int32, (BLOCK, HD), 1)

    def tile(run, carry):
        first = (run * 4 + y) * 256 + HD * j
        block = lax.div(first, BLOCK)
        q = q_ref[run]
        do = do_ref[run]
        highest = jnp.full((1, HD), -jnp.inf, F32)
        for t in range(TOP):
            chosen = selected[t, block]
            kb = jnp.maximum(chosen, 0)
            s = dot(kv_ref[kb, :, :HD], q, contract(1, 1)) * SCALE
            limit = jnp.where(chosen >= 0, first - kb * BLOCK, -2 * BLOCK)
            s = jnp.where(key_at - query_at <= limit, s, -jnp.inf)
            score[t] = s
            highest = jnp.maximum(highest, jnp.max(s, axis=0, keepdims=True))
        totals = jnp.zeros((1, HD), F32)
        for t in range(TOP):
            e = jnp.exp(score[t] - highest)
            score[t] = e
            totals += jnp.sum(e, axis=0, keepdims=True)
        share = 1.0 / totals
        attended = jnp.zeros((HD, HD), F32)
        for t in range(TOP):
            kb = jnp.maximum(selected[t, block], 0)
            p = score[t] * share
            low = p.astype(BF16)
            score[t] = p
            soft[t] = low
            attended += dot(kv_ref[kb, :, HD:], low, contract(0, 0))
        attended = attended.astype(BF16).astype(F32)
        delta = jnp.sum(do.astype(F32).T * attended, axis=0, keepdims=True)
        dq = jnp.zeros((HD, HD), F32)
        for t in range(TOP):
            kb = jnp.maximum(selected[t, block], 0)
            dp = dot(kv_ref[kb, :, HD:], do, contract(1, 1))
            ds = (score[t] * (dp - delta)).astype(BF16)
            total[kb, :, :HD] += dot(ds, q, contract(1, 0))
            total[kb, :, HD:] += dot(soft[t], do, contract(1, 0))
            dq += dot(ds, kv_ref[kb, :, :HD], contract(0, 0))
        dq_ref[run] = (dq * SCALE).astype(BF16)
        return carry

    lax.fori_loop(0, 4, tile, 0)
    for b in range(8):
        dkv_ref[b, :, :HD] = (total[b, :, :HD] * SCALE).astype(BF16)
        dkv_ref[b, :, HD:] = total[b, :, HD:].astype(BF16)


def attend(selected, q, kv, do):
    vmem = pl.BlockSpec(memory_space=pltpu.VMEM)
    return pl.pallas_call(
        attend_kernel,
        name="attend",
        out_shape=(
            jax.ShapeDtypeStruct((4, HD, HD), BF16),
            jax.ShapeDtypeStruct((8, BLOCK, 2 * HD), BF16),
        ),
        in_specs=[pl.BlockSpec(memory_space=pltpu.SMEM), vmem, vmem, vmem],
        out_specs=(vmem, vmem),
        scratch_shapes=[
            pltpu.VMEM((TOP, BLOCK, HD), F32),
            pltpu.VMEM((TOP, BLOCK, HD), BF16),
            pltpu.VMEM((8, BLOCK, 2 * HD), F32),
        ],
        compiler_params=pltpu.CompilerParams(vmem_limit_bytes=VMEM_BYTES),
    )(selected, q, kv, do)


def owner_x(z, jj):
    at = jnp.where(lax.rem(jj, 2) == 0, lax.div(jj, 2), lax.div(7 - jj, 2))
    return turn(at, 2 * lax.rem(z, 2))


def block_of(z, x):
    at = turn(x, 2 * lax.rem(z, 2))
    return jnp.where(at < 2, 2 * at, 7 - 2 * at)


def gradient_kernel(
    dkv, dq, w_in, out,
    wall, gall, core_in, far_out, near_out, far_in, near_in, own_kv,
    xf_out, xn_out, xf_in, xn_in, own_x, fin, fin_in,
    send_sems, load_sem, core_sems, far_sems, near_sems, q_sems, g_sems, xf_sems, xn_sems, f_sems,
):
    z, y, zh, x, j = place()
    d = wall.shape[1] // 4
    f = lax.axis_index("fsdp")
    partner = device(z, y, zh, x, 1 - j)
    right = device(z, turn(y, 1), zh, x, j)
    left = device(z, turn(y, 3), zh, x, j)
    x_right = device(z, y, zh, turn(x, 1), j)
    x_left = device(z, y, zh, turn(x, 3), j)
    up = z >= 2
    end = jnp.logical_or(z == 0, z == 3)
    mid = jnp.logical_not(end)
    flip = lambda h: jnp.where(up, h, 3 - h)
    at_z = lambda h: device(h, y, zh, x, j)
    first_z = flip(jnp.where(end, 2, 1))
    second_z = flip(jnp.where(end, 1, 3))
    far_z = flip(0)

    load = pltpu.make_async_copy(w_in, wall, load_sem)
    load.start()

    across = [at_z(turn(z, t)) for t in (1, 2, 3)]
    barrier, expected = enter([partner, right, left, x_right, x_left] + across, more=4)
    source_z = lax.div(f, 4)
    source_x = owner_x(source_z, lax.rem(f, 4))
    for h in (0, 1):
        for k in (0, 1):
            pl.semaphore_signal(
                barrier, inc=1, device_id=device(source_z, y, h, source_x, k),
                device_id_type=MESH,
            )
    pl.semaphore_wait(barrier, expected)

    mail = Mail(send_sems)

    def spread(src, at, cols, sems):
        there = gall.at[z, at, cols]
        mail.send(src, there, sems.at[z], at_z(first_z))
        mail.send_if(mid, src, there, sems.at[z], at_z(far_z))
        mail.send(src, there, sems.at[z], at_z(second_z))

    def forward(at, cols, sems):
        block = gall.at[far_z, at, cols]
        pl.when(mid)(lambda: got(block, sems.at[far_z]))
        mail.send_if(mid, block, block, sems.at[far_z], at_z(second_z))

    def gathered(at, cols, sems):
        for h in (flip(1), flip(2)):
            pl.when(h != z)(lambda: got(gall.at[h, at, cols], sems.at[h]))
        outer = jnp.where(end, 3 - z, second_z)
        got(gall.at[outer, at, cols], sems.at[outer])

    every, q_cols, kv_cols = pl.ds(0, 4 * HD), pl.ds(2 * HD, HD), pl.ds(0, 2 * HD)
    for n, t in enumerate((2, 1, 3, 0)):
        mail.send(dkv.at[:, turn(y, t), 1 - j], core_in.at[n], core_sems.at[n], partner)
    spread(dq, every, q_cols, q_sems)
    gall[z, :, q_cols] = dq[...]

    def chip_sum(n, t, run):
        return dkv[run, turn(y, t), j].astype(F32) + core_in[n, run].astype(F32)

    def far(h):
        for side, dev in ((0, right), (1, left)):
            far_out[h, side] = chip_sum(0, 2, 2 * h + side).astype(BF16)
            mail.send(far_out.at[h, side], far_in.at[h, side], far_sems.at[h, side], dev)

    def near(h, term):
        for side, (t, dev) in enumerate(((1, right), (3, left))):
            lane = side if term else 1 - side
            total = chip_sum(1 + side, t, 2 * h + lane)
            if term:
                got(far_in.at[h, side], far_sems.at[h, side])
                total += far_in[h, side].astype(F32)
            near_out[h, side, lane] = total.astype(BF16)
            mail.send(
                near_out.at[h, side, lane], near_in.at[h, side, lane],
                near_sems.at[h, side, lane], dev,
            )

    def finish_kv(h):
        for lane in (0, 1):
            for side in (1 - lane, lane):
                got(near_in.at[h, side, lane], near_sems.at[h, side, lane])
        for lane in (0, 1):
            run = 2 * h + lane
            total = chip_sum(3, 0, run)
            for side in (0, 1):
                total += near_in[h, side, lane].astype(F32)
            gall[z, pl.ds(HD * run, HD), kv_cols] = total.astype(BF16)
        at = pl.ds(2 * HD * h, 2 * HD)
        spread(gall.at[z, at, kv_cols], at, kv_cols, g_sems.at[h])

    got(core_in.at[0], core_sems.at[0])
    far(0)
    got(core_in.at[1], core_sems.at[1])
    got(core_in.at[2], core_sems.at[2])
    near(0, False)
    far(1)
    got(core_in.at[3], core_sems.at[3])
    near(0, True)
    near(1, False)
    forward(every, q_cols, q_sems)
    finish_kv(0)
    near(1, True)
    finish_kv(1)

    def part(t, h):
        cols = rows(d * block_of(z, turn(x, t)), d)
        at = pl.ds(2 * HD * h, 2 * HD)
        total = jnp.zeros((d, 2 * HD), F32)
        for head in range(4):
            total += lax.dot_general(
                wall[head, cols], gall[head, at], (((1,), (1,)), ((), ())),
                preferred_element_type=F32,
            )
        return total

    def x_first(h):
        total = part(2, h).astype(BF16)
        for side, dev in ((0, x_right), (1, x_left)):
            xf_out[h, side] = total[:, HD * side : HD * (side + 1)]
            mail.send(xf_out.at[h, side], xf_in.at[h, side], xf_sems.at[h, side], dev)
        for side, (t, dev) in enumerate(((1, x_right), (3, x_left))):
            total = part(t, h)
            alone = 1 - side
            xn_out[h, side, alone] = total[:, HD * alone : HD * (alone + 1)].astype(BF16)
            own_x[h, side] = total[:, HD * side : HD * (side + 1)]
            mail.send(
                xn_out.at[h, side, alone], xn_in.at[h, side, alone],
                xn_sems.at[h, side, alone], dev,
            )

    def x_second(h):
        for side, dev in ((0, x_right), (1, x_left)):
            got(xf_in.at[h, side], xf_sems.at[h, side])
            xn_out[h, side, side] = (
                own_x[h, side] + xf_in[h, side].astype(F32)
            ).astype(BF16)
            mail.send(
                xn_out.at[h, side, side], xn_in.at[h, side, side], xn_sems.at[h, side, side], dev
            )
        total = part(0, h)
        for lane in (0, 1):
            own_x[h, lane] = total[:, HD * lane : HD * (lane + 1)]

    fd = 4 * z + block_of(z, x)

    def x_third(h):
        for lane in (0, 1):
            total = own_x[h, lane]
            for side in (1 - lane, lane):
                got(xn_in.at[h, side, lane], xn_sems.at[h, side, lane])
                total += xn_in[h, side, lane].astype(F32)
            run = 2 * h + lane
            fin[run] = total.astype(BF16)
            mail.send_or_keep(
                jnp.logical_or(run != z, fd != f), fin.at[run], fin_in.at[zh, j],
                f_sems.at[zh, j], (run * 4 + y, fd),
            )

    load.wait()
    gathered(every, q_cols, q_sems)
    halves = [pl.ds(2 * HD * h, 2 * HD) for h in (0, 1)]
    forward(halves[0], kv_cols, g_sems.at[0])
    gathered(halves[0], kv_cols, g_sems.at[0])
    x_first(0)
    forward(halves[1], kv_cols, g_sems.at[1])
    x_second(0)
    gathered(halves[1], kv_cols, g_sems.at[1])
    x_first(1)
    x_third(0)
    x_second(1)
    x_third(1)
    for h in (0, 1):
        for k in (0, 1):
            got(fin_in.at[h, k], f_sems.at[h, k])
    for k in (0, 1):
        out[pl.ds(HD * k, HD)] = (
            (fin_in[0, k].astype(F32) + fin_in[1, k].astype(F32)).T
        ).astype(BF16)
    mail.flush()


def input_gradient(dkv, dq, w_all):
    quarter = w_all.shape[1]
    d = quarter // 4
    any_space = pl.BlockSpec(memory_space=pl.ANY)
    vmem = pl.BlockSpec(memory_space=pltpu.VMEM)
    dma = pltpu.SemaphoreType.DMA
    run = (HD, 2 * HD)
    block = (d, HD)
    return pl.pallas_call(
        gradient_kernel,
        name="input_gradient",
        out_shape=jax.ShapeDtypeStruct((2 * HD, d), BF16),
        in_specs=[vmem, vmem, any_space],
        out_specs=vmem,
        scratch_shapes=[
            pltpu.VMEM(w_all.shape, BF16),
            pltpu.VMEM((4, 4 * HD, 3 * HD), BF16),
            pltpu.VMEM((4, 4) + run, BF16),
            pltpu.VMEM((2, 2) + run, BF16),
            pltpu.VMEM((2, 2, 2) + run, BF16),
            pltpu.VMEM((2, 2) + run, BF16),
            pltpu.VMEM((2, 2, 2) + run, BF16),
            pltpu.VMEM((2, 2) + run, F32),
            pltpu.VMEM((2, 2) + block, BF16),
            pltpu.VMEM((2, 2, 2) + block, BF16),
            pltpu.VMEM((2, 2) + block, BF16),
            pltpu.VMEM((2, 2, 2) + block, BF16),
            pltpu.VMEM((2, 2) + block, F32),
            pltpu.VMEM((4,) + block, BF16),
            pltpu.VMEM((2, 2) + block, BF16),
            dma((48,)), dma, dma((4,)), dma((2, 2)), dma((2, 2, 2)), dma((4,)), dma((2, 4)),
            dma((2, 2)), dma((2, 2, 2)), dma((2, 2)),
        ],
        compiler_params=pltpu.CompilerParams(
            collective_id=1, has_side_effects=True, vmem_limit_bytes=VMEM_BYTES
        ),
    )(dkv, dq, w_all)


def shards(inputs, w_qkv, selected, d_attn):
    w3 = w_qkv.transpose(1, 0, 2)
    q, kv, do, w_all = project_and_gather(inputs, w3, d_attn)
    dq, dkv = attend(
        selected.T, q, kv.reshape(8, BLOCK, 2 * HD), do
    )
    return input_gradient(dkv.reshape(4, 4, 2, HD, 2 * HD), dq.reshape(4 * HD, HD), w_all)


def solution(mesh):
    placed = (P("ctx", None), P("ctx", None, "fsdp"), P(), P("ctx", "fsdp"))
    return jax.shard_map(
        shards, mesh=mesh, in_specs=placed, out_specs=P("ctx", "fsdp"), check_vma=False
    )
```

```python
import functools

import jax
import jax.numpy as jnp
from jax import lax
from jax.experimental import pallas as pl
from jax.experimental.pallas import tpu as pltpu
from jax.sharding import PartitionSpec as P

MESH = pl.DeviceIdType.MESH
F32 = jnp.float32
BF16 = jnp.bfloat16
HD = 128
BLOCK = 512
TOP = 4
SCALE = HD ** (-0.5)
VMEM_BYTES = 60 * 1024 * 1024


def place():
    c = lax.axis_index("ctx")
    f = lax.axis_index("fsdp")
    return (
        lax.div(c, 4), lax.rem(c, 4),
        lax.div(f, 8), lax.rem(lax.div(f, 2), 4), lax.rem(f, 2),
    )


def device(z, y, zh, x, k):
    return (z * 4 + y, zh * 8 + x * 2 + k)


def around(z, y, zh, x, k, by):
    at = lax.rem(4 * zh + z + 8 + by, 8)
    return device(lax.rem(at, 4), y, lax.div(at, 4), x, k)


def turn(i, by):
    return lax.rem(i + by, 4)


def rows(start, size):
    return pl.ds(pl.multiple_of(start, size & -size), size)


class Mail:
    def __init__(self, send_sems):
        self.send_sems = send_sems
        self.used = 0
        self.sent = []

    def copy(self, src, dst, recv, dev):
        sem = self.send_sems.at[self.used]
        self.used += 1
        return pltpu.make_async_remote_copy(
            src_ref=src, dst_ref=dst, send_sem=sem, recv_sem=recv,
            device_id=dev, device_id_type=MESH,
        )

    def send(self, src, dst, recv, dev):
        copy = self.copy(src, dst, recv, dev)
        copy.start()
        self.sent.append((copy, None, None))

    def send_or_keep(self, away, src, dst, recv, dev):
        copy = self.copy(src, dst, recv, dev)
        stay = pltpu.make_async_copy(src, dst, recv)

        @pl.when(away)
        def _():
            copy.start()

        @pl.when(jnp.logical_not(away))
        def _():
            stay.start()

        self.sent.append((copy, away, None))

    def send_if(self, away, src, dst, recv, dev):
        copy = self.copy(src, dst, recv, dev)

        @pl.when(away)
        def _():
            copy.start()

        self.sent.append((copy, away, None))

    def flush(self):
        for copy, away, _ in self.sent:
            if away is None:
                copy.wait_send()
            else:
                pl.when(away)(copy.wait_send)


def got(dst, recv):
    pltpu.make_async_copy(dst, dst, recv).wait()


class Ring:
    def __init__(self, mail, view, pos, core, right, left, partner, ring, cores):
        self.mail, self.view, self.pos, self.core = mail, view, pos, core
        self.right, self.left, self.partner = right, left, partner
        self.ring, self.cores = ring, cores

    def pass_on(self, pos, half, recv, dev):
        ref = self.view(self.core, pos, half)
        self.mail.send(ref, ref, recv, dev)

    def across(self, pos, half, n):
        if self.partner is not None:
            self.pass_on(pos, half, self.cores.at[n], self.partner)

    def start(self):
        self.pass_on(self.pos, None, self.ring.at[0], self.right)
        self.pass_on(self.pos, None, self.ring.at[1], self.left)
        self.across(self.pos, None, 0)

    def relay(self):
        before, after = turn(self.pos, 3), turn(self.pos, 1)
        got(self.view(self.core, before, None), self.ring.at[0])
        self.pass_on(before, 0, self.ring.at[2], self.right)
        self.across(before, None, 1)
        got(self.view(self.core, after, None), self.ring.at[1])
        self.pass_on(after, 1, self.ring.at[3], self.left)
        self.across(after, None, 2)

    def finish(self):
        far = turn(self.pos, 2)
        for half in (0, 1):
            got(self.view(self.core, far, half), self.ring.at[2 + half])
            self.across(far, half, 3 + half)

    def settle(self):
        other = 1 - self.core
        before, after, far = turn(self.pos, 3), turn(self.pos, 1), turn(self.pos, 2)
        got(self.view(other, self.pos, None), self.cores.at[0])
        got(self.view(other, before, None), self.cores.at[1])
        got(self.view(other, after, None), self.cores.at[2])
        got(self.view(other, far, 0), self.cores.at[3])
        got(self.view(other, far, 1), self.cores.at[4])


def enter(devices, more=0):
    barrier = pltpu.get_barrier_semaphore()
    for dev in devices:
        pl.semaphore_signal(barrier, inc=1, device_id=dev, device_id_type=MESH)
    return barrier, len(devices) + more


def project_kernel(
    inp, w3, d_attn, q_out, kv_out, do_out, w_out,
    wall, xall, dall, part, parts_in, via_in, own, kvall,
    send_sems, load_sems, w_ring, w_cores, x_z, x_x, d_sems, p_sems, via_sems,
    kv_ring, kv_cores, out_sems,
):
    z, y, zh, x, j = place()
    partner = device(z, y, zh, x, 1 - j)
    right = device(z, turn(y, 1), zh, x, j)
    left = device(z, turn(y, 3), zh, x, j)
    dq = wall.shape[1]
    d = dq // 4
    up = z >= 2
    end = jnp.logical_or(z == 0, z == 3)
    mid = jnp.logical_not(end)
    flip = lambda h: jnp.where(up, h, 3 - h)
    heads = (
        flip(jnp.where(end, 0, 2)), flip(jnp.where(end, 2, 0)), flip(1), flip(3),
    )
    inner = jnp.where(up, 2, 1)
    first = jnp.where(up, 0, 1)
    kv_cols, q_cols = pl.ds(0, 2 * HD), pl.ds(2 * HD, HD)

    loads = []
    for n, s in enumerate((first, 1 - first)):
        for at in (0, 1):
            loads.append(pltpu.make_async_copy(
                w3.at[1 + at, :, rows(HD * s, HD)],
                wall.at[2 * j + s, rows(d * y, d), pl.ds(HD * at, HD)],
                load_sems.at[2 * n + at],
            ))
    for s in (0, 1):
        loads.append(pltpu.make_async_copy(
            w3.at[0, :, pl.ds(HD * s, HD)],
            wall.at[2 * j + s, rows(d * y, d), q_cols],
            load_sems.at[4 + s],
        ))
    own_x = pltpu.make_async_copy(
        inp.at[rows(HD * j, HD), rows(dq * z, dq)], xall.at[rows(HD * z, HD)], load_sems.at[6]
    )
    for copy in loads:
        copy.start()
    own_x.start()

    peers = [device(turn(z, t), y, zh, x, k) for t in (1, 2, 3) for k in (j, 1 - j)]
    peers += [partner, right, left]
    peers += [device(z, y, zh, turn(x, u), j) for u in (1, 3)]
    peers += [around(z, y, zh, x, j, by) for by in (1, -1, 2, -2)]
    barrier, expected = enter(peers)
    pl.semaphore_wait(barrier, expected)

    mail = Mail(send_sems)

    def w_view(s):
        def view(core, pos, half):
            if half is None:
                return wall.at[2 * core + s, rows(d * pos, d), kv_cols]
            return wall.at[2 * core + s, rows(d * pos + (d // 2) * half, d // 2), kv_cols]
        return view

    def q_view(core, pos, half):
        if half is None:
            return wall.at[pl.ds(2 * core, 2), rows(d * pos, d), q_cols]
        return wall.at[pl.ds(2 * core, 2), rows(d * pos + (d // 2) * half, d // 2), q_cols]

    w_rings = [
        Ring(mail, view, y, j, right, left, partner, w_ring.at[n], w_cores.at[n])
        for n, view in enumerate((w_view(first), w_view(1 - first), q_view))
    ]
    piece = HD // 4

    def quarter(run, of_x, low=0, size=piece):
        return xall.at[rows(HD * run + piece * of_x + low, size)]

    hops = ((1, 0, piece), (-1, 0, piece), (2, 0, piece // 2), (-2, piece // 2, piece // 2))
    opposite = turn(x, 2)

    def x_send(turn_of):
        of_x = (x, opposite)[turn_of]
        for n, (by, low, size) in enumerate(hops):
            mail.send(
                inp.at[rows(HD * j + piece * of_x + low, size), rows(dq * turn(z, 4 + by), dq)],
                quarter(z, of_x, low, size), x_z.at[turn_of, n], around(z, y, zh, x, j, by),
            )

    def x_got(turn_of, n):
        by, low, size = hops[n]
        got(quarter(turn(z, 4 - by), (x, opposite)[turn_of], low, size), x_z.at[turn_of, n])

    def x_share(by):
        mine = quarter(turn(z, 4 - by), x)
        for u in (1, 3):
            mail.send(
                mine, mine, x_x.at[by % 4, u // 2], device(z, y, zh, turn(x, u), j)
            )

    def x_shared(by):
        for u in (1, 3):
            got(quarter(turn(z, 4 - by), turn(x, 4 - u)), x_x.at[by % 4, u // 2])

    blocks = (
        (0, 2 * HD, 0, 2 * HD), (2 * HD, 2 * HD, 0, 2 * HD), (0, 4 * HD, 2 * HD, HD),
    )

    def project(p, i):
        low, size, col, wide = blocks[i]
        at, cols = pl.ds(low, size), pl.ds(col, wide)
        head = heads[p]
        total = jnp.dot(xall[at], wall[head, :, cols], preferred_element_type=F32)
        mine = part.at[p, at, cols]

        def keep():
            own[at, cols] = total

        def store():
            part[p, at, cols] = total.astype(BF16)

        def store_both():
            got(via_in.at[at, cols], via_sems.at[i])
            part[p, at, cols] = (total + via_in[at, cols].astype(F32)).astype(BF16)

        there = parts_in.at[z, at, cols]
        target = device(head, y, zh, x, j)
        if p == 0:
            pl.when(end)(store)
            pl.when(mid)(keep)
            mail.send_if(
                end, mine, via_in.at[at, cols], via_sems.at[i], device(inner, y, zh, x, j)
            )
        elif p == 1:
            pl.when(end)(store)
            pl.when(mid)(store_both)
            mail.send(mine, there, p_sems.at[z, i], target)
        elif p == 2:
            store()
            mail.send(mine, there, p_sems.at[z, i], target)
        else:
            pl.when(mid)(store)
            pl.when(end)(keep)
            mail.send_if(mid, mine, there, p_sems.at[z, i], target)

    for copy in loads[:2]:
        copy.wait()
    w_rings[0].start()
    x_send(0)
    x_send(1)
    for copy in loads[2:]:
        copy.wait()
    for n, by in ((0, 1), (1, -1)):
        x_got(0, n)
        x_share(by)
    w_rings[0].relay()
    w_rings[1].start()
    w_rings[2].start()
    x_got(0, 2)
    x_got(0, 3)
    x_share(2)
    own_x.wait()
    w_rings[0].finish()
    w_rings[0].settle()
    for by in (1, -1, 2):
        x_shared(by)
    for n in range(4):
        x_got(1, n)
    for i in (0, 1):
        project(0, i)
        project(1, i)
    w_rings[1].relay()
    w_rings[1].finish()
    w_rings[2].relay()
    w_rings[1].settle()
    for i in (0, 1):
        project(2, i)
        project(3, i)
    w_rings[2].finish()
    w_rings[2].settle()
    keep_w = pltpu.make_async_copy(wall, w_out, out_sems.at[0])
    keep_w.start()
    for p in range(4):
        project(p, 2)
    for s in (0, 1):
        for k in (0, 1):
            zd = 2 * j + s
            away = jnp.logical_or(zd != z, j != k)
            mail.send_or_keep(
                away,
                d_attn.at[pl.ds(HD * k, HD), pl.ds(HD * s, HD)],
                dall.at[z], d_sems.at[z], device(zd, y, zh, x, k),
            )

    one = jnp.where(z == 1, 2, 1)
    two = jnp.where(end, 2, 0)

    def collect(i, put):
        low, size, col, wide = blocks[i]
        at, cols = pl.ds(low, size), pl.ds(col, wide)
        arrived = lambda source: got(parts_in.at[source, at, cols], p_sems.at[source, i])
        term = lambda source: parts_in[source, at, cols].astype(F32)
        arrived(one)
        arrived(two)

        @pl.when(mid)
        def _():
            arrived(3)
            put((own[at, cols] + term(one) + term(two) + term(3)).astype(BF16))

        @pl.when(end)
        def _():
            put((own[at, cols] + term(one) + term(two)).astype(BF16))

    def put_kv(h):
        def put(low):
            for run in (0, 1):
                kvall[2 * h + run, y, j] = low[HD * run : HD * (run + 1)]
        return put

    def put_q(low):
        for run in range(4):
            q_out[run] = low[HD * run : HD * (run + 1)]

    def kv_view(h):
        def view(core, pos, half):
            if half is None:
                return kvall.at[pl.ds(2 * h, 2), pos, core]
            return kvall.at[pl.ds(2 * h + half, 1), pos, core]
        return view

    kv = [
        Ring(mail, kv_view(h), y, j, right, left, partner, kv_ring.at[h], kv_cores.at[h])
        for h in (0, 1)
    ]
    for h in (0, 1):
        collect(h, put_kv(h))
        kv[h].start()
    for h in (0, 1):
        kv[h].relay()
    for zs in range(4):
        got(dall.at[zs], d_sems.at[zs])
    do_out[...] = dall[...]
    collect(2, put_q)
    for h in (0, 1):
        kv[h].finish()
    for h in (0, 1):
        kv[h].settle()
    keep_kv = pltpu.make_async_copy(kvall, kv_out, out_sems.at[1])
    keep_kv.start()
    mail.flush()
    keep_w.wait()
    keep_kv.wait()


def project_and_gather(inputs, w3, d_attn):
    rows_here, width = inputs.shape
    quarter = width // 4
    any_space = pl.BlockSpec(memory_space=pl.ANY)
    vmem = pl.BlockSpec(memory_space=pltpu.VMEM)
    dma = pltpu.SemaphoreType.DMA
    return pl.pallas_call(
        project_kernel,
        name="project_and_gather",
        out_shape=(
            jax.ShapeDtypeStruct((4, HD, HD), BF16),
            jax.ShapeDtypeStruct((4, 4, 2, HD, 2 * HD), BF16),
            jax.ShapeDtypeStruct((4, HD, HD), BF16),
            jax.ShapeDtypeStruct((4, quarter, 3 * HD), BF16),
        ),
        in_specs=[any_space] * 3,
        out_specs=(vmem, any_space, vmem, any_space),
        scratch_shapes=[
            pltpu.VMEM((4, quarter, 3 * HD), BF16),
            pltpu.VMEM((4 * HD, quarter), BF16),
            pltpu.VMEM((4, HD, HD), BF16),
            pltpu.VMEM((4, 4 * HD, 3 * HD), BF16),
            pltpu.VMEM((4, 4 * HD, 3 * HD), BF16),
            pltpu.VMEM((4 * HD, 3 * HD), BF16),
            pltpu.VMEM((4 * HD, 3 * HD), F32),
            pltpu.VMEM((4, 4, 2, HD, 2 * HD), BF16),
            dma((80,)), dma((7,)), dma((3, 4)), dma((3, 5)), dma((2, 4)), dma((4, 2)),
            dma((4,)), dma((4, 3)), dma((3,)), dma((2, 4)), dma((2, 5)), dma((2,)),
        ],
        compiler_params=pltpu.CompilerParams(
            collective_id=0, has_side_effects=True, vmem_limit_bytes=VMEM_BYTES
        ),
    )(inputs, w3, d_attn)


def attend_kernel(selected, q_ref, kv_ref, do_ref, dq_ref, dkv_ref, score, soft, total):
    _, y, _, _, j = place()
    total[...] = jnp.zeros_like(total)
    contract = lambda a, b: (((a,), (b,)), ((), ()))
    dot = functools.partial(lax.dot_general, preferred_element_type=F32)
    key_at = lax.broadcasted_iota(jnp.int32, (BLOCK, HD), 0)
    query_at = lax.broadcasted_iota(jnp.int32, (BLOCK, HD), 1)

    def tile(run, carry):
        first = (run * 4 + y) * 256 + HD * j
        block = lax.div(first, BLOCK)
        q = q_ref[run]
        do = do_ref[run]
        highest = jnp.full((1, HD), -jnp.inf, F32)
        for t in range(TOP):
            chosen = selected[t, block]
            kb = jnp.maximum(chosen, 0)
            s = dot(kv_ref[kb, :, :HD], q, contract(1, 1)) * SCALE
            limit = jnp.where(chosen >= 0, first - kb * BLOCK, -2 * BLOCK)
            s = jnp.where(key_at - query_at <= limit, s, -jnp.inf)
            score[t] = s
            highest = jnp.maximum(highest, jnp.max(s, axis=0, keepdims=True))
        totals = jnp.zeros((1, HD), F32)
        for t in range(TOP):
            e = jnp.exp(score[t] - highest)
            score[t] = e
            totals += jnp.sum(e, axis=0, keepdims=True)
        share = 1.0 / totals
        attended = jnp.zeros((HD, HD), F32)
        for t in range(TOP):
            kb = jnp.maximum(selected[t, block], 0)
            p = score[t] * share
            low = p.astype(BF16)
            score[t] = p
            soft[t] = low
            attended += dot(kv_ref[kb, :, HD:], low, contract(0, 0))
        attended = attended.astype(BF16).astype(F32)
        delta = jnp.sum(do.astype(F32).T * attended, axis=0, keepdims=True)
        dq = jnp.zeros((HD, HD), F32)
        for t in range(TOP):
            kb = jnp.maximum(selected[t, block], 0)
            dp = dot(kv_ref[kb, :, HD:], do, contract(1, 1))
            ds = (score[t] * (dp - delta)).astype(BF16)
            total[kb, :, :HD] += dot(ds, q, contract(1, 0))
            total[kb, :, HD:] += dot(soft[t], do, contract(1, 0))
            dq += dot(ds, kv_ref[kb, :, :HD], contract(0, 0))
        dq_ref[run] = (dq * SCALE).astype(BF16)
        return carry

    lax.fori_loop(0, 4, tile, 0)
    for b in range(8):
        dkv_ref[b, :, :HD] = (total[b, :, :HD] * SCALE).astype(BF16)
        dkv_ref[b, :, HD:] = total[b, :, HD:].astype(BF16)


def attend(selected, q, kv, do):
    vmem = pl.BlockSpec(memory_space=pltpu.VMEM)
    return pl.pallas_call(
        attend_kernel,
        name="attend",
        out_shape=(
            jax.ShapeDtypeStruct((4, HD, HD), BF16),
            jax.ShapeDtypeStruct((8, BLOCK, 2 * HD), BF16),
        ),
        in_specs=[pl.BlockSpec(memory_space=pltpu.SMEM), vmem, vmem, vmem],
        out_specs=(vmem, vmem),
        scratch_shapes=[
            pltpu.VMEM((TOP, BLOCK, HD), F32),
            pltpu.VMEM((TOP, BLOCK, HD), BF16),
            pltpu.VMEM((8, BLOCK, 2 * HD), F32),
        ],
        compiler_params=pltpu.CompilerParams(vmem_limit_bytes=VMEM_BYTES),
    )(selected, q, kv, do)


def owner_x(z, jj):
    at = jnp.where(lax.rem(jj, 2) == 0, lax.div(jj, 2), lax.div(7 - jj, 2))
    return turn(at, 2 * lax.rem(z, 2))


def block_of(z, x):
    at = turn(x, 2 * lax.rem(z, 2))
    return jnp.where(at < 2, 2 * at, 7 - 2 * at)


def gradient_kernel(
    dkv, dq, w_in, out,
    wall, gall, core_in, far_out, near_out, far_in, near_in, own_kv,
    xf_out, xn_out, xf_in, xn_in, own_x, fin, fin_in,
    send_sems, load_sem, core_sems, far_sems, near_sems, q_sems, g_sems, xf_sems, xn_sems, f_sems,
):
    z, y, zh, x, j = place()
    d = wall.shape[1] // 4
    f = lax.axis_index("fsdp")
    partner = device(z, y, zh, x, 1 - j)
    right = device(z, turn(y, 1), zh, x, j)
    left = device(z, turn(y, 3), zh, x, j)
    x_right = device(z, y, zh, turn(x, 1), j)
    x_left = device(z, y, zh, turn(x, 3), j)
    up = z >= 2
    end = jnp.logical_or(z == 0, z == 3)
    mid = jnp.logical_not(end)
    flip = lambda h: jnp.where(up, h, 3 - h)
    at_z = lambda h: device(h, y, zh, x, j)
    first_z = flip(jnp.where(end, 2, 1))
    second_z = flip(jnp.where(end, 1, 3))
    far_z = flip(0)

    load = pltpu.make_async_copy(w_in, wall, load_sem)
    load.start()

    across = [at_z(turn(z, t)) for t in (1, 2, 3)]
    barrier, expected = enter([partner, right, left, x_right, x_left] + across, more=4)
    source_z = lax.div(f, 4)
    source_x = owner_x(source_z, lax.rem(f, 4))
    for h in (0, 1):
        for k in (0, 1):
            pl.semaphore_signal(
                barrier, inc=1, device_id=device(source_z, y, h, source_x, k),
                device_id_type=MESH,
            )
    pl.semaphore_wait(barrier, expected)

    mail = Mail(send_sems)

    def spread(src, at, cols, sems):
        there = gall.at[z, at, cols]
        mail.send(src, there, sems.at[z], at_z(first_z))
        mail.send_if(mid, src, there, sems.at[z], at_z(far_z))
        mail.send(src, there, sems.at[z], at_z(second_z))

    def forward(at, cols, sems):
        block = gall.at[far_z, at, cols]
        pl.when(mid)(lambda: got(block, sems.at[far_z]))
        mail.send_if(mid, block, block, sems.at[far_z], at_z(second_z))

    def gathered(at, cols, sems):
        for h in (flip(1), flip(2)):
            pl.when(h != z)(lambda: got(gall.at[h, at, cols], sems.at[h]))
        outer = jnp.where(end, 3 - z, second_z)
        got(gall.at[outer, at, cols], sems.at[outer])

    every, q_cols, kv_cols = pl.ds(0, 4 * HD), pl.ds(2 * HD, HD), pl.ds(0, 2 * HD)
    for n, t in enumerate((2, 1, 3, 0)):
        mail.send(dkv.at[:, turn(y, t), 1 - j], core_in.at[n], core_sems.at[n], partner)
    spread(dq, every, q_cols, q_sems)
    gall[z, :, q_cols] = dq[...]

    def chip_sum(n, t, run):
        return dkv[run, turn(y, t), j].astype(F32) + core_in[n, run].astype(F32)

    def far(h):
        for side, dev in ((0, right), (1, left)):
            far_out[h, side] = chip_sum(0, 2, 2 * h + side).astype(BF16)
            mail.send(far_out.at[h, side], far_in.at[h, side], far_sems.at[h, side], dev)

    def near(h, term):
        for side, (t, dev) in enumerate(((1, right), (3, left))):
            lane = side if term else 1 - side
            total = chip_sum(1 + side, t, 2 * h + lane)
            if term:
                got(far_in.at[h, side], far_sems.at[h, side])
                total += far_in[h, side].astype(F32)
            near_out[h, side, lane] = total.astype(BF16)
            mail.send(
                near_out.at[h, side, lane], near_in.at[h, side, lane],
                near_sems.at[h, side, lane], dev,
            )

    def finish_kv(h):
        for lane in (0, 1):
            for side in (1 - lane, lane):
                got(near_in.at[h, side, lane], near_sems.at[h, side, lane])
        for lane in (0, 1):
            run = 2 * h + lane
            total = chip_sum(3, 0, run)
            for side in (0, 1):
                total += near_in[h, side, lane].astype(F32)
            gall[z, pl.ds(HD * run, HD), kv_cols] = total.astype(BF16)
        at = pl.ds(2 * HD * h, 2 * HD)
        spread(gall.at[z, at, kv_cols], at, kv_cols, g_sems.at[h])

    got(core_in.at[0], core_sems.at[0])
    far(0)
    got(core_in.at[1], core_sems.at[1])
    got(core_in.at[2], core_sems.at[2])
    near(0, False)
    far(1)
    got(core_in.at[3], core_sems.at[3])
    near(0, True)
    near(1, False)
    forward(every, q_cols, q_sems)
    finish_kv(0)
    near(1, True)
    finish_kv(1)

    def part(t, h):
        cols = rows(d * block_of(z, turn(x, t)), d)
        at = pl.ds(2 * HD * h, 2 * HD)
        total = jnp.zeros((d, 2 * HD), F32)
        for head in range(4):
            total += lax.dot_general(
                wall[head, cols], gall[head, at], (((1,), (1,)), ((), ())),
                preferred_element_type=F32,
            )
        return total

    def x_first(h):
        total = part(2, h).astype(BF16)
        for side, dev in ((0, x_right), (1, x_left)):
            xf_out[h, side] = total[:, HD * side : HD * (side + 1)]
            mail.send(xf_out.at[h, side], xf_in.at[h, side], xf_sems.at[h, side], dev)
        for side, (t, dev) in enumerate(((1, x_right), (3, x_left))):
            total = part(t, h)
            alone = 1 - side
            xn_out[h, side, alone] = total[:, HD * alone : HD * (alone + 1)].astype(BF16)
            own_x[h, side] = total[:, HD * side : HD * (side + 1)]
            mail.send(
                xn_out.at[h, side, alone], xn_in.at[h, side, alone],
                xn_sems.at[h, side, alone], dev,
            )

    def x_second(h):
        for side, dev in ((0, x_right), (1, x_left)):
            got(xf_in.at[h, side], xf_sems.at[h, side])
            xn_out[h, side, side] = (
                own_x[h, side] + xf_in[h, side].astype(F32)
            ).astype(BF16)
            mail.send(
                xn_out.at[h, side, side], xn_in.at[h, side, side], xn_sems.at[h, side, side], dev
            )
        total = part(0, h)
        for lane in (0, 1):
            own_x[h, lane] = total[:, HD * lane : HD * (lane + 1)]

    fd = 4 * z + block_of(z, x)

    def x_third(h):
        for lane in (0, 1):
            total = own_x[h, lane]
            for side in (1 - lane, lane):
                got(xn_in.at[h, side, lane], xn_sems.at[h, side, lane])
                total += xn_in[h, side, lane].astype(F32)
            run = 2 * h + lane
            fin[run] = total.astype(BF16)
            mail.send_or_keep(
                jnp.logical_or(run != z, fd != f), fin.at[run], fin_in.at[zh, j],
                f_sems.at[zh, j], (run * 4 + y, fd),
            )

    load.wait()
    gathered(every, q_cols, q_sems)
    halves = [pl.ds(2 * HD * h, 2 * HD) for h in (0, 1)]
    forward(halves[0], kv_cols, g_sems.at[0])
    gathered(halves[0], kv_cols, g_sems.at[0])
    x_first(0)
    forward(halves[1], kv_cols, g_sems.at[1])
    x_second(0)
    gathered(halves[1], kv_cols, g_sems.at[1])
    x_first(1)
    x_third(0)
    x_second(1)
    x_third(1)
    for h in (0, 1):
        for k in (0, 1):
            got(fin_in.at[h, k], f_sems.at[h, k])
    for k in (0, 1):
        out[pl.ds(HD * k, HD)] = (
            (fin_in[0, k].astype(F32) + fin_in[1, k].astype(F32)).T
        ).astype(BF16)
    mail.flush()


def input_gradient(dkv, dq, w_all):
    quarter = w_all.shape[1]
    d = quarter // 4
    any_space = pl.BlockSpec(memory_space=pl.ANY)
    vmem = pl.BlockSpec(memory_space=pltpu.VMEM)
    dma = pltpu.SemaphoreType.DMA
    run = (HD, 2 * HD)
    block = (d, HD)
    return pl.pallas_call(
        gradient_kernel,
        name="input_gradient",
        out_shape=jax.ShapeDtypeStruct((2 * HD, d), BF16),
        in_specs=[vmem, vmem, any_space],
        out_specs=vmem,
        scratch_shapes=[
            pltpu.VMEM(w_all.shape, BF16),
            pltpu.VMEM((4, 4 * HD, 3 * HD), BF16),
            pltpu.VMEM((4, 4) + run, BF16),
            pltpu.VMEM((2, 2) + run, BF16),
            pltpu.VMEM((2, 2, 2) + run, BF16),
            pltpu.VMEM((2, 2) + run, BF16),
            pltpu.VMEM((2, 2, 2) + run, BF16),
            pltpu.VMEM((2, 2) + run, F32),
            pltpu.VMEM((2, 2) + block, BF16),
            pltpu.VMEM((2, 2, 2) + block, BF16),
            pltpu.VMEM((2, 2) + block, BF16),
            pltpu.VMEM((2, 2, 2) + block, BF16),
            pltpu.VMEM((2, 2) + block, F32),
            pltpu.VMEM((4,) + block, BF16),
            pltpu.VMEM((2, 2) + block, BF16),
            dma((48,)), dma, dma((4,)), dma((2, 2)), dma((2, 2, 2)), dma((4,)), dma((2, 4)),
            dma((2, 2)), dma((2, 2, 2)), dma((2, 2)),
        ],
        compiler_params=pltpu.CompilerParams(
            collective_id=1, has_side_effects=True, vmem_limit_bytes=VMEM_BYTES
        ),
    )(dkv, dq, w_all)


def shards(inputs, w_qkv, selected, d_attn):
    w3 = w_qkv.transpose(1, 0, 2)
    q, kv, do, w_all = project_and_gather(inputs, w3, d_attn)
    dq, dkv = attend(
        selected.T, q, kv.reshape(8, BLOCK, 2 * HD), do
    )
    return input_gradient(dkv.reshape(4, 4, 2, HD, 2 * HD), dq.reshape(4 * HD, HD), w_all)


def solution(mesh):
    placed = (P("ctx", None), P("ctx", None, "fsdp"), P(), P("ctx", "fsdp"))
    return jax.shard_map(
        shards, mesh=mesh, in_specs=placed, out_specs=P("ctx", "fsdp"), check_vma=False
    )
```

```python
import functools

import jax
import jax.numpy as jnp
from jax import lax
from jax.experimental import pallas as pl
from jax.experimental.pallas import tpu as pltpu
from jax.sharding import PartitionSpec as P

MESH = pl.DeviceIdType.MESH
F32 = jnp.float32
BF16 = jnp.bfloat16
HD = 128
BLOCK = 512
TOP = 4
SCALE = HD ** (-0.5)
VMEM_BYTES = 60 * 1024 * 1024


def place():
    c = lax.axis_index("ctx")
    f = lax.axis_index("fsdp")
    return (
        lax.div(c, 4), lax.rem(c, 4),
        lax.div(f, 8), lax.rem(lax.div(f, 2), 4), lax.rem(f, 2),
    )


def device(z, y, zh, x, k):
    return (z * 4 + y, zh * 8 + x * 2 + k)


def around(z, y, zh, x, k, by):
    at = lax.rem(4 * zh + z + 8 + by, 8)
    return device(lax.rem(at, 4), y, lax.div(at, 4), x, k)


def turn(i, by):
    return lax.rem(i + by, 4)


def rows(start, size):
    return pl.ds(pl.multiple_of(start, size & -size), size)


class Mail:
    def __init__(self, send_sems):
        self.send_sems = send_sems
        self.used = 0
        self.sent = []

    def copy(self, src, dst, recv, dev):
        sem = self.send_sems.at[self.used]
        self.used += 1
        return pltpu.make_async_remote_copy(
            src_ref=src, dst_ref=dst, send_sem=sem, recv_sem=recv,
            device_id=dev, device_id_type=MESH,
        )

    def send(self, src, dst, recv, dev):
        copy = self.copy(src, dst, recv, dev)
        copy.start()
        self.sent.append((copy, None, None))

    def send_or_keep(self, away, src, dst, recv, dev):
        copy = self.copy(src, dst, recv, dev)
        stay = pltpu.make_async_copy(src, dst, recv)

        @pl.when(away)
        def _():
            copy.start()

        @pl.when(jnp.logical_not(away))
        def _():
            stay.start()

        self.sent.append((copy, away, None))

    def send_if(self, away, src, dst, recv, dev):
        copy = self.copy(src, dst, recv, dev)

        @pl.when(away)
        def _():
            copy.start()

        self.sent.append((copy, away, None))

    def flush(self):
        for copy, away, _ in self.sent:
            if away is None:
                copy.wait_send()
            else:
                pl.when(away)(copy.wait_send)


def got(dst, recv):
    pltpu.make_async_copy(dst, dst, recv).wait()


class Ring:
    def __init__(self, mail, view, pos, core, right, left, partner, ring, cores):
        self.mail, self.view, self.pos, self.core = mail, view, pos, core
        self.right, self.left, self.partner = right, left, partner
        self.ring, self.cores = ring, cores

    def pass_on(self, pos, half, recv, dev):
        ref = self.view(self.core, pos, half)
        self.mail.send(ref, ref, recv, dev)

    def across(self, pos, half, n):
        if self.partner is not None:
            self.pass_on(pos, half, self.cores.at[n], self.partner)

    def start(self):
        self.pass_on(self.pos, None, self.ring.at[0], self.right)
        self.pass_on(self.pos, None, self.ring.at[1], self.left)
        self.across(self.pos, None, 0)

    def relay(self):
        before, after = turn(self.pos, 3), turn(self.pos, 1)
        got(self.view(self.core, before, None), self.ring.at[0])
        self.pass_on(before, 0, self.ring.at[2], self.right)
        self.across(before, None, 1)
        got(self.view(self.core, after, None), self.ring.at[1])
        self.pass_on(after, 1, self.ring.at[3], self.left)
        self.across(after, None, 2)

    def finish(self):
        far = turn(self.pos, 2)
        for half in (0, 1):
            got(self.view(self.core, far, half), self.ring.at[2 + half])
            self.across(far, half, 3 + half)

    def settle(self):
        other = 1 - self.core
        before, after, far = turn(self.pos, 3), turn(self.pos, 1), turn(self.pos, 2)
        got(self.view(other, self.pos, None), self.cores.at[0])
        got(self.view(other, before, None), self.cores.at[1])
        got(self.view(other, after, None), self.cores.at[2])
        got(self.view(other, far, 0), self.cores.at[3])
        got(self.view(other, far, 1), self.cores.at[4])


def enter(devices, more=0):
    barrier = pltpu.get_barrier_semaphore()
    for dev in devices:
        pl.semaphore_signal(barrier, inc=1, device_id=dev, device_id_type=MESH)
    return barrier, len(devices) + more


def project_kernel(
    inp, w3, d_attn, q_out, kv_out, do_out, w_out,
    wall, xall, dall, part, parts_in, via_in, own, kvall,
    send_sems, load_sems, w_ring, w_cores, x_z, x_x, d_sems, p_sems, via_sems,
    kv_ring, kv_cores, out_sems,
):
    z, y, zh, x, j = place()
    partner = device(z, y, zh, x, 1 - j)
    right = device(z, turn(y, 1), zh, x, j)
    left = device(z, turn(y, 3), zh, x, j)
    dq = wall.shape[1]
    d = dq // 4
    up = z >= 2
    end = jnp.logical_or(z == 0, z == 3)
    mid = jnp.logical_not(end)
    flip = lambda h: jnp.where(up, h, 3 - h)
    heads = tuple(flip(jnp.where(end, p, (p + 3) % 4)) for p in range(4))
    inside = device(jnp.where(up, 2, 1), y, zh, x, j)
    kinds = [pl.ds(HD * i, HD) for i in range(3)]

    loads = []
    for i, p in enumerate((1, 2, 0)):
        for s in (0, 1):
            loads.append(pltpu.make_async_copy(
                w3.at[p, :, pl.ds(HD * s, HD)],
                wall.at[2 * j + s, rows(d * y, d), kinds[i]],
                load_sems.at[2 * i + s],
            ))
    own_x = pltpu.make_async_copy(
        inp.at[rows(HD * j, HD), rows(dq * z, dq)], xall.at[rows(HD * z, HD)], load_sems.at[6]
    )
    for copy in loads:
        copy.start()
    own_x.start()

    peers = [device(turn(z, t), y, zh, x, k) for t in (1, 2, 3) for k in (j, 1 - j)]
    peers += [partner, right, left]
    peers += [device(z, y, zh, turn(x, u), j) for u in (1, 3)]
    peers += [around(z, y, zh, x, j, by) for by in (1, -1, 2, -2)]
    barrier, expected = enter(peers)
    pl.semaphore_wait(barrier, expected)

    mail = Mail(send_sems)

    def w_view(i):
        def view(core, pos, half):
            if half is None:
                return wall.at[pl.ds(2 * core, 2), rows(d * pos, d), kinds[i]]
            return wall.at[
                pl.ds(2 * core, 2), rows(d * pos + (d // 2) * half, d // 2), kinds[i]
            ]
        return view

    w_rings = [
        Ring(mail, w_view(i), y, j, right, left, partner, w_ring.at[i], w_cores.at[i])
        for i in range(3)
    ]
    piece = HD // 4

    def quarter(run, of_x, low=0, size=piece):
        return xall.at[rows(HD * run + piece * of_x + low, size)]

    hops = ((1, 0, piece), (-1, 0, piece), (2, 0, piece // 2), (-2, piece // 2, piece // 2))
    opposite = turn(x, 2)

    def x_send(turn_of):
        of_x = (x, opposite)[turn_of]
        for n, (by, low, size) in enumerate(hops):
            mail.send(
                inp.at[rows(HD * j + piece * of_x + low, size), rows(dq * turn(z, 4 + by), dq)],
                quarter(z, of_x, low, size), x_z.at[turn_of, n], around(z, y, zh, x, j, by),
            )

    def x_got(turn_of, n):
        by, low, size = hops[n]
        got(quarter(turn(z, 4 - by), (x, opposite)[turn_of], low, size), x_z.at[turn_of, n])

    def x_share(by):
        mine = quarter(turn(z, 4 - by), x)
        for u in (1, 3):
            mail.send(
                mine, mine, x_x.at[by % 4, u // 2], device(z, y, zh, turn(x, u), j)
            )

    def x_shared(by):
        for u in (1, 3):
            got(quarter(turn(z, 4 - by), turn(x, 4 - u)), x_x.at[by % 4, u // 2])

    def project(i):
        cols = kinds[i]
        for p in range(4):
            head = heads[p]
            if p % 2 == 0:
                both = jnp.dot(
                    xall[...],
                    jnp.concatenate([wall[head, :, cols], wall[heads[p + 1], :, cols]], axis=1),
                    preferred_element_type=F32,
                )
            total = both[:, HD * (p % 2) : HD * (p % 2 + 1)]
            if p == 3:
                own[:, cols] = total
                continue
            mine = part.at[p, :, cols]
            there = parts_in.at[z, :, cols]

            def store():
                part[p, :, cols] = total.astype(BF16)

            def store_both():
                got(via_in.at[p - 1, :, cols], via_sems.at[p - 1, i])
                part[p, :, cols] = (total + via_in[p - 1, :, cols].astype(F32)).astype(BF16)

            if p == 0:
                store()
            else:
                pl.when(end)(store)
                pl.when(mid)(store_both)
            if p < 2:
                mail.send_if(end, mine, via_in.at[p, :, cols], via_sems.at[p, i], inside)
                mail.send_if(mid, mine, there, p_sems.at[z, i], device(head, y, zh, x, j))
            else:
                mail.send(mine, there, p_sems.at[z, i], device(head, y, zh, x, j))

    for copy in loads[:2]:
        copy.wait()
    w_rings[0].start()
    x_send(0)
    x_send(1)
    for copy in loads[2:]:
        copy.wait()
    for n, by in ((0, 1), (1, -1)):
        x_got(0, n)
        x_share(by)
    w_rings[0].relay()
    w_rings[1].start()
    x_got(0, 2)
    x_got(0, 3)
    x_share(2)
    own_x.wait()
    w_rings[0].finish()
    w_rings[0].settle()
    for by in (1, -1, 2):
        x_shared(by)
    for n in range(4):
        x_got(1, n)
    w_rings[1].relay()
    w_rings[2].start()
    project(0)
    w_rings[1].finish()
    w_rings[1].settle()
    project(1)
    w_rings[2].relay()

    one = jnp.where(z == 1, 2, 1)
    two = jnp.where(end, 2, jnp.where(up, 3, 0))

    def collect(i):
        cols = kinds[i]
        total = own[:, cols]
        for source in (one, two):
            got(parts_in.at[source, :, cols], p_sems.at[source, i])
            total += parts_in[source, :, cols].astype(F32)
        low = total.astype(BF16)
        for run in range(4):
            if i == 2:
                q_out[run] = low[HD * run : HD * (run + 1)]
            else:
                kvall[run, y, j, :, cols] = low[HD * run : HD * (run + 1)]

    def kv_view(i):
        def view(core, pos, half):
            if half is None:
                return kvall.at[:, pos, core, :, kinds[i]]
            return kvall.at[pl.ds(2 * half, 2), pos, core, :, kinds[i]]
        return view

    kv = [
        Ring(mail, kv_view(i), y, j, right, left, partner, kv_ring.at[i], kv_cores.at[i])
        for i in (0, 1)
    ]
    collect(0)
    kv[0].start()
    w_rings[2].finish()
    w_rings[2].settle()
    keep_w = pltpu.make_async_copy(wall, w_out, out_sems.at[0])
    keep_w.start()
    project(2)
    for s in (0, 1):
        for k in (0, 1):
            zd = 2 * j + s
            away = jnp.logical_or(zd != z, j != k)
            mail.send_or_keep(
                away,
                d_attn.at[pl.ds(HD * k, HD), pl.ds(HD * s, HD)],
                dall.at[z], d_sems.at[z], device(zd, y, zh, x, k),
            )

    kv[0].relay()
    collect(1)
    kv[1].start()
    kv[0].finish()
    kv[1].relay()
    for zs in range(4):
        got(dall.at[zs], d_sems.at[zs])
    do_out[...] = dall[...]
    collect(2)
    kv[1].finish()
    for i in (0, 1):
        kv[i].settle()
    keep_kv = pltpu.make_async_copy(kvall, kv_out, out_sems.at[1])
    keep_kv.start()
    mail.flush()
    keep_w.wait()
    keep_kv.wait()


def project_and_gather(inputs, w3, d_attn):
    rows_here, width = inputs.shape
    quarter = width // 4
    any_space = pl.BlockSpec(memory_space=pl.ANY)
    vmem = pl.BlockSpec(memory_space=pltpu.VMEM)
    dma = pltpu.SemaphoreType.DMA
    return pl.pallas_call(
        project_kernel,
        name="project_and_gather",
        out_shape=(
            jax.ShapeDtypeStruct((4, HD, HD), BF16),
            jax.ShapeDtypeStruct((4, 4, 2, HD, 2 * HD), BF16),
            jax.ShapeDtypeStruct((4, HD, HD), BF16),
            jax.ShapeDtypeStruct((4, quarter, 3 * HD), BF16),
        ),
        in_specs=[any_space] * 3,
        out_specs=(vmem, any_space, vmem, any_space),
        scratch_shapes=[
            pltpu.VMEM((4, quarter, 3 * HD), BF16),
            pltpu.VMEM((4 * HD, quarter), BF16),
            pltpu.VMEM((4, HD, HD), BF16),
            pltpu.VMEM((4, 4 * HD, 3 * HD), BF16),
            pltpu.VMEM((4, 4 * HD, 3 * HD), BF16),
            pltpu.VMEM((2, 4 * HD, 3 * HD), BF16),
            pltpu.VMEM((4 * HD, 3 * HD), F32),
            pltpu.VMEM((4, 4, 2, HD, 2 * HD), BF16),
            dma((80,)), dma((7,)), dma((3, 4)), dma((3, 5)), dma((2, 4)), dma((4, 2)),
            dma((4,)), dma((4, 3)), dma((2, 3)), dma((2, 4)), dma((2, 5)), dma((2,)),
        ],
        compiler_params=pltpu.CompilerParams(
            collective_id=0, has_side_effects=True, vmem_limit_bytes=VMEM_BYTES
        ),
    )(inputs, w3, d_attn)


def attend_kernel(selected, q_ref, kv_ref, do_ref, dq_ref, dkv_ref, score, soft, total):
    _, y, _, _, j = place()
    total[...] = jnp.zeros_like(total)
    contract = lambda a, b: (((a,), (b,)), ((), ()))
    dot = functools.partial(lax.dot_general, preferred_element_type=F32)
    key_at = lax.broadcasted_iota(jnp.int32, (BLOCK, HD), 0)
    query_at = lax.broadcasted_iota(jnp.int32, (BLOCK, HD), 1)

    def tile(run, carry):
        first = (run * 4 + y) * 256 + HD * j
        block = lax.div(first, BLOCK)
        q = q_ref[run]
        do = do_ref[run]
        highest = jnp.full((1, HD), -jnp.inf, F32)
        for t in range(TOP):
            chosen = selected[t, block]
            kb = jnp.maximum(chosen, 0)
            s = dot(kv_ref[kb, :, :HD], q, contract(1, 1)) * SCALE
            limit = jnp.where(chosen >= 0, first - kb * BLOCK, -2 * BLOCK)
            s = jnp.where(key_at - query_at <= limit, s, -jnp.inf)
            score[t] = s
            highest = jnp.maximum(highest, jnp.max(s, axis=0, keepdims=True))
        totals = jnp.zeros((1, HD), F32)
        for t in range(TOP):
            e = jnp.exp(score[t] - highest)
            score[t] = e
            totals += jnp.sum(e, axis=0, keepdims=True)
        share = 1.0 / totals
        attended = jnp.zeros((HD, HD), F32)
        for t in range(TOP):
            kb = jnp.maximum(selected[t, block], 0)
            p = score[t] * share
            low = p.astype(BF16)
            score[t] = p
            soft[t] = low
            attended += dot(kv_ref[kb, :, HD:], low, contract(0, 0))
        attended = attended.astype(BF16).astype(F32)
        delta = jnp.sum(do.astype(F32).T * attended, axis=0, keepdims=True)
        dq = jnp.zeros((HD, HD), F32)
        for t in range(TOP):
            kb = jnp.maximum(selected[t, block], 0)
            dp = dot(kv_ref[kb, :, HD:], do, contract(1, 1))
            ds = (score[t] * (dp - delta)).astype(BF16)
            total[kb, :, :HD] += dot(ds, q, contract(1, 0))
            total[kb, :, HD:] += dot(soft[t], do, contract(1, 0))
            dq += dot(ds, kv_ref[kb, :, :HD], contract(0, 0))
        dq_ref[run] = (dq * SCALE).astype(BF16)
        return carry

    lax.fori_loop(0, 4, tile, 0)
    for b in range(8):
        dkv_ref[b, :, :HD] = (total[b, :, :HD] * SCALE).astype(BF16)
        dkv_ref[b, :, HD:] = total[b, :, HD:].astype(BF16)


def attend(selected, q, kv, do):
    vmem = pl.BlockSpec(memory_space=pltpu.VMEM)
    return pl.pallas_call(
        attend_kernel,
        name="attend",
        out_shape=(
            jax.ShapeDtypeStruct((4, HD, HD), BF16),
            jax.ShapeDtypeStruct((8, BLOCK, 2 * HD), BF16),
        ),
        in_specs=[pl.BlockSpec(memory_space=pltpu.SMEM), vmem, vmem, vmem],
        out_specs=(vmem, vmem),
        scratch_shapes=[
            pltpu.VMEM((TOP, BLOCK, HD), F32),
            pltpu.VMEM((TOP, BLOCK, HD), BF16),
            pltpu.VMEM((8, BLOCK, 2 * HD), F32),
        ],
        compiler_params=pltpu.CompilerParams(vmem_limit_bytes=VMEM_BYTES),
    )(selected, q, kv, do)


def owner_x(z, jj):
    at = jnp.where(lax.rem(jj, 2) == 0, lax.div(jj, 2), lax.div(7 - jj, 2))
    return turn(at, 2 * lax.rem(z, 2))


def block_of(z, x):
    at = turn(x, 2 * lax.rem(z, 2))
    return jnp.where(at < 2, 2 * at, 7 - 2 * at)


def gradient_kernel(
    dkv, dq, w_in, out,
    wall, gall, core_in, far_out, near_out, far_in, near_in, own_kv,
    xf_out, xn_out, xf_in, xn_in, own_x, fin, fin_in,
    send_sems, load_sem, core_sems, far_sems, near_sems, q_sems, g_sems, xf_sems, xn_sems, f_sems,
):
    z, y, zh, x, j = place()
    d = wall.shape[1] // 4
    f = lax.axis_index("fsdp")
    partner = device(z, y, zh, x, 1 - j)
    right = device(z, turn(y, 1), zh, x, j)
    left = device(z, turn(y, 3), zh, x, j)
    x_right = device(z, y, zh, turn(x, 1), j)
    x_left = device(z, y, zh, turn(x, 3), j)
    up = z >= 2
    end = jnp.logical_or(z == 0, z == 3)
    mid = jnp.logical_not(end)
    flip = lambda h: jnp.where(up, h, 3 - h)
    at_z = lambda h: device(h, y, zh, x, j)
    first_z = flip(jnp.where(end, 2, 1))
    second_z = flip(jnp.where(end, 1, 3))
    far_z = flip(0)

    load = pltpu.make_async_copy(w_in, wall, load_sem)
    load.start()

    across = [at_z(turn(z, t)) for t in (1, 2, 3)]
    barrier, expected = enter([partner, right, left, x_right, x_left] + across, more=4)
    source_z = lax.div(f, 4)
    source_x = owner_x(source_z, lax.rem(f, 4))
    for h in (0, 1):
        for k in (0, 1):
            pl.semaphore_signal(
                barrier, inc=1, device_id=device(source_z, y, h, source_x, k),
                device_id_type=MESH,
            )
    pl.semaphore_wait(barrier, expected)

    mail = Mail(send_sems)

    def spread(src, at, cols, sems):
        there = gall.at[z, at, cols]
        mail.send(src, there, sems.at[z], at_z(first_z))
        mail.send(src, there, sems.at[z], at_z(second_z))

    def forward(at, cols, sems):
        for h in (first_z, far_z):
            block = gall.at[h, at, cols]
            pl.when(mid)(lambda: got(block, sems.at[h]))
            mail.send_if(mid, block, block, sems.at[h], at_z(second_z))

    def gathered(at, cols, sems):
        def wait(h):
            got(gall.at[h, at, cols], sems.at[h])

        wait(second_z)

        @pl.when(end)
        def _():
            wait(first_z)
            wait(3 - z)

    every, q_cols, kv_cols = pl.ds(0, 4 * HD), pl.ds(2 * HD, HD), pl.ds(0, 2 * HD)
    for n, t in enumerate((2, 1, 3, 0)):
        mail.send(dkv.at[:, turn(y, t), 1 - j], core_in.at[n], core_sems.at[n], partner)
    spread(dq, every, q_cols, q_sems)
    gall[z, :, q_cols] = dq[...]

    def chip_sum(n, t, run):
        return dkv[run, turn(y, t), j].astype(F32) + core_in[n, run].astype(F32)

    def far(h):
        for side, dev in ((0, right), (1, left)):
            far_out[h, side] = chip_sum(0, 2, 2 * h + side).astype(BF16)
            mail.send(far_out.at[h, side], far_in.at[h, side], far_sems.at[h, side], dev)

    def near(h, term):
        for side, (t, dev) in enumerate(((1, right), (3, left))):
            lane = side if term else 1 - side
            total = chip_sum(1 + side, t, 2 * h + lane)
            if term:
                got(far_in.at[h, side], far_sems.at[h, side])
                total += far_in[h, side].astype(F32)
            near_out[h, side, lane] = total.astype(BF16)
            mail.send(
                near_out.at[h, side, lane], near_in.at[h, side, lane],
                near_sems.at[h, side, lane], dev,
            )

    def finish_kv(h):
        for lane in (0, 1):
            for side in (1 - lane, lane):
                got(near_in.at[h, side, lane], near_sems.at[h, side, lane])
        for lane in (0, 1):
            run = 2 * h + lane
            total = chip_sum(3, 0, run)
            for side in (0, 1):
                total += near_in[h, side, lane].astype(F32)
            gall[z, pl.ds(HD * run, HD), kv_cols] = total.astype(BF16)
        at = pl.ds(2 * HD * h, 2 * HD)
        spread(gall.at[z, at, kv_cols], at, kv_cols, g_sems.at[h])

    got(core_in.at[0], core_sems.at[0])
    far(0)
    got(core_in.at[1], core_sems.at[1])
    got(core_in.at[2], core_sems.at[2])
    near(0, False)
    far(1)
    got(core_in.at[3], core_sems.at[3])
    near(0, True)
    near(1, False)
    forward(every, q_cols, q_sems)
    finish_kv(0)
    near(1, True)
    finish_kv(1)

    def part(t, h):
        cols = rows(d * block_of(z, turn(x, t)), d)
        at = pl.ds(2 * HD * h, 2 * HD)
        total = jnp.zeros((d, 2 * HD), F32)
        for head in range(4):
            total += lax.dot_general(
                wall[head, cols], gall[head, at], (((1,), (1,)), ((), ())),
                preferred_element_type=F32,
            )
        return total

    def x_first(h):
        total = part(2, h).astype(BF16)
        for side, dev in ((0, x_right), (1, x_left)):
            xf_out[h, side] = total[:, HD * side : HD * (side + 1)]
            mail.send(xf_out.at[h, side], xf_in.at[h, side], xf_sems.at[h, side], dev)
        for side, (t, dev) in enumerate(((1, x_right), (3, x_left))):
            total = part(t, h)
            alone = 1 - side
            xn_out[h, side, alone] = total[:, HD * alone : HD * (alone + 1)].astype(BF16)
            own_x[h, side] = total[:, HD * side : HD * (side + 1)]
            mail.send(
                xn_out.at[h, side, alone], xn_in.at[h, side, alone],
                xn_sems.at[h, side, alone], dev,
            )

    def x_second(h):
        for side, dev in ((0, x_right), (1, x_left)):
            got(xf_in.at[h, side], xf_sems.at[h, side])
            xn_out[h, side, side] = (
                own_x[h, side] + xf_in[h, side].astype(F32)
            ).astype(BF16)
            mail.send(
                xn_out.at[h, side, side], xn_in.at[h, side, side], xn_sems.at[h, side, side], dev
            )
        total = part(0, h)
        for lane in (0, 1):
            own_x[h, lane] = total[:, HD * lane : HD * (lane + 1)]

    fd = 4 * z + block_of(z, x)

    def x_third(h):
        for lane in (0, 1):
            total = own_x[h, lane]
            for side in (1 - lane, lane):
                got(xn_in.at[h, side, lane], xn_sems.at[h, side, lane])
                total += xn_in[h, side, lane].astype(F32)
            run = 2 * h + lane
            fin[run] = total.astype(BF16)
            mail.send_or_keep(
                jnp.logical_or(run != z, fd != f), fin.at[run], fin_in.at[zh, j],
                f_sems.at[zh, j], (run * 4 + y, fd),
            )

    load.wait()
    gathered(every, q_cols, q_sems)
    halves = [pl.ds(2 * HD * h, 2 * HD) for h in (0, 1)]
    forward(halves[0], kv_cols, g_sems.at[0])
    gathered(halves[0], kv_cols, g_sems.at[0])
    x_first(0)
    forward(halves[1], kv_cols, g_sems.at[1])
    x_second(0)
    gathered(halves[1], kv_cols, g_sems.at[1])
    x_first(1)
    x_third(0)
    x_second(1)
    x_third(1)
    for h in (0, 1):
        for k in (0, 1):
            got(fin_in.at[h, k], f_sems.at[h, k])
    for k in (0, 1):
        out[pl.ds(HD * k, HD)] = (
            (fin_in[0, k].astype(F32) + fin_in[1, k].astype(F32)).T
        ).astype(BF16)
    mail.flush()


def input_gradient(dkv, dq, w_all):
    quarter = w_all.shape[1]
    d = quarter // 4
    any_space = pl.BlockSpec(memory_space=pl.ANY)
    vmem = pl.BlockSpec(memory_space=pltpu.VMEM)
    dma = pltpu.SemaphoreType.DMA
    run = (HD, 2 * HD)
    block = (d, HD)
    return pl.pallas_call(
        gradient_kernel,
        name="input_gradient",
        out_shape=jax.ShapeDtypeStruct((2 * HD, d), BF16),
        in_specs=[vmem, vmem, any_space],
        out_specs=vmem,
        scratch_shapes=[
            pltpu.VMEM(w_all.shape, BF16),
            pltpu.VMEM((4, 4 * HD, 3 * HD), BF16),
            pltpu.VMEM((4, 4) + run, BF16),
            pltpu.VMEM((2, 2) + run, BF16),
            pltpu.VMEM((2, 2, 2) + run, BF16),
            pltpu.VMEM((2, 2) + run, BF16),
            pltpu.VMEM((2, 2, 2) + run, BF16),
            pltpu.VMEM((2, 2) + run, F32),
            pltpu.VMEM((2, 2) + block, BF16),
            pltpu.VMEM((2, 2, 2) + block, BF16),
            pltpu.VMEM((2, 2) + block, BF16),
            pltpu.VMEM((2, 2, 2) + block, BF16),
            pltpu.VMEM((2, 2) + block, F32),
            pltpu.VMEM((4,) + block, BF16),
            pltpu.VMEM((2, 2) + block, BF16),
            dma((48,)), dma, dma((4,)), dma((2, 2)), dma((2, 2, 2)), dma((4,)), dma((2, 4)),
            dma((2, 2)), dma((2, 2, 2)), dma((2, 2)),
        ],
        compiler_params=pltpu.CompilerParams(
            collective_id=1, has_side_effects=True, vmem_limit_bytes=VMEM_BYTES
        ),
    )(dkv, dq, w_all)


def shards(inputs, w_qkv, selected, d_attn):
    w3 = w_qkv.transpose(1, 0, 2)
    q, kv, do, w_all = project_and_gather(inputs, w3, d_attn)
    dq, dkv = attend(
        selected.T, q, kv.reshape(8, BLOCK, 2 * HD), do
    )
    return input_gradient(dkv.reshape(4, 4, 2, HD, 2 * HD), dq.reshape(4 * HD, HD), w_all)


def solution(mesh):
    placed = (P("ctx", None), P("ctx", None, "fsdp"), P(), P("ctx", "fsdp"))
    return jax.shard_map(
        shards, mesh=mesh, in_specs=placed, out_specs=P("ctx", "fsdp"), check_vma=False
    )
```

```python
import functools

import jax
import jax.numpy as jnp
from jax import lax
from jax.experimental import pallas as pl
from jax.experimental.pallas import tpu as pltpu
from jax.sharding import PartitionSpec as P

MESH = pl.DeviceIdType.MESH
F32 = jnp.float32
BF16 = jnp.bfloat16
HD = 128
BLOCK = 512
TOP = 4
SCALE = HD ** (-0.5)
AHEAD = 2
VMEM_BYTES = 60 * 1024 * 1024


def place():
    c = lax.axis_index("ctx")
    f = lax.axis_index("fsdp")
    return (
        lax.div(c, 4), lax.rem(c, 4),
        lax.div(f, 8), lax.rem(lax.div(f, 2), 4), lax.rem(f, 2),
    )


def device(z, y, zh, x, k):
    return (z * 4 + y, zh * 8 + x * 2 + k)


def around(z, y, zh, x, k, by):
    at = lax.rem(4 * zh + z + 8 + by, 8)
    return device(lax.rem(at, 4), y, lax.div(at, 4), x, k)


def turn(i, by):
    return lax.rem(i + by, 4)


def rows(start, size):
    return pl.ds(pl.multiple_of(start, size & -size), size)


class Mail:
    def __init__(self, send_sems):
        self.send_sems = send_sems
        self.used = 0
        self.sent = []

    def copy(self, src, dst, recv, dev):
        sem = self.send_sems.at[self.used]
        self.used += 1
        return pltpu.make_async_remote_copy(
            src_ref=src, dst_ref=dst, send_sem=sem, recv_sem=recv,
            device_id=dev, device_id_type=MESH,
        )

    def send(self, src, dst, recv, dev):
        copy = self.copy(src, dst, recv, dev)
        copy.start()
        self.sent.append((copy, None, None))

    def send_or_keep(self, away, src, dst, recv, dev):
        copy = self.copy(src, dst, recv, dev)
        stay = pltpu.make_async_copy(src, dst, recv)

        @pl.when(away)
        def _():
            copy.start()

        @pl.when(jnp.logical_not(away))
        def _():
            stay.start()

        self.sent.append((copy, away, None))

    def send_if(self, away, src, dst, recv, dev):
        copy = self.copy(src, dst, recv, dev)

        @pl.when(away)
        def _():
            copy.start()

        self.sent.append((copy, away, None))

    def flush(self):
        for copy, away, _ in self.sent:
            if away is None:
                copy.wait_send()
            else:
                pl.when(away)(copy.wait_send)


def got(dst, recv):
    pltpu.make_async_copy(dst, dst, recv).wait()


class Ring:
    def __init__(self, mail, view, pos, core, right, left, partner, ring, cores):
        self.mail, self.view, self.pos, self.core = mail, view, pos, core
        self.right, self.left, self.partner = right, left, partner
        self.ring, self.cores = ring, cores

    def pass_on(self, pos, half, recv, dev):
        ref = self.view(self.core, pos, half)
        self.mail.send(ref, ref, recv, dev)

    def across(self, pos, half, n):
        if self.partner is not None:
            self.pass_on(pos, half, self.cores.at[n], self.partner)

    def start(self):
        self.pass_on(self.pos, None, self.ring.at[0], self.right)
        self.pass_on(self.pos, None, self.ring.at[1], self.left)
        self.across(self.pos, None, 0)

    def relay(self):
        before, after = turn(self.pos, 3), turn(self.pos, 1)
        got(self.view(self.core, before, None), self.ring.at[0])
        self.pass_on(before, 0, self.ring.at[2], self.right)
        self.across(before, None, 1)
        got(self.view(self.core, after, None), self.ring.at[1])
        self.pass_on(after, 1, self.ring.at[3], self.left)
        self.across(after, None, 2)

    def finish(self):
        far = turn(self.pos, 2)
        for half in (0, 1):
            got(self.view(self.core, far, half), self.ring.at[2 + half])
            self.across(far, half, 3 + half)

    def settle(self):
        other = 1 - self.core
        before, after, far = turn(self.pos, 3), turn(self.pos, 1), turn(self.pos, 2)
        got(self.view(other, self.pos, None), self.cores.at[0])
        got(self.view(other, before, None), self.cores.at[1])
        got(self.view(other, after, None), self.cores.at[2])
        got(self.view(other, far, 0), self.cores.at[3])
        got(self.view(other, far, 1), self.cores.at[4])


def enter(devices, more=0):
    barrier = pltpu.get_barrier_semaphore()
    for dev in devices:
        pl.semaphore_signal(barrier, inc=1, device_id=dev, device_id_type=MESH)
    return barrier, len(devices) + more


def project_kernel(
    inp, w3, d_attn, q_out, kv_out, do_out, w_out,
    wall, xall, dall, part, parts_in, via_in, own, kvall,
    send_sems, load_sems, w_ring, w_cores, x_z, x_x, d_sems, p_sems, via_sems,
    kv_ring, kv_cores, out_sems,
):
    z, y, zh, x, j = place()
    partner = device(z, y, zh, x, 1 - j)
    right = device(z, turn(y, 1), zh, x, j)
    left = device(z, turn(y, 3), zh, x, j)
    dq = wall.shape[1]
    d = dq // 4
    up = z >= 2
    end = jnp.logical_or(z == 0, z == 3)
    mid = jnp.logical_not(end)
    flip = lambda h: jnp.where(up, h, 3 - h)
    heads = tuple(flip(jnp.where(end, p, (p + 3) % 4)) for p in range(4))
    inside = device(jnp.where(up, 2, 1), y, zh, x, j)
    kinds = [pl.ds(HD * i, HD) for i in range(3)]

    loads = []
    for i, p in enumerate((1, 2, 0)):
        for s in (0, 1):
            loads.append(pltpu.make_async_copy(
                w3.at[p, :, pl.ds(HD * s, HD)],
                wall.at[2 * j + s, rows(d * y, d), kinds[i]],
                load_sems.at[2 * i + s],
            ))
    own_x = pltpu.make_async_copy(
        inp.at[rows(HD * j, HD), rows(dq * z, dq)], xall.at[rows(HD * z, HD)], load_sems.at[6]
    )
    for copy in loads:
        copy.start()
    own_x.start()

    peers = [device(turn(z, t), y, zh, x, k) for t in (1, 2, 3) for k in (j, 1 - j)]
    peers += [partner, right, left]
    peers += [device(z, y, zh, turn(x, u), j) for u in (1, 3)]
    peers += [around(z, y, zh, x, j, by) for by in (1, -1, 2, -2)]
    barrier, expected = enter(peers)
    pl.semaphore_wait(barrier, expected)

    mail = Mail(send_sems)

    def w_view(i):
        def view(core, pos, half):
            if half is None:
                return wall.at[pl.ds(2 * core, 2), rows(d * pos, d), kinds[i]]
            return wall.at[
                pl.ds(2 * core, 2), rows(d * pos + (d // 2) * half, d // 2), kinds[i]
            ]
        return view

    w_rings = [
        Ring(mail, w_view(i), y, j, right, left, partner, w_ring.at[i], w_cores.at[i])
        for i in range(3)
    ]
    piece = HD // 4

    def quarter(run, of_x, low=0, size=piece):
        return xall.at[rows(HD * run + piece * of_x + low, size)]

    hops = ((1, 0, piece), (-1, 0, piece), (2, 0, piece // 2), (-2, piece // 2, piece // 2))
    opposite = turn(x, 2)

    def x_send(turn_of):
        of_x = (x, opposite)[turn_of]
        for n, (by, low, size) in enumerate(hops):
            mail.send(
                inp.at[rows(HD * j + piece * of_x + low, size), rows(dq * turn(z, 4 + by), dq)],
                quarter(z, of_x, low, size), x_z.at[turn_of, n], around(z, y, zh, x, j, by),
            )

    def x_got(turn_of, n):
        by, low, size = hops[n]
        got(quarter(turn(z, 4 - by), (x, opposite)[turn_of], low, size), x_z.at[turn_of, n])

    def x_share(by):
        mine = quarter(turn(z, 4 - by), x)
        for u in (1, 3):
            mail.send(
                mine, mine, x_x.at[by % 4, u // 2], device(z, y, zh, turn(x, u), j)
            )

    def x_shared(by):
        for u in (1, 3):
            got(quarter(turn(z, 4 - by), turn(x, 4 - u)), x_x.at[by % 4, u // 2])

    def project(i):
        cols = kinds[i]
        for p in range(4):
            head = heads[p]
            if p % 2 == 0:
                both = jnp.dot(
                    xall[...],
                    jnp.concatenate([wall[head, :, cols], wall[heads[p + 1], :, cols]], axis=1),
                    preferred_element_type=F32,
                )
            total = both[:, HD * (p % 2) : HD * (p % 2 + 1)]
            if p == 3:
                own[:, cols] = total
                continue
            mine = part.at[p, :, cols]
            there = parts_in.at[z, :, cols]

            def store():
                part[p, :, cols] = total.astype(BF16)

            def store_both():
                got(via_in.at[p - 1, :, cols], via_sems.at[p - 1, i])
                part[p, :, cols] = (total + via_in[p - 1, :, cols].astype(F32)).astype(BF16)

            if p == 0:
                store()
            else:
                pl.when(end)(store)
                pl.when(mid)(store_both)
            if p < 2:
                mail.send_if(end, mine, via_in.at[p, :, cols], via_sems.at[p, i], inside)
                mail.send_if(mid, mine, there, p_sems.at[z, i], device(head, y, zh, x, j))
            else:
                mail.send(mine, there, p_sems.at[z, i], device(head, y, zh, x, j))

    for copy in loads[:2]:
        copy.wait()
    w_rings[0].start()
    x_send(0)
    x_send(1)
    for copy in loads[2:]:
        copy.wait()
    for n, by in ((0, 1), (1, -1)):
        x_got(0, n)
        x_share(by)
    w_rings[0].relay()
    w_rings[1].start()
    x_got(0, 2)
    x_got(0, 3)
    x_share(2)
    own_x.wait()
    w_rings[0].finish()
    w_rings[0].settle()
    for by in (1, -1, 2):
        x_shared(by)
    for n in range(4):
        x_got(1, n)
    w_rings[1].relay()
    w_rings[2].start()
    project(0)
    w_rings[1].finish()
    w_rings[1].settle()
    project(1)
    w_rings[2].relay()

    one = jnp.where(z == 1, 2, 1)
    two = jnp.where(end, 2, jnp.where(up, 3, 0))

    def collect(i):
        cols = kinds[i]
        total = own[:, cols]
        for source in (one, two):
            got(parts_in.at[source, :, cols], p_sems.at[source, i])
            total += parts_in[source, :, cols].astype(F32)
        low = total.astype(BF16)
        for run in range(4):
            if i == 2:
                q_out[run] = low[HD * run : HD * (run + 1)]
            else:
                kvall[run, y, j, :, cols] = low[HD * run : HD * (run + 1)]

    def kv_view(i):
        def view(core, pos, half):
            if half is None:
                return kvall.at[:, pos, core, :, kinds[i]]
            return kvall.at[pl.ds(2 * half, 2), pos, core, :, kinds[i]]
        return view

    kv = [
        Ring(mail, kv_view(i), y, j, right, left, partner, kv_ring.at[i], kv_cores.at[i])
        for i in (0, 1)
    ]
    collect(0)
    kv[0].start()
    w_rings[2].finish()
    w_rings[2].settle()
    keep_w = pltpu.make_async_copy(wall, w_out, out_sems.at[0])
    keep_w.start()
    project(2)
    for s in (0, 1):
        for k in (0, 1):
            zd = 2 * j + s
            away = jnp.logical_or(zd != z, j != k)
            mail.send_or_keep(
                away,
                d_attn.at[pl.ds(HD * k, HD), pl.ds(HD * s, HD)],
                dall.at[z], d_sems.at[z], device(zd, y, zh, x, k),
            )

    kv[0].relay()
    collect(1)
    kv[1].start()
    kv[0].finish()
    kv[1].relay()
    for zs in range(4):
        got(dall.at[zs], d_sems.at[zs])
    do_out[...] = dall[...]
    collect(2)
    kv[1].finish()
    for i in (0, 1):
        kv[i].settle()
    keep_kv = pltpu.make_async_copy(kvall, kv_out, out_sems.at[1])
    keep_kv.start()
    mail.flush()
    keep_w.wait()
    keep_kv.wait()


def project_and_gather(inputs, w3, d_attn):
    rows_here, width = inputs.shape
    quarter = width // 4
    any_space = pl.BlockSpec(memory_space=pl.ANY)
    vmem = pl.BlockSpec(memory_space=pltpu.VMEM)
    dma = pltpu.SemaphoreType.DMA
    return pl.pallas_call(
        project_kernel,
        name="project_and_gather",
        out_shape=(
            jax.ShapeDtypeStruct((4, HD, HD), BF16),
            jax.ShapeDtypeStruct((4, 4, 2, HD, 2 * HD), BF16),
            jax.ShapeDtypeStruct((4, HD, HD), BF16),
            jax.ShapeDtypeStruct((4, quarter, 3 * HD), BF16),
        ),
        in_specs=[any_space] * 3,
        out_specs=(vmem, any_space, vmem, any_space),
        scratch_shapes=[
            pltpu.VMEM((4, quarter, 3 * HD), BF16),
            pltpu.VMEM((4 * HD, quarter), BF16),
            pltpu.VMEM((4, HD, HD), BF16),
            pltpu.VMEM((4, 4 * HD, 3 * HD), BF16),
            pltpu.VMEM((4, 4 * HD, 3 * HD), BF16),
            pltpu.VMEM((2, 4 * HD, 3 * HD), BF16),
            pltpu.VMEM((4 * HD, 3 * HD), F32),
            pltpu.VMEM((4, 4, 2, HD, 2 * HD), BF16),
            dma((80,)), dma((7,)), dma((3, 4)), dma((3, 5)), dma((2, 4)), dma((4, 2)),
            dma((4,)), dma((4, 3)), dma((2, 3)), dma((2, 4)), dma((2, 5)), dma((2,)),
        ],
        compiler_params=pltpu.CompilerParams(
            collective_id=0, has_side_effects=True, vmem_limit_bytes=VMEM_BYTES
        ),
    )(inputs, w3, d_attn)


def attend_kernel(selected, q_ref, kv_ref, do_ref, dq_ref, dkv_ref, score, soft, total):
    _, y, _, _, j = place()
    total[...] = jnp.zeros_like(total)
    contract = lambda a, b: (((a,), (b,)), ((), ()))
    dot = functools.partial(lax.dot_general, preferred_element_type=F32)
    key_at = lax.broadcasted_iota(jnp.int32, (BLOCK, HD), 0)
    query_at = lax.broadcasted_iota(jnp.int32, (BLOCK, HD), 1)

    def tile(run, carry):
        first = (run * 4 + y) * 256 + HD * j
        block = lax.div(first, BLOCK)
        q = q_ref[run]
        do = do_ref[run]
        highest = jnp.full((1, HD), -jnp.inf, F32)
        for t in range(TOP):
            chosen = selected[t, block]
            kb = jnp.maximum(chosen, 0)
            s = dot(kv_ref[kb, :, :HD], q, contract(1, 1)) * SCALE
            limit = jnp.where(chosen >= 0, first - kb * BLOCK, -2 * BLOCK)
            s = jnp.where(key_at - query_at <= limit, s, -jnp.inf)
            score[t] = s
            highest = jnp.maximum(highest, jnp.max(s, axis=0, keepdims=True))
        totals = jnp.zeros((1, HD), F32)
        for t in range(TOP):
            e = jnp.exp(score[t] - highest)
            score[t] = e
            totals += jnp.sum(e, axis=0, keepdims=True)
        share = 1.0 / totals
        attended = jnp.zeros((HD, HD), F32)
        for t in range(TOP):
            kb = jnp.maximum(selected[t, block], 0)
            p = score[t] * share
            low = p.astype(BF16)
            score[t] = p
            soft[t] = low
            attended += dot(kv_ref[kb, :, HD:], low, contract(0, 0))
        attended = attended.astype(BF16).astype(F32)
        delta = jnp.sum(do.astype(F32).T * attended, axis=0, keepdims=True)
        dq = jnp.zeros((HD, HD), F32)
        for t in range(TOP):
            kb = jnp.maximum(selected[t, block], 0)
            dp = dot(kv_ref[kb, :, HD:], do, contract(1, 1))
            ds = (score[t] * (dp - delta)).astype(BF16)
            total[kb, :, :HD] += dot(ds, q, contract(1, 0))
            total[kb, :, HD:] += dot(soft[t], do, contract(1, 0))
            dq += dot(ds, kv_ref[kb, :, :HD], contract(0, 0))
        dq_ref[run] = (dq * SCALE).astype(BF16)
        return carry

    lax.fori_loop(0, 4, tile, 0)
    for b in range(8):
        dkv_ref[b, :, :HD] = (total[b, :, :HD] * SCALE).astype(BF16)
        dkv_ref[b, :, HD:] = total[b, :, HD:].astype(BF16)


def attend(selected, q, kv, do):
    vmem = pl.BlockSpec(memory_space=pltpu.VMEM)
    return pl.pallas_call(
        attend_kernel,
        name="attend",
        out_shape=(
            jax.ShapeDtypeStruct((4, HD, HD), BF16),
            jax.ShapeDtypeStruct((8, BLOCK, 2 * HD), BF16),
        ),
        in_specs=[pl.BlockSpec(memory_space=pltpu.SMEM), vmem, vmem, vmem],
        out_specs=(vmem, vmem),
        scratch_shapes=[
            pltpu.VMEM((TOP, BLOCK, HD), F32),
            pltpu.VMEM((TOP, BLOCK, HD), BF16),
            pltpu.VMEM((8, BLOCK, 2 * HD), F32),
        ],
        compiler_params=pltpu.CompilerParams(vmem_limit_bytes=VMEM_BYTES),
    )(selected, q, kv, do)


def owner_x(z, jj):
    at = jnp.where(lax.rem(jj, 2) == 0, lax.div(jj, 2), lax.div(7 - jj, 2))
    return turn(at, 2 * lax.rem(z, 2))


def block_of(z, x):
    at = turn(x, 2 * lax.rem(z, 2))
    return jnp.where(at < 2, 2 * at, 7 - 2 * at)


def gradient_kernel(
    dkv, dq, w_in, out,
    wall, gall, core_in, far_out, near_out, far_in, near_in,
    xf_out, xn_out, xf_in, xn_in, own_x, fin, fin_in,
    send_sems, load_sem, core_sems, far_sems, near_sems, q_sems, g_sems, xf_sems, xn_sems, f_sems,
):
    z, y, zh, x, j = place()
    d = wall.shape[1] // 4
    f = lax.axis_index("fsdp")
    partner = device(z, y, zh, x, 1 - j)
    right = device(z, turn(y, 1), zh, x, j)
    left = device(z, turn(y, 3), zh, x, j)
    x_right = device(z, y, zh, turn(x, 1), j)
    x_left = device(z, y, zh, turn(x, 3), j)
    up = z >= 2
    end = jnp.logical_or(z == 0, z == 3)
    mid = jnp.logical_not(end)
    flip = lambda h: jnp.where(up, h, 3 - h)
    at_z = lambda h: device(h, y, zh, x, j)
    first_z = flip(jnp.where(end, 2, 1))
    second_z = flip(jnp.where(end, 1, 3))
    far_z = flip(0)

    load = pltpu.make_async_copy(w_in, wall, load_sem)
    load.start()

    across = [at_z(turn(z, t)) for t in (1, 2, 3)]
    barrier, expected = enter([partner, right, left, x_right, x_left] + across, more=4)
    source_z = lax.div(f, 4)
    source_x = owner_x(source_z, lax.rem(f, 4))
    for h in (0, 1):
        for k in (0, 1):
            pl.semaphore_signal(
                barrier, inc=1, device_id=device(source_z, y, h, source_x, k),
                device_id_type=MESH,
            )
    pl.semaphore_wait(barrier, expected)

    mail = Mail(send_sems)

    def spread(src, at, cols, sems):
        there = gall.at[z, at, cols]
        mail.send(src, there, sems.at[z], at_z(first_z))
        mail.send(src, there, sems.at[z], at_z(second_z))

    def forward(at, cols, sems):
        for h in (first_z, far_z):
            block = gall.at[h, at, cols]
            pl.when(mid)(lambda: got(block, sems.at[h]))
            mail.send_if(mid, block, block, sems.at[h], at_z(second_z))

    def gathered(at, cols, sems):
        def wait(h):
            got(gall.at[h, at, cols], sems.at[h])

        wait(second_z)

        @pl.when(end)
        def _():
            wait(first_z)
            wait(3 - z)

    runs = [pl.ds(HD * r, HD) for r in range(4)]
    every, q_cols, kv_cols = pl.ds(0, 4 * HD), pl.ds(2 * HD, HD), pl.ds(0, 2 * HD)
    for n, t in enumerate((2, 1, 3, 0)):
        mail.send(dkv.at[:, turn(y, t), 1 - j], core_in.at[n], core_sems.at[n], partner)
    spread(dq, every, q_cols, q_sems)
    gall[z, :, q_cols] = dq[...]

    def chip_sum(n, t, run):
        return dkv[run, turn(y, t), j].astype(F32) + core_in[n, run].astype(F32)

    def far(h):
        for side, dev in ((0, right), (1, left)):
            far_out[h, side] = chip_sum(0, 2, 2 * h + side).astype(BF16)
            mail.send(far_out.at[h, side], far_in.at[h, side], far_sems.at[h, side], dev)

    def near(h, term):
        for side, (t, dev) in enumerate(((1, right), (3, left))):
            lane = side if term else 1 - side
            total = chip_sum(1 + side, t, 2 * h + lane)
            if term:
                got(far_in.at[h, side], far_sems.at[h, side])
                total += far_in[h, side].astype(F32)
            near_out[h, side, lane] = total.astype(BF16)
            mail.send(
                near_out.at[h, side, lane], near_in.at[h, side, lane],
                near_sems.at[h, side, lane], dev,
            )

    def spread_run(run):
        at = runs[run]
        spread(gall.at[z, at, kv_cols], at, kv_cols, g_sems.at[run])

    def finish_kv(h):
        for lane in (0, 1):
            for side in (1 - lane, lane):
                got(near_in.at[h, side, lane], near_sems.at[h, side, lane])
        for lane in (0, 1):
            run = 2 * h + lane
            total = chip_sum(3, 0, run)
            for side in (0, 1):
                total += near_in[h, side, lane].astype(F32)
            at = runs[run]
            gall[z, at, kv_cols] = total.astype(BF16)
            if run < AHEAD:
                spread_run(run)

    got(core_in.at[0], core_sems.at[0])
    far(0)
    got(core_in.at[1], core_sems.at[1])
    got(core_in.at[2], core_sems.at[2])
    near(0, False)
    far(1)
    got(core_in.at[3], core_sems.at[3])
    near(0, True)
    near(1, False)
    forward(every, q_cols, q_sems)
    finish_kv(0)
    near(1, True)
    finish_kv(1)

    def part(t, r):
        cols = rows(d * block_of(z, turn(x, t)), d)
        total = jnp.zeros((d, HD), F32)
        for head in range(4):
            total += lax.dot_general(
                wall[head, cols], gall[head, runs[r]], (((1,), (1,)), ((), ())),
                preferred_element_type=F32,
            )
        return total[: d // 2], total[d // 2 :]

    def x_first(r):
        total = part(2, r)
        for side, dev in ((0, x_right), (1, x_left)):
            xf_out[r, side] = total[side].astype(BF16)
            mail.send(xf_out.at[r, side], xf_in.at[r, side], xf_sems.at[r, side], dev)
        for side, (t, dev) in enumerate(((1, x_right), (3, x_left))):
            total = part(t, r)
            alone = 1 - side
            xn_out[r, side, alone] = total[alone].astype(BF16)
            own_x[r, side] = total[side]
            mail.send(
                xn_out.at[r, side, alone], xn_in.at[r, side, alone],
                xn_sems.at[r, side, alone], dev,
            )

    def x_second(r):
        for side, dev in ((0, x_right), (1, x_left)):
            got(xf_in.at[r, side], xf_sems.at[r, side])
            xn_out[r, side, side] = (
                own_x[r, side] + xf_in[r, side].astype(F32)
            ).astype(BF16)
            mail.send(
                xn_out.at[r, side, side], xn_in.at[r, side, side], xn_sems.at[r, side, side], dev
            )
        total = part(0, r)
        for lane in (0, 1):
            own_x[r, lane] = total[lane]

    fd = 4 * z + block_of(z, x)

    def x_third(r):
        for lane in (0, 1):
            total = own_x[r, lane]
            for side in (1 - lane, lane):
                got(xn_in.at[r, side, lane], xn_sems.at[r, side, lane])
                total += xn_in[r, side, lane].astype(F32)
            fin[r, pl.ds((d // 2) * lane, d // 2)] = total.astype(BF16)
        mail.send_or_keep(
            jnp.logical_or(r != z, fd != f), fin.at[r], fin_in.at[zh, j],
            f_sems.at[zh, j], (r * 4 + y, fd),
        )

    load.wait()
    gathered(every, q_cols, q_sems)
    for r in range(4):
        forward(runs[r], kv_cols, g_sems.at[r])
        if r + AHEAD < 4:
            spread_run(r + AHEAD)
        if r >= 1:
            x_second(r - 1)
        gathered(runs[r], kv_cols, g_sems.at[r])
        x_first(r)
        if r >= 1:
            x_third(r - 1)
    x_second(3)
    x_third(3)
    for h in (0, 1):
        for k in (0, 1):
            got(fin_in.at[h, k], f_sems.at[h, k])
    for k in (0, 1):
        out[pl.ds(HD * k, HD)] = (
            (fin_in[0, k].astype(F32) + fin_in[1, k].astype(F32)).T
        ).astype(BF16)
    mail.flush()


def input_gradient(dkv, dq, w_all):
    quarter = w_all.shape[1]
    d = quarter // 4
    any_space = pl.BlockSpec(memory_space=pl.ANY)
    vmem = pl.BlockSpec(memory_space=pltpu.VMEM)
    dma = pltpu.SemaphoreType.DMA
    run = (HD, 2 * HD)
    block, lane = (d, HD), (d // 2, HD)
    return pl.pallas_call(
        gradient_kernel,
        name="input_gradient",
        out_shape=jax.ShapeDtypeStruct((2 * HD, d), BF16),
        in_specs=[vmem, vmem, any_space],
        out_specs=vmem,
        scratch_shapes=[
            pltpu.VMEM(w_all.shape, BF16),
            pltpu.VMEM((4, 4 * HD, 3 * HD), BF16),
            pltpu.VMEM((4, 4) + run, BF16),
            pltpu.VMEM((2, 2) + run, BF16),
            pltpu.VMEM((2, 2, 2) + run, BF16),
            pltpu.VMEM((2, 2) + run, BF16),
            pltpu.VMEM((2, 2, 2) + run, BF16),
            pltpu.VMEM((4, 2) + lane, BF16),
            pltpu.VMEM((4, 2, 2) + lane, BF16),
            pltpu.VMEM((4, 2) + lane, BF16),
            pltpu.VMEM((4, 2, 2) + lane, BF16),
            pltpu.VMEM((4, 2) + lane, F32),
            pltpu.VMEM((4,) + block, BF16),
            pltpu.VMEM((2, 2) + block, BF16),
            dma((72,)), dma, dma((4,)), dma((2, 2)), dma((2, 2, 2)), dma((4,)), dma((4, 4)),
            dma((4, 2)), dma((4, 2, 2)), dma((2, 2)),
        ],
        compiler_params=pltpu.CompilerParams(
            collective_id=1, has_side_effects=True, vmem_limit_bytes=VMEM_BYTES
        ),
    )(dkv, dq, w_all)


def shards(inputs, w_qkv, selected, d_attn):
    w3 = w_qkv.transpose(1, 0, 2)
    q, kv, do, w_all = project_and_gather(inputs, w3, d_attn)
    dq, dkv = attend(
        selected.T, q, kv.reshape(8, BLOCK, 2 * HD), do
    )
    return input_gradient(dkv.reshape(4, 4, 2, HD, 2 * HD), dq.reshape(4 * HD, HD), w_all)


def solution(mesh):
    placed = (P("ctx", None), P("ctx", None, "fsdp"), P(), P("ctx", "fsdp"))
    return jax.shard_map(
        shards, mesh=mesh, in_specs=placed, out_specs=P("ctx", "fsdp"), check_vma=False
    )
```

```python
import functools

import jax
import jax.numpy as jnp
from jax import lax
from jax.experimental import pallas as pl
from jax.experimental.pallas import tpu as pltpu
from jax.sharding import PartitionSpec as P

MESH = pl.DeviceIdType.MESH
F32 = jnp.float32
BF16 = jnp.bfloat16
HD = 128
BLOCK = 512
TOP = 4
SCALE = HD ** (-0.5)
AHEAD = 2
VMEM_BYTES = 60 * 1024 * 1024


def place():
    c = lax.axis_index("ctx")
    f = lax.axis_index("fsdp")
    return (
        lax.div(c, 4), lax.rem(c, 4),
        lax.div(f, 8), lax.rem(lax.div(f, 2), 4), lax.rem(f, 2),
    )


def device(z, y, zh, x, k):
    return (z * 4 + y, zh * 8 + x * 2 + k)


def around(z, y, zh, x, k, by):
    at = lax.rem(4 * zh + z + 8 + by, 8)
    return device(lax.rem(at, 4), y, lax.div(at, 4), x, k)


def turn(i, by):
    return lax.rem(i + by, 4)


def rows(start, size):
    return pl.ds(pl.multiple_of(start, size & -size), size)


class Mail:
    def __init__(self, send_sems):
        self.send_sems = send_sems
        self.used = 0
        self.sent = []

    def copy(self, src, dst, recv, dev):
        sem = self.send_sems.at[self.used]
        self.used += 1
        return pltpu.make_async_remote_copy(
            src_ref=src, dst_ref=dst, send_sem=sem, recv_sem=recv,
            device_id=dev, device_id_type=MESH,
        )

    def send(self, src, dst, recv, dev):
        copy = self.copy(src, dst, recv, dev)
        copy.start()
        self.sent.append((copy, None, None))

    def send_or_keep(self, away, src, dst, recv, dev):
        copy = self.copy(src, dst, recv, dev)
        stay = pltpu.make_async_copy(src, dst, recv)

        @pl.when(away)
        def _():
            copy.start()

        @pl.when(jnp.logical_not(away))
        def _():
            stay.start()

        self.sent.append((copy, away, None))

    def send_if(self, away, src, dst, recv, dev):
        copy = self.copy(src, dst, recv, dev)

        @pl.when(away)
        def _():
            copy.start()

        self.sent.append((copy, away, None))

    def flush(self):
        for copy, away, _ in self.sent:
            if away is None:
                copy.wait_send()
            else:
                pl.when(away)(copy.wait_send)


def got(dst, recv):
    pltpu.make_async_copy(dst, dst, recv).wait()


class Ring:
    def __init__(self, mail, view, pos, core, right, left, partner, ring, cores):
        self.mail, self.view, self.pos, self.core = mail, view, pos, core
        self.right, self.left, self.partner = right, left, partner
        self.ring, self.cores = ring, cores

    def pass_on(self, pos, half, recv, dev):
        ref = self.view(self.core, pos, half)
        self.mail.send(ref, ref, recv, dev)

    def across(self, pos, half, n):
        if self.partner is not None:
            self.pass_on(pos, half, self.cores.at[n], self.partner)

    def start(self):
        self.pass_on(self.pos, None, self.ring.at[0], self.right)
        self.pass_on(self.pos, None, self.ring.at[1], self.left)
        self.across(self.pos, None, 0)

    def relay(self):
        before, after = turn(self.pos, 3), turn(self.pos, 1)
        got(self.view(self.core, before, None), self.ring.at[0])
        self.pass_on(before, 0, self.ring.at[2], self.right)
        self.across(before, None, 1)
        got(self.view(self.core, after, None), self.ring.at[1])
        self.pass_on(after, 1, self.ring.at[3], self.left)
        self.across(after, None, 2)

    def finish(self):
        far = turn(self.pos, 2)
        for half in (0, 1):
            got(self.view(self.core, far, half), self.ring.at[2 + half])
            self.across(far, half, 3 + half)

    def settle(self):
        other = 1 - self.core
        before, after, far = turn(self.pos, 3), turn(self.pos, 1), turn(self.pos, 2)
        got(self.view(other, self.pos, None), self.cores.at[0])
        got(self.view(other, before, None), self.cores.at[1])
        got(self.view(other, after, None), self.cores.at[2])
        got(self.view(other, far, 0), self.cores.at[3])
        got(self.view(other, far, 1), self.cores.at[4])


def enter(devices, more=0):
    barrier = pltpu.get_barrier_semaphore()
    for dev in devices:
        pl.semaphore_signal(barrier, inc=1, device_id=dev, device_id_type=MESH)
    return barrier, len(devices) + more


def project_kernel(
    inp, w3, d_attn, q_out, kv_out, do_out, w_out,
    wall, xall, dall, part, parts_in, via_in, own, kvall,
    send_sems, load_sems, w_ring, w_cores, x_z, x_x, d_sems, p_sems, via_sems,
    kv_ring, kv_cores, out_sems,
):
    z, y, zh, x, j = place()
    partner = device(z, y, zh, x, 1 - j)
    right = device(z, turn(y, 1), zh, x, j)
    left = device(z, turn(y, 3), zh, x, j)
    dq = wall.shape[1]
    d = dq // 4
    up = z >= 2
    end = jnp.logical_or(z == 0, z == 3)
    mid = jnp.logical_not(end)
    flip = lambda h: jnp.where(up, h, 3 - h)
    heads = tuple(flip(jnp.where(end, p, (p + 3) % 4)) for p in range(4))
    inside = device(jnp.where(up, 2, 1), y, zh, x, j)
    kinds = [pl.ds(HD * i, HD) for i in range(3)]

    loads = []
    for i, p in enumerate((1, 2, 0)):
        for s in (0, 1):
            loads.append(pltpu.make_async_copy(
                w3.at[p, :, pl.ds(HD * s, HD)],
                wall.at[2 * j + s, rows(d * y, d), kinds[i]],
                load_sems.at[2 * i + s],
            ))
    own_x = pltpu.make_async_copy(
        inp.at[rows(HD * j, HD), rows(dq * z, dq)], xall.at[rows(HD * z, HD)], load_sems.at[6]
    )
    for copy in loads:
        copy.start()
    own_x.start()

    peers = [device(turn(z, t), y, zh, x, k) for t in (1, 2, 3) for k in (j, 1 - j)]
    peers += [partner, right, left]
    peers += [device(z, y, zh, turn(x, u), j) for u in (1, 3)]
    peers += [around(z, y, zh, x, j, by) for by in (1, -1, 2, -2)]
    barrier, expected = enter(peers)
    pl.semaphore_wait(barrier, expected)

    mail = Mail(send_sems)

    def w_view(i):
        def view(core, pos, half):
            if half is None:
                return wall.at[pl.ds(2 * core, 2), rows(d * pos, d), kinds[i]]
            return wall.at[
                pl.ds(2 * core, 2), rows(d * pos + (d // 2) * half, d // 2), kinds[i]
            ]
        return view

    w_rings = [
        Ring(mail, w_view(i), y, j, right, left, partner, w_ring.at[i], w_cores.at[i])
        for i in range(3)
    ]
    piece = HD // 4

    def quarter(run, of_x, low=0, size=piece):
        return xall.at[rows(HD * run + piece * of_x + low, size)]

    hops = ((1, 0, piece), (-1, 0, piece), (2, 0, piece // 2), (-2, piece // 2, piece // 2))
    opposite = turn(x, 2)

    def x_send(turn_of):
        of_x = (x, opposite)[turn_of]
        for n, (by, low, size) in enumerate(hops):
            mail.send(
                inp.at[rows(HD * j + piece * of_x + low, size), rows(dq * turn(z, 4 + by), dq)],
                quarter(z, of_x, low, size), x_z.at[turn_of, n], around(z, y, zh, x, j, by),
            )

    def x_got(turn_of, n):
        by, low, size = hops[n]
        got(quarter(turn(z, 4 - by), (x, opposite)[turn_of], low, size), x_z.at[turn_of, n])

    def x_share(by):
        mine = quarter(turn(z, 4 - by), x)
        for u in (1, 3):
            mail.send(
                mine, mine, x_x.at[by % 4, u // 2], device(z, y, zh, turn(x, u), j)
            )

    def x_shared(by):
        for u in (1, 3):
            got(quarter(turn(z, 4 - by), turn(x, 4 - u)), x_x.at[by % 4, u // 2])

    def project(i):
        cols = kinds[i]
        for p in range(4):
            head = heads[p]
            if p % 2 == 0:
                both = jnp.dot(
                    xall[...],
                    jnp.concatenate([wall[head, :, cols], wall[heads[p + 1], :, cols]], axis=1),
                    preferred_element_type=F32,
                )
            total = both[:, HD * (p % 2) : HD * (p % 2 + 1)]
            if p == 3:
                own[:, cols] = total
                continue
            mine = part.at[p, :, cols]
            there = parts_in.at[z, :, cols]

            def store():
                part[p, :, cols] = total.astype(BF16)

            def store_both():
                got(via_in.at[p - 1, :, cols], via_sems.at[p - 1, i])
                part[p, :, cols] = (total + via_in[p - 1, :, cols].astype(F32)).astype(BF16)

            if p == 0:
                store()
            else:
                pl.when(end)(store)
                pl.when(mid)(store_both)
            if p < 2:
                mail.send_if(end, mine, via_in.at[p, :, cols], via_sems.at[p, i], inside)
                mail.send_if(mid, mine, there, p_sems.at[z, i], device(head, y, zh, x, j))
            else:
                mail.send(mine, there, p_sems.at[z, i], device(head, y, zh, x, j))

    for copy in loads[:2]:
        copy.wait()
    w_rings[0].start()
    x_send(0)
    x_send(1)
    for copy in loads[2:]:
        copy.wait()
    for n, by in ((0, 1), (1, -1)):
        x_got(0, n)
        x_share(by)
    w_rings[0].relay()
    w_rings[1].start()
    x_got(0, 2)
    x_got(0, 3)
    x_share(2)
    own_x.wait()
    w_rings[0].finish()
    w_rings[0].settle()
    for by in (1, -1, 2):
        x_shared(by)
    for n in range(4):
        x_got(1, n)
    w_rings[1].relay()
    w_rings[2].start()
    project(0)
    w_rings[1].finish()
    w_rings[1].settle()
    project(1)
    w_rings[2].relay()

    one = jnp.where(z == 1, 2, 1)
    two = jnp.where(end, 2, jnp.where(up, 3, 0))

    def collect(i):
        cols = kinds[i]
        total = own[:, cols]
        for source in (one, two):
            got(parts_in.at[source, :, cols], p_sems.at[source, i])
            total += parts_in[source, :, cols].astype(F32)
        low = total.astype(BF16)
        for run in range(4):
            if i == 2:
                q_out[run] = low[HD * run : HD * (run + 1)]
            else:
                kvall[run, y, j, :, cols] = low[HD * run : HD * (run + 1)]

    def kv_view(i):
        def view(core, pos, half):
            if half is None:
                return kvall.at[:, pos, core, :, kinds[i]]
            return kvall.at[pl.ds(2 * half, 2), pos, core, :, kinds[i]]
        return view

    kv = [
        Ring(mail, kv_view(i), y, j, right, left, partner, kv_ring.at[i], kv_cores.at[i])
        for i in (0, 1)
    ]
    collect(0)
    kv[0].start()
    w_rings[2].finish()
    w_rings[2].settle()
    keep_w = pltpu.make_async_copy(wall, w_out, out_sems.at[0])
    keep_w.start()
    project(2)
    for s in (0, 1):
        for k in (0, 1):
            zd = 2 * j + s
            away = jnp.logical_or(zd != z, j != k)
            mail.send_or_keep(
                away,
                d_attn.at[pl.ds(HD * k, HD), pl.ds(HD * s, HD)],
                dall.at[z], d_sems.at[z], device(zd, y, zh, x, k),
            )

    kv[0].relay()
    collect(1)
    kv[1].start()
    kv[0].finish()
    kv[1].relay()
    for zs in range(4):
        got(dall.at[zs], d_sems.at[zs])
    do_out[...] = dall[...]
    collect(2)
    kv[1].finish()
    for i in (0, 1):
        kv[i].settle()
    keep_kv = pltpu.make_async_copy(kvall, kv_out, out_sems.at[1])
    keep_kv.start()
    mail.flush()
    keep_w.wait()
    keep_kv.wait()


def project_and_gather(inputs, w3, d_attn):
    rows_here, width = inputs.shape
    quarter = width // 4
    any_space = pl.BlockSpec(memory_space=pl.ANY)
    vmem = pl.BlockSpec(memory_space=pltpu.VMEM)
    dma = pltpu.SemaphoreType.DMA
    return pl.pallas_call(
        project_kernel,
        name="project_and_gather",
        out_shape=(
            jax.ShapeDtypeStruct((4, HD, HD), BF16),
            jax.ShapeDtypeStruct((4, 4, 2, HD, 2 * HD), BF16),
            jax.ShapeDtypeStruct((4, HD, HD), BF16),
            jax.ShapeDtypeStruct((4, quarter, 3 * HD), BF16),
        ),
        in_specs=[any_space] * 3,
        out_specs=(vmem, any_space, vmem, any_space),
        scratch_shapes=[
            pltpu.VMEM((4, quarter, 3 * HD), BF16),
            pltpu.VMEM((4 * HD, quarter), BF16),
            pltpu.VMEM((4, HD, HD), BF16),
            pltpu.VMEM((4, 4 * HD, 3 * HD), BF16),
            pltpu.VMEM((4, 4 * HD, 3 * HD), BF16),
            pltpu.VMEM((2, 4 * HD, 3 * HD), BF16),
            pltpu.VMEM((4 * HD, 3 * HD), F32),
            pltpu.VMEM((4, 4, 2, HD, 2 * HD), BF16),
            dma((80,)), dma((7,)), dma((3, 4)), dma((3, 5)), dma((2, 4)), dma((4, 2)),
            dma((4,)), dma((4, 3)), dma((2, 3)), dma((2, 4)), dma((2, 5)), dma((2,)),
        ],
        compiler_params=pltpu.CompilerParams(
            collective_id=0, has_side_effects=True, vmem_limit_bytes=VMEM_BYTES
        ),
    )(inputs, w3, d_attn)


def attend_kernel(selected, q_ref, kv_ref, do_ref, dq_ref, dkv_ref, score, dprob, pair, total):
    _, y, _, _, j = place()
    total[...] = jnp.zeros_like(total)
    pair[...] = jnp.zeros_like(pair)
    contract = lambda a, b: (((a,), (b,)), ((), ()))
    dot = functools.partial(lax.dot_general, preferred_element_type=F32)
    key_at = lax.broadcasted_iota(jnp.int32, (BLOCK, HD), 0)
    query_at = lax.broadcasted_iota(jnp.int32, (BLOCK, HD), 1)

    def tile(run, carry):
        first = (run * 4 + y) * 256 + HD * j
        block = lax.div(first, BLOCK)
        pair[:HD, :HD] = q_ref[run]
        pair[HD:, HD:] = do_ref[run]
        both = pair[...]
        highest = jnp.full((1, HD), -jnp.inf, F32)
        for t in range(TOP):
            chosen = selected[t, block]
            kb = jnp.maximum(chosen, 0)
            products = dot(kv_ref[kb], both, contract(1, 1))
            limit = jnp.where(chosen >= 0, first - kb * BLOCK, -2 * BLOCK)
            s = jnp.where(key_at - query_at <= limit, products[:, :HD] * SCALE, -jnp.inf)
            score[t] = s
            dprob[t] = products[:, HD:]
            highest = jnp.maximum(highest, jnp.max(s, axis=0, keepdims=True))
        totals = jnp.zeros((1, HD), F32)
        delta = jnp.zeros((1, HD), F32)
        for t in range(TOP):
            e = jnp.exp(score[t] - highest)
            score[t] = e
            totals += jnp.sum(e, axis=0, keepdims=True)
            delta += jnp.sum(e * dprob[t], axis=0, keepdims=True)
        share = 1.0 / totals
        delta = delta * share
        dq = jnp.zeros((HD, HD), F32)
        for t in range(TOP):
            kb = jnp.maximum(selected[t, block], 0)
            p = score[t] * share
            ds = (p * (dprob[t] - delta)).astype(BF16)
            total[kb] += dot(
                jnp.concatenate([ds, p.astype(BF16)], axis=1), both, contract(1, 0)
            )
            dq += dot(ds, kv_ref[kb, :, :HD], contract(0, 0))
        dq_ref[run] = (dq * SCALE).astype(BF16)
        return carry

    lax.fori_loop(0, 4, tile, 0)
    for b in range(8):
        dkv_ref[b, :, :HD] = (total[b, :, :HD] * SCALE).astype(BF16)
        dkv_ref[b, :, HD:] = total[b, :, HD:].astype(BF16)


def attend(selected, q, kv, do):
    vmem = pl.BlockSpec(memory_space=pltpu.VMEM)
    return pl.pallas_call(
        attend_kernel,
        name="attend",
        out_shape=(
            jax.ShapeDtypeStruct((4, HD, HD), BF16),
            jax.ShapeDtypeStruct((8, BLOCK, 2 * HD), BF16),
        ),
        in_specs=[pl.BlockSpec(memory_space=pltpu.SMEM), vmem, vmem, vmem],
        out_specs=(vmem, vmem),
        scratch_shapes=[
            pltpu.VMEM((TOP, BLOCK, HD), F32),
            pltpu.VMEM((TOP, BLOCK, HD), F32),
            pltpu.VMEM((2 * HD, 2 * HD), BF16),
            pltpu.VMEM((8, BLOCK, 2 * HD), F32),
        ],
        compiler_params=pltpu.CompilerParams(vmem_limit_bytes=VMEM_BYTES),
    )(selected, q, kv, do)


def owner_x(z, jj):
    at = jnp.where(lax.rem(jj, 2) == 0, lax.div(jj, 2), lax.div(7 - jj, 2))
    return turn(at, 2 * lax.rem(z, 2))


def block_of(z, x):
    at = turn(x, 2 * lax.rem(z, 2))
    return jnp.where(at < 2, 2 * at, 7 - 2 * at)


def gradient_kernel(
    dkv, dq, w_in, out,
    wall, gall, core_in, far_out, near_out, far_in, near_in,
    xf_out, xn_out, xf_in, xn_in, own_x, fin, fin_in,
    send_sems, load_sem, core_sems, far_sems, near_sems, q_sems, g_sems, xf_sems, xn_sems, f_sems,
):
    z, y, zh, x, j = place()
    d = wall.shape[1] // 4
    f = lax.axis_index("fsdp")
    partner = device(z, y, zh, x, 1 - j)
    right = device(z, turn(y, 1), zh, x, j)
    left = device(z, turn(y, 3), zh, x, j)
    x_right = device(z, y, zh, turn(x, 1), j)
    x_left = device(z, y, zh, turn(x, 3), j)
    up = z >= 2
    end = jnp.logical_or(z == 0, z == 3)
    mid = jnp.logical_not(end)
    flip = lambda h: jnp.where(up, h, 3 - h)
    at_z = lambda h: device(h, y, zh, x, j)
    first_z = flip(jnp.where(end, 2, 1))
    second_z = flip(jnp.where(end, 1, 3))
    far_z = flip(0)

    load = pltpu.make_async_copy(w_in, wall, load_sem)
    load.start()

    across = [at_z(turn(z, t)) for t in (1, 2, 3)]
    barrier, expected = enter([partner, right, left, x_right, x_left] + across, more=4)
    source_z = lax.div(f, 4)
    source_x = owner_x(source_z, lax.rem(f, 4))
    for h in (0, 1):
        for k in (0, 1):
            pl.semaphore_signal(
                barrier, inc=1, device_id=device(source_z, y, h, source_x, k),
                device_id_type=MESH,
            )
    pl.semaphore_wait(barrier, expected)

    mail = Mail(send_sems)

    def spread(src, at, cols, sems):
        there = gall.at[z, at, cols]
        mail.send(src, there, sems.at[z], at_z(first_z))
        mail.send(src, there, sems.at[z], at_z(second_z))

    def forward(at, cols, sems):
        for h in (first_z, far_z):
            block = gall.at[h, at, cols]
            pl.when(mid)(lambda: got(block, sems.at[h]))
            mail.send_if(mid, block, block, sems.at[h], at_z(second_z))

    def gathered(at, cols, sems):
        def wait(h):
            got(gall.at[h, at, cols], sems.at[h])

        wait(second_z)

        @pl.when(end)
        def _():
            wait(first_z)
            wait(3 - z)

    runs = [pl.ds(HD * r, HD) for r in range(4)]
    every, q_cols, kv_cols = pl.ds(0, 4 * HD), pl.ds(2 * HD, HD), pl.ds(0, 2 * HD)
    for n, t in enumerate((2, 1, 3, 0)):
        mail.send(dkv.at[:, turn(y, t), 1 - j], core_in.at[n], core_sems.at[n], partner)
    spread(dq, every, q_cols, q_sems)
    gall[z, :, q_cols] = dq[...]

    def chip_sum(n, t, run):
        return dkv[run, turn(y, t), j].astype(F32) + core_in[n, run].astype(F32)

    def far(h):
        for side, dev in ((0, right), (1, left)):
            far_out[h, side] = chip_sum(0, 2, 2 * h + side).astype(BF16)
            mail.send(far_out.at[h, side], far_in.at[h, side], far_sems.at[h, side], dev)

    def near(h, term):
        for side, (t, dev) in enumerate(((1, right), (3, left))):
            lane = side if term else 1 - side
            total = chip_sum(1 + side, t, 2 * h + lane)
            if term:
                got(far_in.at[h, side], far_sems.at[h, side])
                total += far_in[h, side].astype(F32)
            near_out[h, side, lane] = total.astype(BF16)
            mail.send(
                near_out.at[h, side, lane], near_in.at[h, side, lane],
                near_sems.at[h, side, lane], dev,
            )

    def spread_run(run):
        at = runs[run]
        spread(gall.at[z, at, kv_cols], at, kv_cols, g_sems.at[run])

    def finish_kv(h):
        for lane in (0, 1):
            for side in (1 - lane, lane):
                got(near_in.at[h, side, lane], near_sems.at[h, side, lane])
        for lane in (0, 1):
            run = 2 * h + lane
            total = chip_sum(3, 0, run)
            for side in (0, 1):
                total += near_in[h, side, lane].astype(F32)
            at = runs[run]
            gall[z, at, kv_cols] = total.astype(BF16)
            if run < AHEAD:
                spread_run(run)

    got(core_in.at[0], core_sems.at[0])
    far(0)
    got(core_in.at[1], core_sems.at[1])
    got(core_in.at[2], core_sems.at[2])
    near(0, False)
    far(1)
    got(core_in.at[3], core_sems.at[3])
    near(0, True)
    near(1, False)
    forward(every, q_cols, q_sems)
    finish_kv(0)
    near(1, True)
    finish_kv(1)

    def part(t, r):
        cols = rows(d * block_of(z, turn(x, t)), d)
        total = jnp.zeros((d, HD), F32)
        for head in range(4):
            total += lax.dot_general(
                wall[head, cols], gall[head, runs[r]], (((1,), (1,)), ((), ())),
                preferred_element_type=F32,
            )
        return total[: d // 2], total[d // 2 :]

    def x_first(r):
        total = part(2, r)
        for side, dev in ((0, x_right), (1, x_left)):
            xf_out[r, side] = total[side].astype(BF16)
            mail.send(xf_out.at[r, side], xf_in.at[r, side], xf_sems.at[r, side], dev)
        for side, (t, dev) in enumerate(((1, x_right), (3, x_left))):
            total = part(t, r)
            alone = 1 - side
            xn_out[r, side, alone] = total[alone].astype(BF16)
            own_x[r, side] = total[side]
            mail.send(
                xn_out.at[r, side, alone], xn_in.at[r, side, alone],
                xn_sems.at[r, side, alone], dev,
            )

    def x_second(r):
        for side, dev in ((0, x_right), (1, x_left)):
            got(xf_in.at[r, side], xf_sems.at[r, side])
            xn_out[r, side, side] = (
                own_x[r, side] + xf_in[r, side].astype(F32)
            ).astype(BF16)
            mail.send(
                xn_out.at[r, side, side], xn_in.at[r, side, side], xn_sems.at[r, side, side], dev
            )
        total = part(0, r)
        for lane in (0, 1):
            own_x[r, lane] = total[lane]

    fd = 4 * z + block_of(z, x)

    def x_third(r):
        for lane in (0, 1):
            total = own_x[r, lane]
            for side in (1 - lane, lane):
                got(xn_in.at[r, side, lane], xn_sems.at[r, side, lane])
                total += xn_in[r, side, lane].astype(F32)
            fin[r, pl.ds((d // 2) * lane, d // 2)] = total.astype(BF16)
        mail.send_or_keep(
            jnp.logical_or(r != z, fd != f), fin.at[r], fin_in.at[zh, j],
            f_sems.at[zh, j], (r * 4 + y, fd),
        )

    load.wait()
    gathered(every, q_cols, q_sems)
    for r in range(4):
        forward(runs[r], kv_cols, g_sems.at[r])
        if r + AHEAD < 4:
            spread_run(r + AHEAD)
        if r >= 1:
            x_second(r - 1)
        gathered(runs[r], kv_cols, g_sems.at[r])
        x_first(r)
        if r >= 1:
            x_third(r - 1)
    x_second(3)
    x_third(3)
    for h in (0, 1):
        for k in (0, 1):
            got(fin_in.at[h, k], f_sems.at[h, k])
    for k in (0, 1):
        out[pl.ds(HD * k, HD)] = (
            (fin_in[0, k].astype(F32) + fin_in[1, k].astype(F32)).T
        ).astype(BF16)
    mail.flush()


def input_gradient(dkv, dq, w_all):
    quarter = w_all.shape[1]
    d = quarter // 4
    any_space = pl.BlockSpec(memory_space=pl.ANY)
    vmem = pl.BlockSpec(memory_space=pltpu.VMEM)
    dma = pltpu.SemaphoreType.DMA
    run = (HD, 2 * HD)
    block, lane = (d, HD), (d // 2, HD)
    return pl.pallas_call(
        gradient_kernel,
        name="input_gradient",
        out_shape=jax.ShapeDtypeStruct((2 * HD, d), BF16),
        in_specs=[vmem, vmem, any_space],
        out_specs=vmem,
        scratch_shapes=[
            pltpu.VMEM(w_all.shape, BF16),
            pltpu.VMEM((4, 4 * HD, 3 * HD), BF16),
            pltpu.VMEM((4, 4) + run, BF16),
            pltpu.VMEM((2, 2) + run, BF16),
            pltpu.VMEM((2, 2, 2) + run, BF16),
            pltpu.VMEM((2, 2) + run, BF16),
            pltpu.VMEM((2, 2, 2) + run, BF16),
            pltpu.VMEM((4, 2) + lane, BF16),
            pltpu.VMEM((4, 2, 2) + lane, BF16),
            pltpu.VMEM((4, 2) + lane, BF16),
            pltpu.VMEM((4, 2, 2) + lane, BF16),
            pltpu.VMEM((4, 2) + lane, F32),
            pltpu.VMEM((4,) + block, BF16),
            pltpu.VMEM((2, 2) + block, BF16),
            dma((72,)), dma, dma((4,)), dma((2, 2)), dma((2, 2, 2)), dma((4,)), dma((4, 4)),
            dma((4, 2)), dma((4, 2, 2)), dma((2, 2)),
        ],
        compiler_params=pltpu.CompilerParams(
            collective_id=1, has_side_effects=True, vmem_limit_bytes=VMEM_BYTES
        ),
    )(dkv, dq, w_all)


def shards(inputs, w_qkv, selected, d_attn):
    w3 = w_qkv.transpose(1, 0, 2)
    q, kv, do, w_all = project_and_gather(inputs, w3, d_attn)
    dq, dkv = attend(
        selected.T, q, kv.reshape(8, BLOCK, 2 * HD), do
    )
    return input_gradient(dkv.reshape(4, 4, 2, HD, 2 * HD), dq.reshape(4 * HD, HD), w_all)


def solution(mesh):
    placed = (P("ctx", None), P("ctx", None, "fsdp"), P(), P("ctx", "fsdp"))
    return jax.shard_map(
        shards, mesh=mesh, in_specs=placed, out_specs=P("ctx", "fsdp"), check_vma=False
    )
```

```python
import functools

import jax
import jax.numpy as jnp
from jax import lax
from jax.experimental import pallas as pl
from jax.experimental.pallas import tpu as pltpu
from jax.sharding import PartitionSpec as P

MESH = pl.DeviceIdType.MESH
F32 = jnp.float32
BF16 = jnp.bfloat16
HD = 128
BLOCK = 512
TOP = 4
SCALE = HD ** (-0.5)
AHEAD = 2
VMEM_BYTES = 60 * 1024 * 1024


def place():
    c = lax.axis_index("ctx")
    f = lax.axis_index("fsdp")
    return (
        lax.div(c, 4), lax.rem(c, 4),
        lax.div(f, 8), lax.rem(lax.div(f, 2), 4), lax.rem(f, 2),
    )


def device(z, y, zh, x, k):
    return (z * 4 + y, zh * 8 + x * 2 + k)


def around(z, y, zh, x, k, by):
    at = lax.rem(4 * zh + z + 8 + by, 8)
    return device(lax.rem(at, 4), y, lax.div(at, 4), x, k)


def turn(i, by):
    return lax.rem(i + by, 4)


def rows(start, size):
    return pl.ds(pl.multiple_of(start, size & -size), size)


class Mail:
    def __init__(self, send_sems):
        self.send_sems = send_sems
        self.used = 0
        self.sent = []

    def copy(self, src, dst, recv, dev):
        sem = self.send_sems.at[self.used]
        self.used += 1
        return pltpu.make_async_remote_copy(
            src_ref=src, dst_ref=dst, send_sem=sem, recv_sem=recv,
            device_id=dev, device_id_type=MESH,
        )

    def send(self, src, dst, recv, dev):
        copy = self.copy(src, dst, recv, dev)
        copy.start()
        self.sent.append((copy, None, None))

    def send_or_keep(self, away, src, dst, recv, dev):
        copy = self.copy(src, dst, recv, dev)
        stay = pltpu.make_async_copy(src, dst, recv)

        @pl.when(away)
        def _():
            copy.start()

        @pl.when(jnp.logical_not(away))
        def _():
            stay.start()

        self.sent.append((copy, away, None))

    def send_if(self, away, src, dst, recv, dev):
        copy = self.copy(src, dst, recv, dev)

        @pl.when(away)
        def _():
            copy.start()

        self.sent.append((copy, away, None))

    def flush(self):
        for copy, away, _ in self.sent:
            if away is None:
                copy.wait_send()
            else:
                pl.when(away)(copy.wait_send)


def got(dst, recv):
    pltpu.make_async_copy(dst, dst, recv).wait()


class Ring:
    def __init__(self, mail, view, pos, core, right, left, partner, ring, cores):
        self.mail, self.view, self.pos, self.core = mail, view, pos, core
        self.right, self.left, self.partner = right, left, partner
        self.ring, self.cores = ring, cores

    def pass_on(self, pos, half, recv, dev):
        ref = self.view(self.core, pos, half)
        self.mail.send(ref, ref, recv, dev)

    def across(self, pos, half, n):
        if self.partner is not None:
            self.pass_on(pos, half, self.cores.at[n], self.partner)

    def start(self):
        self.pass_on(self.pos, None, self.ring.at[0], self.right)
        self.pass_on(self.pos, None, self.ring.at[1], self.left)
        self.across(self.pos, None, 0)

    def relay(self):
        before, after = turn(self.pos, 3), turn(self.pos, 1)
        got(self.view(self.core, before, None), self.ring.at[0])
        self.pass_on(before, 0, self.ring.at[2], self.right)
        self.across(before, None, 1)
        got(self.view(self.core, after, None), self.ring.at[1])
        self.pass_on(after, 1, self.ring.at[3], self.left)
        self.across(after, None, 2)

    def finish(self):
        far = turn(self.pos, 2)
        for half in (0, 1):
            got(self.view(self.core, far, half), self.ring.at[2 + half])
            self.across(far, half, 3 + half)

    def settle(self):
        other = 1 - self.core
        before, after, far = turn(self.pos, 3), turn(self.pos, 1), turn(self.pos, 2)
        got(self.view(other, self.pos, None), self.cores.at[0])
        got(self.view(other, before, None), self.cores.at[1])
        got(self.view(other, after, None), self.cores.at[2])
        got(self.view(other, far, 0), self.cores.at[3])
        got(self.view(other, far, 1), self.cores.at[4])


def enter(devices, more=0):
    barrier = pltpu.get_barrier_semaphore()
    for dev in devices:
        pl.semaphore_signal(barrier, inc=1, device_id=dev, device_id_type=MESH)
    return barrier, len(devices) + more


def project_kernel(
    inp, w3, d_attn, q_out, kv_out, do_out, w_out,
    wall, xall, dall, part, parts_in, via_in, own, kvall,
    send_sems, load_sems, w_ring, w_cores, x_z, x_x, d_sems, p_sems, via_sems,
    kv_ring, kv_cores, out_sems,
):
    z, y, zh, x, j = place()
    partner = device(z, y, zh, x, 1 - j)
    right = device(z, turn(y, 1), zh, x, j)
    left = device(z, turn(y, 3), zh, x, j)
    dq = wall.shape[1]
    d = dq // 4
    up = z >= 2
    end = jnp.logical_or(z == 0, z == 3)
    mid = jnp.logical_not(end)
    flip = lambda h: jnp.where(up, h, 3 - h)
    heads = tuple(flip(jnp.where(end, p, (p + 3) % 4)) for p in range(4))
    inside = device(jnp.where(up, 2, 1), y, zh, x, j)
    kinds = [pl.ds(HD * i, HD) for i in range(3)]

    loads = []
    for i, p in enumerate((1, 2, 0)):
        for s in (0, 1):
            loads.append(pltpu.make_async_copy(
                w3.at[p, :, pl.ds(HD * s, HD)],
                wall.at[2 * j + s, rows(d * y, d), kinds[i]],
                load_sems.at[2 * i + s],
            ))
    own_x = pltpu.make_async_copy(
        inp.at[rows(HD * j, HD), rows(dq * z, dq)], xall.at[rows(HD * z, HD)], load_sems.at[6]
    )
    for copy in loads:
        copy.start()
    own_x.start()

    peers = [device(turn(z, t), y, zh, x, k) for t in (1, 2, 3) for k in (j, 1 - j)]
    peers += [partner, right, left]
    peers += [device(z, y, zh, turn(x, u), j) for u in (1, 3)]
    peers += [around(z, y, zh, x, j, by) for by in (1, -1, 2, -2)]
    barrier, expected = enter(peers)
    pl.semaphore_wait(barrier, expected)

    mail = Mail(send_sems)

    def w_view(i):
        def view(core, pos, half):
            if half is None:
                return wall.at[pl.ds(2 * core, 2), rows(d * pos, d), kinds[i]]
            return wall.at[
                pl.ds(2 * core, 2), rows(d * pos + (d // 2) * half, d // 2), kinds[i]
            ]
        return view

    w_rings = [
        Ring(mail, w_view(i), y, j, right, left, partner, w_ring.at[i], w_cores.at[i])
        for i in range(3)
    ]
    piece = HD // 4

    def quarter(run, of_x, low=0, size=piece):
        return xall.at[rows(HD * run + piece * of_x + low, size)]

    hops = ((1, 0, piece), (-1, 0, piece), (2, 0, piece // 2), (-2, piece // 2, piece // 2))
    opposite = turn(x, 2)

    def x_send(turn_of):
        of_x = (x, opposite)[turn_of]
        for n, (by, low, size) in enumerate(hops):
            mail.send(
                inp.at[rows(HD * j + piece * of_x + low, size), rows(dq * turn(z, 4 + by), dq)],
                quarter(z, of_x, low, size), x_z.at[turn_of, n], around(z, y, zh, x, j, by),
            )

    def x_got(turn_of, n):
        by, low, size = hops[n]
        got(quarter(turn(z, 4 - by), (x, opposite)[turn_of], low, size), x_z.at[turn_of, n])

    def x_share(by):
        mine = quarter(turn(z, 4 - by), x)
        for u in (1, 3):
            mail.send(
                mine, mine, x_x.at[by % 4, u // 2], device(z, y, zh, turn(x, u), j)
            )

    def x_shared(by):
        for u in (1, 3):
            got(quarter(turn(z, 4 - by), turn(x, 4 - u)), x_x.at[by % 4, u // 2])

    def project(i):
        cols = kinds[i]
        for p in range(4):
            head = heads[p]
            if p % 2 == 0:
                both = jnp.dot(
                    xall[...],
                    jnp.concatenate([wall[head, :, cols], wall[heads[p + 1], :, cols]], axis=1),
                    preferred_element_type=F32,
                )
            total = both[:, HD * (p % 2) : HD * (p % 2 + 1)]
            if p == 3:
                own[:, cols] = total
                continue
            mine = part.at[p, :, cols]
            there = parts_in.at[z, :, cols]

            def store():
                part[p, :, cols] = total.astype(BF16)

            def store_both():
                got(via_in.at[p - 1, :, cols], via_sems.at[p - 1, i])
                part[p, :, cols] = (total + via_in[p - 1, :, cols].astype(F32)).astype(BF16)

            if p == 0:
                store()
            else:
                pl.when(end)(store)
                pl.when(mid)(store_both)
            if p < 2:
                mail.send_if(end, mine, via_in.at[p, :, cols], via_sems.at[p, i], inside)
                mail.send_if(mid, mine, there, p_sems.at[z, i], device(head, y, zh, x, j))
            else:
                mail.send(mine, there, p_sems.at[z, i], device(head, y, zh, x, j))

    for copy in loads[:2]:
        copy.wait()
    w_rings[0].start()
    x_send(0)
    x_send(1)
    for copy in loads[2:]:
        copy.wait()
    for n, by in ((0, 1), (1, -1)):
        x_got(0, n)
        x_share(by)
    w_rings[0].relay()
    w_rings[1].start()
    x_got(0, 2)
    x_got(0, 3)
    x_share(2)
    own_x.wait()
    w_rings[0].finish()
    w_rings[0].settle()
    for by in (1, -1, 2):
        x_shared(by)
    for n in range(4):
        x_got(1, n)
    w_rings[1].relay()
    w_rings[2].start()
    project(0)
    w_rings[1].finish()
    w_rings[1].settle()
    project(1)
    w_rings[2].relay()

    one = jnp.where(z == 1, 2, 1)
    two = jnp.where(end, 2, jnp.where(up, 3, 0))

    def collect(i):
        cols = kinds[i]
        total = own[:, cols]
        for source in (one, two):
            got(parts_in.at[source, :, cols], p_sems.at[source, i])
            total += parts_in[source, :, cols].astype(F32)
        low = total.astype(BF16)
        for run in range(4):
            if i == 2:
                q_out[run] = low[HD * run : HD * (run + 1)]
            else:
                kvall[run, y, j, :, cols] = low[HD * run : HD * (run + 1)]

    def kv_view(i):
        def view(core, pos, half):
            if half is None:
                return kvall.at[:, pos, core, :, kinds[i]]
            return kvall.at[pl.ds(2 * half, 2), pos, core, :, kinds[i]]
        return view

    kv = [
        Ring(mail, kv_view(i), y, j, right, left, partner, kv_ring.at[i], kv_cores.at[i])
        for i in (0, 1)
    ]
    collect(0)
    kv[0].start()
    w_rings[2].finish()
    w_rings[2].settle()
    keep_w = pltpu.make_async_copy(wall, w_out, out_sems.at[0])
    keep_w.start()
    project(2)
    for s in (0, 1):
        for k in (0, 1):
            zd = 2 * j + s
            away = jnp.logical_or(zd != z, j != k)
            mail.send_or_keep(
                away,
                d_attn.at[pl.ds(HD * k, HD), pl.ds(HD * s, HD)],
                dall.at[z], d_sems.at[z], device(zd, y, zh, x, k),
            )

    kv[0].relay()
    collect(1)
    kv[1].start()
    kv[0].finish()
    kv[1].relay()
    for zs in range(4):
        got(dall.at[zs], d_sems.at[zs])
    do_out[...] = dall[...]
    collect(2)
    kv[1].finish()
    for i in (0, 1):
        kv[i].settle()
    keep_kv = pltpu.make_async_copy(kvall, kv_out, out_sems.at[1])
    keep_kv.start()
    mail.flush()
    keep_w.wait()
    keep_kv.wait()


def project_and_gather(inputs, w3, d_attn):
    rows_here, width = inputs.shape
    quarter = width // 4
    any_space = pl.BlockSpec(memory_space=pl.ANY)
    vmem = pl.BlockSpec(memory_space=pltpu.VMEM)
    dma = pltpu.SemaphoreType.DMA
    return pl.pallas_call(
        project_kernel,
        name="project_and_gather",
        out_shape=(
            jax.ShapeDtypeStruct((4, HD, HD), BF16),
            jax.ShapeDtypeStruct((4, 4, 2, HD, 2 * HD), BF16),
            jax.ShapeDtypeStruct((4, HD, HD), BF16),
            jax.ShapeDtypeStruct((4, quarter, 3 * HD), BF16),
        ),
        in_specs=[any_space] * 3,
        out_specs=(vmem, any_space, vmem, any_space),
        scratch_shapes=[
            pltpu.VMEM((4, quarter, 3 * HD), BF16),
            pltpu.VMEM((4 * HD, quarter), BF16),
            pltpu.VMEM((4, HD, HD), BF16),
            pltpu.VMEM((4, 4 * HD, 3 * HD), BF16),
            pltpu.VMEM((4, 4 * HD, 3 * HD), BF16),
            pltpu.VMEM((2, 4 * HD, 3 * HD), BF16),
            pltpu.VMEM((4 * HD, 3 * HD), F32),
            pltpu.VMEM((4, 4, 2, HD, 2 * HD), BF16),
            dma((80,)), dma((7,)), dma((3, 4)), dma((3, 5)), dma((2, 4)), dma((4, 2)),
            dma((4,)), dma((4, 3)), dma((2, 3)), dma((2, 4)), dma((2, 5)), dma((2,)),
        ],
        compiler_params=pltpu.CompilerParams(
            collective_id=0, has_side_effects=True, vmem_limit_bytes=VMEM_BYTES
        ),
    )(inputs, w3, d_attn)


def attend_kernel(selected, q_ref, kv_ref, do_ref, dq_ref, dkv_ref, score, dprob, pair, total):
    _, y, _, _, j = place()
    total[...] = jnp.zeros_like(total)
    pair[...] = jnp.zeros_like(pair)
    contract = lambda a, b: (((a,), (b,)), ((), ()))
    dot = functools.partial(lax.dot_general, preferred_element_type=F32)
    key_at = lax.broadcasted_iota(jnp.int32, (BLOCK, HD), 0)
    query_at = lax.broadcasted_iota(jnp.int32, (BLOCK, HD), 1)

    def tile(run, carry):
        first = (run * 4 + y) * 256 + HD * j
        block = lax.div(first, BLOCK)
        pair[:HD, :HD] = q_ref[run]
        pair[HD:, HD:] = do_ref[run]
        both = pair[...]
        highest = jnp.full((1, HD), -jnp.inf, F32)
        for t in range(TOP):
            chosen = selected[t, block]
            kb = jnp.maximum(chosen, 0)
            products = dot(kv_ref[kb], both, contract(1, 1))
            limit = jnp.where(chosen >= 0, first - kb * BLOCK, -2 * BLOCK)
            s = jnp.where(key_at - query_at <= limit, products[:, :HD] * SCALE, -jnp.inf)
            score[t] = s
            dprob[t] = products[:, HD:]
            highest = jnp.maximum(highest, jnp.max(s, axis=0, keepdims=True))
        totals = jnp.zeros((1, HD), F32)
        delta = jnp.zeros((1, HD), F32)
        for t in range(TOP):
            e = jnp.exp(score[t] - highest)
            score[t] = e
            totals += jnp.sum(e, axis=0, keepdims=True)
            delta += jnp.sum(e * dprob[t], axis=0, keepdims=True)
        share = 1.0 / totals
        delta = delta * share
        dq = jnp.zeros((HD, HD), F32)
        for t in range(TOP):
            kb = jnp.maximum(selected[t, block], 0)
            p = score[t] * share
            ds = (p * (dprob[t] - delta)).astype(BF16)
            total[kb] += dot(
                jnp.concatenate([ds, p.astype(BF16)], axis=1), both, contract(1, 0)
            )
            dq += dot(ds, kv_ref[kb, :, :HD], contract(0, 0))
        dq_ref[run] = (dq * SCALE).astype(BF16)
        return carry

    lax.fori_loop(0, 4, tile, 0)
    for b in range(8):
        dkv_ref[b, :, :HD] = (total[b, :, :HD] * SCALE).astype(BF16)
        dkv_ref[b, :, HD:] = total[b, :, HD:].astype(BF16)


def attend(selected, q, kv, do):
    vmem = pl.BlockSpec(memory_space=pltpu.VMEM)
    return pl.pallas_call(
        attend_kernel,
        name="attend",
        out_shape=(
            jax.ShapeDtypeStruct((4, HD, HD), BF16),
            jax.ShapeDtypeStruct((8, BLOCK, 2 * HD), BF16),
        ),
        in_specs=[pl.BlockSpec(memory_space=pltpu.SMEM), vmem, vmem, vmem],
        out_specs=(vmem, vmem),
        scratch_shapes=[
            pltpu.VMEM((TOP, BLOCK, HD), F32),
            pltpu.VMEM((TOP, BLOCK, HD), F32),
            pltpu.VMEM((2 * HD, 2 * HD), BF16),
            pltpu.VMEM((8, BLOCK, 2 * HD), F32),
        ],
        compiler_params=pltpu.CompilerParams(vmem_limit_bytes=VMEM_BYTES),
    )(selected, q, kv, do)


def owner_x(z, jj):
    at = jnp.where(lax.rem(jj, 2) == 0, lax.div(jj, 2), lax.div(7 - jj, 2))
    return turn(at, 2 * lax.rem(z, 2))


def block_of(z, x):
    at = turn(x, 2 * lax.rem(z, 2))
    return jnp.where(at < 2, 2 * at, 7 - 2 * at)


def gradient_kernel(
    dkv, dq, w_in, out,
    wall, gall, core_in, far_out, near_out, far_in, near_in,
    xf_out, xn_out, xf_in, xn_in, own_x, fin, fin_in,
    send_sems, load_sem, core_sems, far_sems, near_sems, q_sems, g_sems, xf_sems, xn_sems, f_sems,
):
    z, y, zh, x, j = place()
    d = wall.shape[1] // 4
    f = lax.axis_index("fsdp")
    partner = device(z, y, zh, x, 1 - j)
    right = device(z, turn(y, 1), zh, x, j)
    left = device(z, turn(y, 3), zh, x, j)
    x_right = device(z, y, zh, turn(x, 1), j)
    x_left = device(z, y, zh, turn(x, 3), j)
    up = z >= 2
    end = jnp.logical_or(z == 0, z == 3)
    mid = jnp.logical_not(end)
    flip = lambda h: jnp.where(up, h, 3 - h)
    at_z = lambda h: device(h, y, zh, x, j)
    first_z = flip(jnp.where(end, 2, 1))
    second_z = flip(jnp.where(end, 1, 3))
    far_z = flip(0)

    load = pltpu.make_async_copy(w_in, wall, load_sem)
    load.start()

    across = [at_z(turn(z, t)) for t in (1, 2, 3)]
    barrier, expected = enter([partner, right, left, x_right, x_left] + across, more=4)
    source_z = lax.div(f, 4)
    source_x = owner_x(source_z, lax.rem(f, 4))
    for h in (0, 1):
        for k in (0, 1):
            pl.semaphore_signal(
                barrier, inc=1, device_id=device(source_z, y, h, source_x, k),
                device_id_type=MESH,
            )
    pl.semaphore_wait(barrier, expected)

    mail = Mail(send_sems)

    def spread(src, at, cols, sems):
        there = gall.at[z, at, cols]
        mail.send(src, there, sems.at[z], at_z(first_z))
        mail.send(src, there, sems.at[z], at_z(second_z))

    def forward(at, cols, sems):
        for h in (first_z, far_z):
            block = gall.at[h, at, cols]
            pl.when(mid)(lambda: got(block, sems.at[h]))
            mail.send_if(mid, block, block, sems.at[h], at_z(second_z))

    def gathered(at, cols, sems):
        def wait(h):
            got(gall.at[h, at, cols], sems.at[h])

        wait(second_z)

        @pl.when(end)
        def _():
            wait(first_z)
            wait(3 - z)

    runs = [pl.ds(HD * r, HD) for r in range(4)]
    every, q_cols, kv_cols = pl.ds(0, 4 * HD), pl.ds(2 * HD, HD), pl.ds(0, 2 * HD)
    for n, t in enumerate((2, 1, 3, 0)):
        mail.send(dkv.at[:, turn(y, t), 1 - j], core_in.at[n], core_sems.at[n], partner)
    spread(dq, every, q_cols, q_sems)
    gall[z, :, q_cols] = dq[...]

    def chip_sum(n, t, run):
        return dkv[run, turn(y, t), j].astype(F32) + core_in[n, run].astype(F32)

    def far(h):
        for side, dev in ((0, right), (1, left)):
            far_out[h, side] = chip_sum(0, 2, 2 * h + side).astype(BF16)
            mail.send(far_out.at[h, side], far_in.at[h, side], far_sems.at[h, side], dev)

    def near(h, term):
        for side, (t, dev) in enumerate(((1, right), (3, left))):
            lane = side if term else 1 - side
            total = chip_sum(1 + side, t, 2 * h + lane)
            if term:
                got(far_in.at[h, side], far_sems.at[h, side])
                total += far_in[h, side].astype(F32)
            near_out[h, side, lane] = total.astype(BF16)
            mail.send(
                near_out.at[h, side, lane], near_in.at[h, side, lane],
                near_sems.at[h, side, lane], dev,
            )

    def spread_run(run):
        at = runs[run]
        spread(gall.at[z, at, kv_cols], at, kv_cols, g_sems.at[run])

    def finish_kv(h):
        for lane in (0, 1):
            for side in (1 - lane, lane):
                got(near_in.at[h, side, lane], near_sems.at[h, side, lane])
        for lane in (0, 1):
            run = 2 * h + lane
            total = chip_sum(3, 0, run)
            for side in (0, 1):
                total += near_in[h, side, lane].astype(F32)
            at = runs[run]
            gall[z, at, kv_cols] = total.astype(BF16)
            if run < AHEAD:
                spread_run(run)

    got(core_in.at[0], core_sems.at[0])
    far(0)
    got(core_in.at[1], core_sems.at[1])
    got(core_in.at[2], core_sems.at[2])
    near(0, False)
    far(1)
    got(core_in.at[3], core_sems.at[3])
    near(0, True)
    near(1, False)
    forward(every, q_cols, q_sems)
    finish_kv(0)
    near(1, True)
    finish_kv(1)

    def part(t, r):
        cols = rows(d * block_of(z, turn(x, t)), d)
        total = jnp.zeros((d, HD), F32)
        for head in range(4):
            total += lax.dot_general(
                wall[head, cols], gall[head, runs[r]], (((1,), (1,)), ((), ())),
                preferred_element_type=F32,
            )
        return total[: d // 2], total[d // 2 :]

    def x_first(r):
        total = part(2, r)
        for side, dev in ((0, x_right), (1, x_left)):
            xf_out[r, side] = total[side].astype(BF16)
            mail.send(xf_out.at[r, side], xf_in.at[r, side], xf_sems.at[r, side], dev)
        for side, (t, dev) in enumerate(((1, x_right), (3, x_left))):
            total = part(t, r)
            alone = 1 - side
            xn_out[r, side, alone] = total[alone].astype(BF16)
            own_x[r, side] = total[side]
            mail.send(
                xn_out.at[r, side, alone], xn_in.at[r, side, alone],
                xn_sems.at[r, side, alone], dev,
            )

    def x_second(r):
        for side, dev in ((0, x_right), (1, x_left)):
            got(xf_in.at[r, side], xf_sems.at[r, side])
            xn_out[r, side, side] = (
                own_x[r, side] + xf_in[r, side].astype(F32)
            ).astype(BF16)
            mail.send(
                xn_out.at[r, side, side], xn_in.at[r, side, side], xn_sems.at[r, side, side], dev
            )
        total = part(0, r)
        for lane in (0, 1):
            own_x[r, lane] = total[lane]

    fd = 4 * z + block_of(z, x)

    def x_third(r):
        for lane in (0, 1):
            total = own_x[r, lane]
            for side in (1 - lane, lane):
                got(xn_in.at[r, side, lane], xn_sems.at[r, side, lane])
                total += xn_in[r, side, lane].astype(F32)
            fin[r, pl.ds((d // 2) * lane, d // 2)] = total.astype(BF16)
        mail.send_or_keep(
            jnp.logical_or(r != z, fd != f), fin.at[r], fin_in.at[zh, j],
            f_sems.at[zh, j], (r * 4 + y, fd),
        )

    load.wait()
    gathered(every, q_cols, q_sems)
    for r in range(4):
        forward(runs[r], kv_cols, g_sems.at[r])
        if r + AHEAD < 4:
            spread_run(r + AHEAD)
        if r >= 1:
            x_second(r - 1)
        gathered(runs[r], kv_cols, g_sems.at[r])
        x_first(r)
        if r >= 1:
            x_third(r - 1)
    x_second(3)
    x_third(3)
    for h in (0, 1):
        for k in (0, 1):
            got(fin_in.at[h, k], f_sems.at[h, k])
    for h in (0, 1):
        for k in (0, 1):
            out[h, pl.ds(HD * k, HD)] = fin_in[h, k].T
    mail.flush()


def input_gradient(dkv, dq, w_all):
    quarter = w_all.shape[1]
    d = quarter // 4
    any_space = pl.BlockSpec(memory_space=pl.ANY)
    vmem = pl.BlockSpec(memory_space=pltpu.VMEM)
    dma = pltpu.SemaphoreType.DMA
    run = (HD, 2 * HD)
    block, lane = (d, HD), (d // 2, HD)
    return pl.pallas_call(
        gradient_kernel,
        name="input_gradient",
        out_shape=jax.ShapeDtypeStruct((2, 2 * HD, d), BF16),
        in_specs=[vmem, vmem, any_space],
        out_specs=vmem,
        scratch_shapes=[
            pltpu.VMEM(w_all.shape, BF16),
            pltpu.VMEM((4, 4 * HD, 3 * HD), BF16),
            pltpu.VMEM((4, 4) + run, BF16),
            pltpu.VMEM((2, 2) + run, BF16),
            pltpu.VMEM((2, 2, 2) + run, BF16),
            pltpu.VMEM((2, 2) + run, BF16),
            pltpu.VMEM((2, 2, 2) + run, BF16),
            pltpu.VMEM((4, 2) + lane, BF16),
            pltpu.VMEM((4, 2, 2) + lane, BF16),
            pltpu.VMEM((4, 2) + lane, BF16),
            pltpu.VMEM((4, 2, 2) + lane, BF16),
            pltpu.VMEM((4, 2) + lane, F32),
            pltpu.VMEM((4,) + block, BF16),
            pltpu.VMEM((2, 2) + block, BF16),
            dma((72,)), dma, dma((4,)), dma((2, 2)), dma((2, 2, 2)), dma((4,)), dma((4, 4)),
            dma((4, 2)), dma((4, 2, 2)), dma((2, 2)),
        ],
        compiler_params=pltpu.CompilerParams(
            collective_id=1, has_side_effects=True, vmem_limit_bytes=VMEM_BYTES
        ),
    )(dkv, dq, w_all)


def shards(inputs, w_qkv, selected, d_attn):
    w3 = w_qkv.transpose(1, 0, 2)
    q, kv, do, w_all = project_and_gather(inputs, w3, d_attn)
    dq, dkv = attend(
        selected.T, q, kv.reshape(8, BLOCK, 2 * HD), do
    )
    halves = input_gradient(dkv.reshape(4, 4, 2, HD, 2 * HD), dq.reshape(4 * HD, HD), w_all)
    return (halves[0].astype(F32) + halves[1].astype(F32)).astype(BF16)


def solution(mesh):
    placed = (P("ctx", None), P("ctx", None, "fsdp"), P(), P("ctx", "fsdp"))
    return jax.shard_map(
        shards, mesh=mesh, in_specs=placed, out_specs=P("ctx", "fsdp"), check_vma=False
    )
```
